32 devices in a mesh: dp: 16 (over z, y, core), seq: 2 (over x).
Axes of the slice: x: 2, y: 2, z: 4, core: 2. Of those that a mesh axis runs over, the one named last changes fastest.
Arguments:
- x_in: bfloat16 [16, 256, 1024], P('dp', 'seq'), may hold values from -6 to 6
- cotangent: bfloat16 [16, 256, 1024], P('dp', 'seq'), may hold values from -6 to 6
- params: float32 [6602752], P(('dp', 'seq')), may hold values from -8 to 8
- moment_one: float32 [6602752], P(('dp', 'seq')), may hold values from -6 to 6
- moment_two: float32 [6602752], P(('dp', 'seq')), may hold values from 10 to 1000
Outputs:
- y_out: bfloat16 [16, 256, 1024], P('dp', 'seq')
- input_grad: bfloat16 [16, 256, 1024], P('dp', 'seq')
- weight_grads: float32 [6602752], P(('dp', 'seq'))
- new_params: float32 [6602752], P(('dp', 'seq'))
- new_moment_one: float32 [6602752], P(('dp', 'seq'))
- new_moment_two: float32 [6602752], P(('dp', 'seq'))
The draws below stay inside these ranges and needn't reach their ends.
All inputs are finite; a program needn't handle non-finite values.
Results may differ from the reference program's by a relative error of at most 0.012.
Values may be sent and summed in bfloat16 or wider, within the bound.
No kernel may reach another device: no remote copies, remote signals or barrier semaphores. Data moves between devices by JAX's collectives and lax.ppermute only.
A program may use at most 192 MiB of HBM per device.

```python
import math
import jax
import jax.numpy as jnp
from jax import lax

D = 1024
DI = 2048
N = 128
K = 4
SPAN = 128
H = 32
CONV = 2304
PROJ = 4384
SEQS = 16
LEN = 256
RAW = 6601056
PARAMS = 6602752


def draw_params(key, part):
    keys = jax.random.split(key, 12)
    in_weight = jax.random.truncated_normal(keys[0], -6.0, 6.0, (D * PROJ,), jnp.float32) * D ** (-0.5)
    out_weight = jax.random.truncated_normal(keys[1], -6.0, 6.0, (DI * D,), jnp.float32) * DI ** (-0.5)
    conv_weight = jax.random.truncated_normal(keys[2], -6.0, 6.0, (K * CONV,), jnp.float32) * 0.5
    conv_bias = jax.random.uniform(keys[3], (CONV,), jnp.float32, -0.5, 0.5)
    norm_gain = jax.random.uniform(keys[4], (D,), jnp.float32, 0.6, 1.4)
    gate_gain = jax.random.uniform(keys[5], (DI,), jnp.float32, 0.6, 1.4)
    slow_share = 0.5
    slow = jax.random.uniform(keys[6], (H,), jnp.float32) < slow_share
    slow_log = jnp.log(0.3 / (LEN * 0.05)) + jax.random.uniform(keys[7], (H,), jnp.float32, -0.5, 0.5)
    fast_log = jax.random.uniform(keys[8], (H,), jnp.float32, -0.7, 0.7)
    a_log = jnp.where(slow, slow_log, fast_log)
    dt_bias = jax.random.uniform(keys[9], (H,), jnp.float32, -3.5, -2.5)
    skip_gain = jax.random.uniform(keys[10], (H,), jnp.float32, 0.5, 1.5)
    filler = jax.random.truncated_normal(keys[11], -6.0, 6.0, (PARAMS - RAW,), jnp.float32) * 0.02
    return jnp.concatenate([in_weight, out_weight, conv_weight, conv_bias, norm_gain, gate_gain, a_log, dt_bias, skip_gain, filler])


def block_scale(key, dims, cuts, low, high):
    loudness, own = 1.0, jax.random.fold_in(key, 6)
    for axis_at, blocks in cuts:
        heights = jnp.exp(jax.random.uniform(jax.random.fold_in(own, axis_at), (blocks,), jnp.float32, low / len(cuts), high / len(cuts)))
        loudness = loudness * jnp.repeat(heights, dims[axis_at] // blocks).reshape([-1 if axis == axis_at else 1 for axis in range(len(dims))])
    return loudness


def normal_values(stream_key, shape, scale, bound, cuts=(), kind=jnp.bfloat16):
    drawn = jax.random.normal(stream_key, shape, jnp.float32) * scale
    if len(cuts) > 0:
        drawn = block_scale(stream_key, shape, cuts, -0.22, 0.18) * drawn
    return jnp.clip(drawn, min=-bound, max=bound).astype(kind)


def setup_inputs(seed: int = 0) -> dict:
    arg_keys = jax.random.split(jax.random.key(seed), 6)
    x_in = normal_values(arg_keys[0], (SEQS, LEN, D), 1.0, 6.0, ((0, 16), (1, 2)))
    cotangent = normal_values(arg_keys[1], (SEQS, LEN, D), 1.0, 6.0, ((0, 16), (1, 2)))
    params = draw_params(jax.random.fold_in(arg_keys[5], 71), 0)
    moment_one = normal_values(arg_keys[3], (PARAMS,), 1.0, 6.0, ((0, 32),), jnp.float32)
    moment_two = jnp.clip(jnp.exp(math.log(1000.0) - 4.6051702 * jax.random.uniform(arg_keys[4], (PARAMS,), jnp.float32) ** block_scale(arg_keys[4], (PARAMS,), ((0, 32),), -0.2, 0.2)), 10.0, 1000.0)
    return dict(x_in=x_in, cotangent=cotangent, params=params, moment_one=moment_one, moment_two=moment_two)


HIGH = lax.Precision.HIGHEST
norm_eps = 1e-05
learn_rate = 0.005
beta_one = 0.9
beta_two = 0.95
adam_eps = 1e-08
weight_decay = 0.1
adam_step = 10

def unpack(flat):
    lengths = (D * PROJ, DI * D, K * CONV, CONV, D, DI, H, H, H)
    pieces = []
    offset = 0
    for length in lengths:
        pieces.append(lax.slice_in_dim(flat, offset, offset + length))
        offset = offset + length
    return (pieces[0].reshape(D, PROJ), pieces[1].reshape(DI, D), pieces[2].reshape(K, CONV)) + tuple(pieces[3:])

def front(tokens, in_weight, norm_gain):
    wide = tokens.astype(jnp.float32)
    scale = lax.rsqrt(lax.optimization_barrier(jnp.mean(wide * wide, axis=-1, keepdims=True)) + norm_eps)
    normed = (wide * scale * norm_gain[None, :]).astype(jnp.bfloat16)
    mixed = jnp.dot(normed, in_weight, preferred_element_type=jnp.float32).astype(jnp.bfloat16)
    return (wide, scale, normed, mixed)

def pre_mix(xbc_ext, dt_raw, conv_weight, conv_bias, dt_bias):
    width = conv_weight.shape[0]
    rows = xbc_ext.shape[0] - width + 1
    accum = conv_bias[None, :] + conv_weight[0][None, :] * xbc_ext[0:rows]
    for tap in range(1, width):
        accum = accum + conv_weight[tap][None, :] * xbc_ext[tap:tap + rows]
    return (jax.nn.silu(accum), jax.nn.softplus(dt_raw + dt_bias[None, :]))

def ssd_zero(values, step_size, b_mat, c_mat, a_log, skip_gain):
    rows, inner = values.shape
    heads = step_size.shape[1]
    hsize = inner // heads
    blocks = rows // SPAN
    log_rate = step_size * (-jnp.exp(a_log))[None, :]
    within = jnp.cumsum(log_rate.reshape(blocks, SPAN, heads), axis=1)
    vals = values.reshape(blocks, SPAN, heads, hsize)
    steps_blk = step_size.reshape(blocks, SPAN, heads)
    b_blk = b_mat.reshape(blocks, SPAN, -1)
    c_blk = c_mat.reshape(blocks, SPAN, -1)
    within_h = jnp.transpose(within, (0, 2, 1))
    steps_h = jnp.transpose(steps_blk, (0, 2, 1))
    vals_h = jnp.transpose(vals, (0, 2, 1, 3))
    causal = (jnp.arange(SPAN)[:, None] >= jnp.arange(SPAN)[None, :])[None, None, :, :]
    gaps = within_h[:, :, :, None] - within_h[:, :, None, :]
    intersection = jnp.einsum('ctn,csn->cts', c_blk, b_blk, precision=HIGH)
    mixing = jnp.exp(jnp.where(causal, gaps, -10000.0)) * intersection[:, None, :, :] * steps_h[:, :, None, :]
    local_out = jnp.einsum('chts,chsp->cthp', mixing, vals_h, precision=HIGH)
    tail = jnp.exp(within[:, -1:, :] - within) * steps_blk
    block_states = jnp.einsum('clhp,cln->chpn', tail[..., None] * vals, b_blk, precision=HIGH)
    block_decay = jnp.exp(within[:, -1, :])

    def advance(carry, pair):
        rate, fresh = pair
        return (rate[:, None, None] * carry + fresh, carry)
    final, entering = lax.scan(advance, jnp.zeros(block_states.shape[1:], jnp.float32), (block_decay, block_states))
    carried = jnp.einsum('ctn,chpn->cthp', c_blk, entering, precision=HIGH) * jnp.exp(within)[..., None]
    output = local_out + carried + skip_gain[None, None, :, None] * vals
    before = jnp.cumsum(within[:, -1, :], axis=0) - within[:, -1, :]
    cumall = (within + before[:, None, :]).reshape(rows, heads)
    return (output.reshape(rows, inner), final, cumall)

def post_mix(ssd_out, gate_in, gate_gain):
    gated = ssd_out * jax.nn.silu(gate_in)
    scale = lax.rsqrt(lax.optimization_barrier(jnp.mean(gated * gated, axis=-1, keepdims=True)) + norm_eps)
    return gated * scale * gate_gain[None, :]

def back_norm(wide, scale, norm_gain, d_normed):
    weighted = d_normed * norm_gain[None, :]
    d_gain = lax.optimization_barrier(jnp.sum(d_normed * wide * scale, axis=0))
    d_wide = scale * weighted - wide * scale ** 3 * lax.optimization_barrier(jnp.mean(weighted * wide, axis=-1, keepdims=True))
    return (d_wide, d_gain)

def adamw(param_vec, grad_vec, first, second):
    first_new = beta_one * first + (1.0 - beta_one) * grad_vec
    second_new = beta_two * second + (1.0 - beta_two) * grad_vec * grad_vec
    first_hat = first_new / (1.0 - beta_one ** adam_step)
    second_hat = second_new / (1.0 - beta_two ** adam_step)
    updated = param_vec - learn_rate * (first_hat / (jnp.sqrt(second_hat) + adam_eps) + weight_decay * param_vec)
    return (updated, first_new, second_new)

def reference(x_in, cotangent, params, moment_one, moment_two):
    rounded = params.astype(jnp.bfloat16)
    in_w, out_w, conv_wb, conv_bb, norm_gb, gate_gb, a_logb, dt_biasb, skipb = unpack(rounded)
    conv_w = conv_wb.astype(jnp.float32)
    conv_b = conv_bb.astype(jnp.float32)
    norm_g = norm_gb.astype(jnp.float32)
    gate_g = gate_gb.astype(jnp.float32)
    a_log = a_logb.astype(jnp.float32)
    dt_bias = dt_biasb.astype(jnp.float32)
    skip_gain = skipb.astype(jnp.float32)

    def per_sequence(total, pair):
        tokens, cot = pair
        wide, scale, normed, mixed = front(tokens, in_w, norm_g)
        gate_in = mixed[:, :DI].astype(jnp.float32)
        xbc_ext = jnp.concatenate([jnp.zeros((K - 1, CONV), jnp.bfloat16), mixed[:, DI:DI + CONV]], axis=0).astype(jnp.float32)
        dt_raw = mixed[:, DI + CONV:].astype(jnp.float32)
        (act, step_size), pre_pull = jax.vjp(pre_mix, xbc_ext, dt_raw, conv_w, conv_b, dt_bias)
        values = act[:, :DI]
        b_mat = act[:, DI:DI + N]
        c_mat = act[:, DI + N:]
        (ssd_out, final_state, cumall), ssd_pull = jax.vjp(ssd_zero, values, step_size, b_mat, c_mat, a_log, skip_gain)
        gated, post_pull = jax.vjp(post_mix, ssd_out, gate_in, gate_g)
        gated_norm = gated.astype(jnp.bfloat16)
        result = (wide + jnp.dot(gated_norm, out_w, preferred_element_type=jnp.float32)).astype(jnp.bfloat16)
        d_out_w = jnp.dot(gated_norm.T, cot, preferred_element_type=jnp.float32)
        d_gated = jnp.dot(cot, out_w.T, preferred_element_type=jnp.float32)
        d_ssd, d_gate_in, d_gate_g = post_pull(d_gated)
        d_values, d_step, d_bmat, d_cmat, d_alog, d_skip = ssd_pull((d_ssd, jnp.zeros_like(final_state), jnp.zeros_like(cumall)))
        d_ext, d_dtraw, d_convw, d_convb, d_dtbias = pre_pull((jnp.concatenate([d_values, d_bmat, d_cmat], axis=1), d_step))
        d_mixed = jnp.concatenate([d_gate_in, d_ext[K - 1:], d_dtraw], axis=1).astype(jnp.bfloat16)
        d_in_w = jnp.dot(normed.T, d_mixed, preferred_element_type=jnp.float32)
        d_normed = jnp.dot(d_mixed, in_w.T, preferred_element_type=jnp.float32)
        d_wide, d_norm_g = back_norm(wide, scale, norm_g, d_normed)
        d_tokens = (cot.astype(jnp.float32) + d_wide).astype(jnp.bfloat16)
        grad_vec = jnp.concatenate([d_in_w.reshape(-1), d_out_w.reshape(-1), d_convw.reshape(-1), d_convb, d_norm_g, d_gate_g, d_alog, d_dtbias, d_skip, jnp.zeros((PARAMS - RAW,), jnp.float32)])
        return (total + grad_vec, (result, d_tokens))
    grads, (outputs, input_grad) = lax.scan(per_sequence, jnp.zeros((PARAMS,), jnp.float32), (x_in, cotangent))
    updated, first_new, second_new = adamw(params, grads, moment_one, moment_two)
    return (outputs, input_grad, grads, updated, first_new, second_new)
```

```python
import jax
import jax.numpy as jnp
import numpy as np
from jax import lax
from jax.sharding import PartitionSpec as P

D = 1024
DI = 2048
N = 128
K = 4
SPAN = 128
H = 32
CONV = 2304
PROJ = 4384
WIDE = 4480
IN = D * PROJ
OUT = DI * D
SMALL = K * CONV + CONV + D + DI + 3 * H

norm_eps = 1e-05
learn_rate = 0.005
beta_one = 0.9
beta_two = 0.95
adam_eps = 1e-08
weight_decay = 0.1
adam_step = 10

bf16 = jnp.bfloat16
f32 = jnp.float32


def ceil_to(value, unit):
    return -(-value // unit) * unit


def factors(count):
    core = 2 if count % 2 == 0 else 1
    rest = count // core
    mid = 1
    while rest % (mid * 2) == 0 and (mid * 2) ** 2 <= rest * 1:
        mid *= 2
    return rest // mid, mid, core


def dot(a, b, dims=((1,), (0,))):
    return lax.dot_general(a, b, (dims, ((), ())), preferred_element_type=f32)


def pre_mix(xbc_ext, dt_raw, conv_weight, conv_bias, dt_bias):
    width = conv_weight.shape[0]
    rows = xbc_ext.shape[0] - width + 1
    accum = conv_bias[None, :] + conv_weight[0][None, :] * xbc_ext[0:rows]
    for tap in range(1, width):
        accum = accum + conv_weight[tap][None, :] * xbc_ext[tap : tap + rows]
    return (jax.nn.silu(accum), jax.nn.softplus(dt_raw + dt_bias[None, :]))


def ssd_zero(values, step_size, b_mat, c_mat, a_log, skip_gain):
    rows, inner = values.shape
    heads = step_size.shape[1]
    hsize = inner // heads
    blocks = rows // SPAN
    log_rate = step_size * (-jnp.exp(a_log))[None, :]
    within = jnp.cumsum(log_rate.reshape(blocks, SPAN, heads), axis=1)
    vals = values.reshape(blocks, SPAN, heads, hsize)
    steps_blk = step_size.reshape(blocks, SPAN, heads)
    b_blk = b_mat.reshape(blocks, SPAN, -1)
    c_blk = c_mat.reshape(blocks, SPAN, -1)
    within_h = jnp.transpose(within, (0, 2, 1))
    steps_h = jnp.transpose(steps_blk, (0, 2, 1))
    vals_h = jnp.transpose(vals, (0, 2, 1, 3))
    causal = (jnp.arange(SPAN)[:, None] >= jnp.arange(SPAN)[None, :])[None, None, :, :]
    gaps = within_h[:, :, :, None] - within_h[:, :, None, :]
    intersection = jnp.einsum("ctn,csn->cts", c_blk, b_blk)
    mixing = (
        jnp.exp(jnp.where(causal, gaps, -10000.0))
        * intersection[:, None, :, :]
        * steps_h[:, :, None, :]
    )
    local_out = jnp.einsum("chts,chsp->cthp", mixing, vals_h)
    tail = jnp.exp(within[:, -1:, :] - within) * steps_blk
    block_states = jnp.einsum("clhp,cln->chpn", tail[..., None] * vals, b_blk)
    block_decay = jnp.exp(within[:, -1, :])
    state = jnp.zeros(block_states.shape[1:], f32)
    entering = []
    for blk in range(blocks):
        entering.append(state)
        state = block_decay[blk][:, None, None] * state + block_states[blk]
    entering = jnp.stack(entering)
    carried = jnp.einsum("ctn,chpn->cthp", c_blk, entering) * jnp.exp(within)[..., None]
    output = local_out + carried + skip_gain[None, None, :, None] * vals
    return output.reshape(rows, inner)


def adamw(param_vec, grad_vec, first, second):
    first_new = beta_one * first + (1.0 - beta_one) * grad_vec
    second_new = beta_two * second + (1.0 - beta_two) * grad_vec * grad_vec
    first_hat = first_new / (1.0 - beta_one**adam_step)
    second_hat = second_new / (1.0 - beta_two**adam_step)
    updated = param_vec - learn_rate * (
        first_hat / (jnp.sqrt(second_hat) + adam_eps) + weight_decay * param_vec
    )
    return (updated, first_new, second_new)


class Plan:
    def __init__(self, dp, seq, flat):
        self.dp, self.seq, self.flat = dp, seq, flat
        self.total = dp * seq
        count = self.total
        self.mix = IN // flat
        last_in = -(-IN // flat)
        rows_in = max(
            -(-(((k * flat) % PROJ) + min(flat, IN - k * flat)) // PROJ) for k in range(last_in)
        )
        rows_out = max(
            -(-(((k * flat - IN) % D) + flat) // D) for k in range(self.mix, count)
        )
        self.rows = ceil_to(max(rows_in, -(-rows_out // 4)), 8)
        self.in_len = IN - self.mix * flat
        self.mix_in = -(-(((self.mix * flat) % PROJ) + self.in_len) // PROJ)
        self.mix_out = -(-(flat - self.in_len) // D)
        self.mix_free = self.rows - self.mix_in
        assert 4 * self.mix_free >= self.mix_out
        rows = self.rows
        self.j_in = self.mix // seq + 1
        self.j_out = self.mix // seq
        n_in, n_out = self.j_in, dp - self.j_out
        self.in_map = np.full((seq, n_in, rows), -1, np.int32)
        self.out_map = np.full((seq, n_out, 4, rows), -1, np.int32)
        m = np.arange(rows)
        for s in range(seq):
            for j in range(n_in):
                k = j * seq + s
                if k > self.mix:
                    continue
                first = (k * flat) // PROJ
                used = min(rows, D - first)
                if k == self.mix:
                    used = self.mix_in
                self.in_map[s, j, :used] = first + m[:used]
            for j in range(n_out):
                k = (j + self.j_out) * seq + s
                if k < self.mix:
                    continue
                for b in range(4):
                    if k == self.mix:
                        q = b * self.mix_free + (m - self.mix_in)
                        ok = (m >= self.mix_in) & (q < self.mix_out)
                    else:
                        q = (k * flat - IN) // D + b * rows + m
                        ok = q < min(DI, -(-((k + 1) * flat - IN) // D))
                    self.out_map[s, j, b] = np.where(ok, q, -1)

    def pack(self, flat, k):
        rows, size = self.rows, self.flat
        shift = (k * size) % PROJ
        span = rows * PROJ
        buf = jnp.pad(flat, (PROJ, span - size))
        win = lax.dynamic_slice(buf, (PROJ - shift,), (span,)).reshape(rows, PROJ)
        win = jnp.pad(win, ((0, 0), (0, WIDE - PROJ)))
        off = (k * size - IN) % D
        span = 4 * rows * D
        buf = jnp.pad(flat, (D, span - size))
        out = lax.dynamic_slice(buf, (D - off,), (span,)).reshape(4, rows, D)
        out = jnp.concatenate([out[b] for b in range(4)] + [jnp.zeros((rows, WIDE - 4 * D), flat.dtype)], axis=1)
        head = flat[self.in_len :]
        free = self.mix_free
        head = jnp.pad(head, (0, 4 * free * D - head.shape[0])).reshape(4, free, D)
        low = jnp.concatenate([head[b] for b in range(4)] + [jnp.zeros((free, WIDE - 4 * D), flat.dtype)], axis=1)
        mixed = jnp.concatenate([win[: self.mix_in], low], axis=0)
        return jnp.where(k < self.mix, win, jnp.where(k > self.mix, out, mixed))

    def unpack(self, chunk, k):
        rows, size = self.rows, self.flat
        shift = (k * size) % PROJ
        line = chunk[:, :PROJ].reshape(-1)
        line = jnp.pad(line, (0, max(0, PROJ + size - rows * PROJ)))
        win = lax.dynamic_slice(line, (shift,), (size,))
        off = (k * size - IN) % D
        line = jnp.concatenate([chunk[:, b * D : (b + 1) * D] for b in range(4)], axis=0).reshape(-1)
        line = jnp.pad(line, (0, max(0, D + size - 4 * rows * D)))
        out = lax.dynamic_slice(line, (off,), (size,))
        low = chunk[self.mix_in :]
        low = jnp.concatenate([low[:, b * D : (b + 1) * D] for b in range(4)], axis=0)
        mixed = jnp.concatenate([win[: self.in_len], low.reshape(-1)[: size - self.in_len]])
        return jnp.where(k < self.mix, win, jnp.where(k > self.mix, out, mixed))


def make(dp, seq):
    za, yb, cc = factors(dp)

    def place(z, y, c):
        return ((z % za) * yb + (y % yb)) * cc + (c % cc)

    def perm(dz, dy, dc):
        return [
            (place(z, y, c), place(z + dz, y + dy, c + dc))
            for z in range(za)
            for y in range(yb)
            for c in range(cc)
        ]

    z_next, y_next, c_next = perm(1, 0, 0), perm(0, 1, 0), perm(0, 0, 1)

    def gather_dp(chunk):
        j = lax.axis_index("dp")
        z, y, c = j // (yb * cc), (j // cc) % yb, j % cc
        whole = jnp.zeros((dp,) + chunk.shape, chunk.dtype)
        slots = []
        cur = chunk
        for r in range(za):
            if r:
                cur = lax.ppermute(cur, "dp", z_next)
            side = cur
            for t in range(yb):
                if t:
                    side = lax.ppermute(side, "dp", y_next)
                slots.append((z - r, y - t, c, side))
                if cc == 2:
                    slots.append((z - r, y - t, c + 1, lax.ppermute(side, "dp", c_next)))
        for zi, yi, ci, data in slots:
            at = (((zi + za) % za) * yb + (yi + yb) % yb) * cc + ci % cc
            whole = lax.dynamic_update_index_in_dim(whole, data, at, 0)
        return whole

    def scatter_dp(parts):
        j = lax.axis_index("dp")
        z, y, c = j // (yb * cc), (j // cc) % yb, j % cc

        def pick(zi, yi, ci):
            at = (((zi + za) % za) * yb + (yi + yb) % yb) * cc + ci % cc
            return lax.dynamic_index_in_dim(parts, at, 0, False)

        def core_sum(zi, yi):
            own = pick(zi, yi, c)
            if cc == 2:
                got = lax.ppermute(pick(zi, yi, c + 1), "dp", c_next)
                own = (own.astype(f32) + got.astype(f32)).astype(bf16)
            return own

        def mid_sum(zi):
            acc = None
            for r in range(1, yb + 1):
                mine = core_sum(zi, y - r)
                if acc is not None:
                    acc = (acc.astype(f32) + mine.astype(f32)).astype(bf16)
                else:
                    acc = mine
                if r < yb:
                    acc = lax.ppermute(acc, "dp", y_next)
            return acc

        acc = None
        for r in range(1, za + 1):
            mine = mid_sum(z - r)
            if acc is not None:
                acc = acc.astype(f32) + mine.astype(f32)
            else:
                acc = mine
            if r < za:
                acc = lax.ppermute(acc.astype(bf16), "dp", z_next)
        return acc.astype(f32)

    def swap_seq(a):
        return lax.ppermute(a, "seq", [(0, 1), (1, 0)])

    def halves(a, axis):
        n = a.shape[axis] // 2
        return lax.slice_in_dim(a, 0, n, axis=axis), lax.slice_in_dim(a, n, 2 * n, axis=axis)

    def gather_seq(a, axis):
        if seq != 2:
            return lax.all_gather(a, "seq", axis=axis, tiled=True)
        first = lax.axis_index("seq") == 0
        other = swap_seq(a)
        return jnp.concatenate([jnp.where(first, a, other), jnp.where(first, other, a)], axis=axis)

    def scatter_seq(a, axis):
        if seq != 2:
            return lax.psum_scatter(a, "seq", scatter_dimension=axis, tiled=True)
        first = lax.axis_index("seq") == 0
        low, high = halves(a, axis)
        got = swap_seq(jnp.where(first, high, low).astype(bf16))
        return jnp.where(first, low, high) + got.astype(f32)

    def sum_seq(a):
        if seq != 2:
            return lax.psum(a, "seq")
        a = a.astype(bf16)
        return a.astype(f32) + swap_seq(a).astype(f32)

    def sum_seq_wide(a):
        if seq != 2:
            return lax.psum(a, "seq")
        return a + swap_seq(a)

    def own_seq(a, axis):
        n = a.shape[axis] // seq
        return lax.dynamic_slice_in_dim(a, lax.axis_index("seq") * n, n, axis)

    def sum_all(a):
        for axis, count in (("seq", seq), ("dp", dp)):
            step = 1
            while step < count:
                a = a + lax.ppermute(a, axis, [(i, i ^ step) for i in range(count)])
                step *= 2
        return a

    def on_device(x_in, cotangent, params, moment_one, moment_two):
        size = params.shape[0]
        plan = Plan(dp, seq, size)
        rows = plan.rows
        s = lax.axis_index("seq")
        k = lax.axis_index("dp") * seq + s
        halfs = params.astype(bf16)

        x_own = x_in[0]
        cot_own = cotangent[0]
        tokens = gather_seq(x_own, 0)
        cot = gather_seq(cot_own, 0)

        base = IN + OUT
        at = base - k * size
        padded = jnp.pad(halfs, (SMALL, SMALL))
        tail = lax.dynamic_slice(padded, (jnp.clip(at + SMALL, 0, size + SMALL),), (SMALL,))
        tail = jnp.pad(tail, (0, -SMALL % D)).reshape(-1, D)
        small = sum_all(tail).reshape(-1)
        pieces = []
        offset = 0
        for length in (K * CONV, CONV, D, DI, H, H, H):
            pieces.append(small[offset : offset + length].astype(f32))
            offset += length
        conv_w, conv_b, norm_g, gate_g, a_log, dt_bias, skip_gain = pieces
        conv_w = conv_w.reshape(K, CONV)

        chunk = plan.pack(halfs, k)
        whole = gather_dp(chunk)
        n_in, n_out = plan.j_in, dp - plan.j_out
        w_in = whole[:n_in].reshape(n_in * rows, WIDE)
        w_out = [
            whole[plan.j_out :, :, b * D : (b + 1) * D].reshape(n_out * rows, D) for b in range(4)
        ]
        in_map = lax.dynamic_index_in_dim(jnp.asarray(plan.in_map.reshape(seq, -1)), s, 0, False)
        out_map = lax.dynamic_index_in_dim(
            jnp.asarray(plan.out_map.transpose(0, 2, 1, 3).reshape(seq, 4, -1)), s, 0, False
        )
        pick_in = (jnp.arange(D)[:, None] == in_map[None, :]).astype(bf16)
        pick_out = [(jnp.arange(DI)[:, None] == out_map[b][None, :]).astype(bf16) for b in range(4)]

        wide = tokens.astype(f32)
        scale = lax.rsqrt(jnp.mean(wide * wide, axis=-1, keepdims=True) + norm_eps)
        normed = (wide * scale * norm_g[None, :]).astype(bf16)
        normed_k = dot(normed, pick_in).astype(bf16)
        partial = dot(normed_k, w_in)

        x_part = scatter_seq(partial[:, DI : 2 * DI], 1)
        bcdt = sum_seq(partial[:, 2 * DI : PROJ])
        z_part = scatter_seq(partial[:, :DI], 1)
        gate_in = z_part.astype(bf16).astype(f32)
        xbc = jnp.concatenate([x_part, bcdt[:, : 2 * N]], axis=1).astype(bf16).astype(f32)
        dt_raw = own_seq(bcdt[:, 2 * N :], 1).astype(bf16).astype(f32)
        xbc_ext = jnp.pad(xbc, ((K - 1, 0), (0, 0)))
        inner = DI // seq

        def channels(a):
            return jnp.concatenate([own_seq(a[..., :DI], a.ndim - 1), a[..., DI:]], axis=-1)

        (act, step_size), pre_pull = jax.vjp(
            pre_mix, xbc_ext, dt_raw, channels(conv_w), channels(conv_b), own_seq(dt_bias, 0)
        )
        values = act[:, :inner]
        b_mat = act[:, inner : inner + N]
        c_mat = act[:, inner + N :]
        ssd_out, ssd_pull = jax.vjp(
            ssd_zero, values, step_size, b_mat, c_mat, own_seq(a_log, 0), own_seq(skip_gain, 0)
        )

        d_gated = None
        for b in range(4):
            piece = dot(cot, w_out[b], ((1,), (1,))).astype(bf16)
            piece = dot(piece, pick_out[b], ((1,), (1,)))
            d_gated = piece if d_gated is None else d_gated + piece
        d_gated = scatter_seq(d_gated, 1)

        gain = own_seq(gate_g, 0)[None, :]
        sig = jax.nn.sigmoid(gate_in)
        swish = gate_in * sig
        gated = ssd_out * swish
        weighted = d_gated * gain
        sums = jnp.stack([jnp.sum(gated * gated, axis=1), jnp.sum(weighted * gated, axis=1)])
        sums = sum_seq_wide(sums)
        g_scale = lax.rsqrt(sums[0] / DI + norm_eps)[:, None]
        cross = (sums[1] / DI)[:, None]
        gated_norm = (gated * g_scale * gain).astype(bf16)
        d_gate_g = jnp.sum(d_gated * gated * g_scale, axis=0)
        d_pre = g_scale * weighted - gated * g_scale**3 * cross
        d_ssd = d_pre * swish
        d_gate_in = d_pre * ssd_out * (sig + swish * (1.0 - sig))

        gn_full = gather_seq(gated_norm, 1)
        gn_k = [dot(gn_full, pick_out[b]).astype(bf16) for b in range(4)]
        y_part = None
        for b in range(4):
            piece = dot(gn_k[b], w_out[b])
            y_part = piece if y_part is None else y_part + piece
        y_own = scatter_seq(y_part, 0) + x_own.astype(f32)

        d_values, d_step, d_bmat, d_cmat, d_alog, d_skip = ssd_pull(d_ssd)
        d_ext, d_dtraw, d_convw, d_convb, d_dtbias = pre_pull(
            (jnp.concatenate([d_values, d_bmat, d_cmat], axis=1), d_step)
        )
        d_xbc = d_ext[K - 1 :]
        d_z_full = gather_seq(d_gate_in.astype(bf16), 1)
        d_x_full = gather_seq(d_xbc[:, :inner].astype(bf16), 1)
        d_bc = sum_seq(d_xbc[:, inner:]).astype(bf16)
        d_dt_full = gather_seq(d_dtraw.astype(bf16), 1)
        pad = jnp.zeros((d_bc.shape[0], WIDE - PROJ), bf16)
        d_mixed = jnp.concatenate([d_z_full, d_x_full, d_bc, d_dt_full, pad], axis=1)

        g_in = dot(normed_k, d_mixed, ((0,), (0,))).astype(bf16).reshape(n_in, rows, WIDE)
        g_out = jnp.concatenate(
            [dot(gn_k[b], cot, ((0,), (0,))).astype(bf16).reshape(n_out, rows, D) for b in range(4)]
            + [jnp.zeros((n_out, rows, WIDE - 4 * D), bf16)],
            axis=2,
        )
        both = n_in + n_out - dp
        parts = jnp.concatenate(
            [g_in[: n_in - both], g_in[n_in - both :] + g_out[:both], g_out[both:]], axis=0
        )

        dn_k = dot(d_mixed, w_in, ((1,), (1,))).astype(bf16)
        d_normed = scatter_seq(dot(dn_k, pick_in, ((1,), (1,))), 0)
        wide_own = x_own.astype(f32)
        scale_own = lax.rsqrt(jnp.mean(wide_own * wide_own, axis=-1, keepdims=True) + norm_eps)
        a_own = d_normed * norm_g[None, :]
        d_norm_g = jnp.sum(d_normed * wide_own * scale_own, axis=0)
        d_wide = scale_own * a_own - wide_own * scale_own**3 * jnp.mean(
            a_own * wide_own, axis=-1, keepdims=True
        )
        input_grad = (cot_own.astype(f32) + d_wide).astype(bf16)

        def spread(a, width):
            full = jnp.zeros(a.shape[:-1] + (width,), f32)
            start = (0,) * (a.ndim - 1) + (s * a.shape[-1],)
            return lax.dynamic_update_slice(full, a, start)

        def spread_channels(a):
            return jnp.concatenate([spread(a[..., :inner], DI), a[..., inner:]], axis=-1)

        small_grad = jnp.concatenate(
            [
                spread_channels(d_convw).reshape(-1),
                spread_channels(d_convb),
                d_norm_g,
                spread(d_gate_g, DI),
                spread(d_alog, H),
                spread(d_dtbias, H),
                spread(d_skip, H),
            ]
        )
        small_grad = jnp.pad(small_grad, (0, -SMALL % D)).reshape(-1, D)
        small_grad = sum_all(small_grad).reshape(-1)[:SMALL]

        grad_chunk = scatter_dp(parts)
        shard = plan.unpack(grad_chunk, k)
        wing = jnp.pad(small_grad, (size, size))
        shard = shard + lax.dynamic_slice(
            wing, (jnp.clip(size - at, 0, size + SMALL),), (size,)
        )
        updated, first_new, second_new = adamw(params, shard, moment_one, moment_two)
        return (y_own.astype(bf16)[None], input_grad[None], shard, updated, first_new, second_new)

    return on_device


def solution(mesh):
    return jax.shard_map(
        make(mesh.shape["dp"], mesh.shape["seq"]),
        mesh=mesh,
        in_specs=(
            P("dp", "seq", None),
            P("dp", "seq", None),
            P(("dp", "seq")),
            P(("dp", "seq")),
            P(("dp", "seq")),
        ),
        out_specs=(
            P("dp", "seq", None),
            P("dp", "seq", None),
            P(("dp", "seq")),
            P(("dp", "seq")),
            P(("dp", "seq")),
            P(("dp", "seq")),
        ),
        check_vma=False,
    )
```

```python
import functools
import jax
import jax.numpy as jnp
import numpy as np
from jax import lax
from jax.experimental import pallas as pl
from jax.experimental.pallas import tpu as pltpu
from jax.sharding import PartitionSpec as P

D = 1024
DI = 2048
N = 128
K = 4
SPAN = 128
H = 32
CONV = 2304
PROJ = 4384
WIDE = 4480
IN = D * PROJ
OUT = DI * D
SMALL = K * CONV + CONV + D + DI + 3 * H

norm_eps = 1e-05
learn_rate = 0.005
beta_one = 0.9
beta_two = 0.95
adam_eps = 1e-08
weight_decay = 0.1
adam_step = 10

bf16 = jnp.bfloat16
f32 = jnp.float32


def ceil_to(value, unit):
    return -(-value // unit) * unit


def factors(count):
    core = 2 if count % 2 == 0 else 1
    rest = count // core
    mid = 1
    while rest % (mid * 2) == 0 and (mid * 2) ** 2 <= rest * 1:
        mid *= 2
    return rest // mid, mid, core


def dot(a, b, dims=((1,), (0,))):
    return lax.dot_general(a, b, (dims, ((), ())), preferred_element_type=f32)


def col_roll(a, steps):
    rows = a.shape[0]
    at = lax.broadcasted_iota(jnp.int32, a.shape, 0)
    if steps >= 0:
        return jnp.where(at >= steps, pltpu.roll(a, steps, 0), 0.0)
    return jnp.where(at < rows + steps, pltpu.roll(a, rows + steps, 0), 0.0)


def conv_act(x, taps, bias):
    acc = bias + taps[K - 1 : K] * x
    for k in range(1, K):
        acc = acc + taps[K - 1 - k : K - k] * col_roll(x, k)
    sig = 1.0 / (1.0 + jnp.exp(-acc))
    return acc, sig


def conv_back(x, taps, d_acc):
    d_x = taps[K - 1 : K] * d_acc
    d_taps = [jnp.sum(d_acc * x, axis=0, keepdims=True)]
    for k in range(1, K):
        d_x = d_x + taps[K - 1 - k : K - k] * col_roll(d_acc, -k)
        d_taps.insert(0, jnp.sum(d_acc * col_roll(x, k), axis=0, keepdims=True))
    return d_x, d_taps, jnp.sum(d_acc, axis=0, keepdims=True)


def fine(a, b, dims):
    return lax.dot_general(
        a, b, (dims, ((), ())), precision=lax.Precision.HIGHEST, preferred_element_type=f32
    )


def tri_parts():
    row = lax.broadcasted_iota(jnp.int32, (SPAN, SPAN), 0)
    col = lax.broadcasted_iota(jnp.int32, (SPAN, SPAN), 1)
    return row >= col, row == col


def rates(c, step_ref, turn_ref, alog_ref, alog_turn_ref, lower):
    span = slice(c * SPAN, (c + 1) * SPAN)
    rate = step_ref[span, :] * -jnp.exp(alog_ref[...])
    rate_turn = turn_ref[:, span] * -jnp.exp(alog_turn_ref[...])
    within = fine(lower, rate, ((1,), (0,)))
    within_turn = fine(rate_turn, lower, ((1,), (1,)))
    return rate, within, within_turn


def lanes_of(pair, first, second):
    lane = lax.broadcasted_iota(jnp.int32, (1, 2 * pair), 1)
    return jnp.where(lane < pair, first, second)


def ssd_forward_kernel(
    hsize, x_ref, bc_ref, wx_ref, bx_ref, wb_ref, bb_ref, step_ref, turn_ref, alog_ref, alog_turn_ref, skip_ref, out_ref
):
    rows, inner = x_ref.shape
    blocks = rows // SPAN
    causal, _ = tri_parts()
    lower = causal.astype(f32)
    acc, sig = conv_act(bc_ref[...].astype(f32), wb_ref[...], bb_ref[...])
    bc = (acc * sig).astype(bf16)
    b_blk = [bc[c * SPAN : (c + 1) * SPAN, :N] for c in range(blocks)]
    c_blk = [bc[c * SPAN : (c + 1) * SPAN, N:] for c in range(blocks)]
    cross = [dot(c_blk[c], b_blk[c], ((1,), (1,))) for c in range(blocks)]
    rated = [rates(c, step_ref, turn_ref, alog_ref, alog_turn_ref, lower) for c in range(blocks)]
    width = 2 * hsize
    lane = lax.broadcasted_iota(jnp.int32, (1, width), 1)
    masks = [(lane < hsize).astype(f32), (lane >= hsize).astype(f32)]
    for g in range(inner // width):
        cols = slice(g * width, (g + 1) * width)
        acc, sig = conv_act(x_ref[:, cols].astype(f32), wx_ref[:, cols], bx_ref[:, cols])
        vals = acc * sig
        state = None
        for c in range(blocks):
            span = slice(c * SPAN, (c + 1) * SPAN)
            _, within, within_turn = rated[c]
            v = vals[span]
            mix, split = [], []
            for i in range(2):
                h = 2 * g + i
                gap = within[:, h : h + 1] - within_turn[h : h + 1, :]
                mix.append(
                    (jnp.exp(jnp.where(causal, gap, -10000.0)) * cross[c] * turn_ref[h : h + 1, span]).astype(bf16)
                )
                split.append((v * masks[i]).astype(bf16))
            out = dot(jnp.concatenate(mix, axis=1), jnp.concatenate(split, axis=0))
            w0, w1 = within[:, 2 * g : 2 * g + 1], within[:, 2 * g + 1 : 2 * g + 2]
            if state is not None:
                out = out + lanes_of(hsize, jnp.exp(w0), jnp.exp(w1)) * dot(c_blk[c], state.astype(bf16))
            out_ref[span, cols] = out + skip_ref[:, cols] * v
            if c < blocks - 1:
                e0, e1 = w0[SPAN - 1 :], w1[SPAN - 1 :]
                tail = lanes_of(
                    hsize,
                    jnp.exp(e0 - w0) * step_ref[span, 2 * g : 2 * g + 1],
                    jnp.exp(e1 - w1) * step_ref[span, 2 * g + 1 : 2 * g + 2],
                )
                fresh = dot(b_blk[c], (tail * v).astype(bf16), ((0,), (0,)))
                if state is not None:
                    fresh = fresh + lanes_of(hsize, jnp.exp(e0), jnp.exp(e1)) * state
                state = fresh


def ssd_backward_kernel(
    hsize, x_ref, bc_ref, wx_ref, bx_ref, wb_ref, bb_ref, step_ref, turn_ref, alog_ref, alog_turn_ref, skip_ref,
    slope_ref, dy_ref, dx_ref, dbc_ref, ddt_ref, dwx_ref, dbx_ref, dwb_ref, dbb_ref, dhead_ref, dskip_ref,
    dcross_ref, dbmat_ref, dcmat_ref, col_ref, scol_ref, row_ref, srow_ref,
):
    rows, inner = x_ref.shape
    heads = step_ref.shape[1]
    blocks = rows // SPAN
    causal, eye = tri_parts()
    lower = causal.astype(f32)
    eye = eye.astype(f32)
    bc_in = bc_ref[...].astype(f32)
    bc_acc, bc_sig = conv_act(bc_in, wb_ref[...], bb_ref[...])
    bc = (bc_acc * bc_sig).astype(bf16)
    b_blk = [bc[c * SPAN : (c + 1) * SPAN, :N] for c in range(blocks)]
    c_blk = [bc[c * SPAN : (c + 1) * SPAN, N:] for c in range(blocks)]
    cross = [dot(c_blk[c], b_blk[c], ((1,), (1,))) for c in range(blocks)]
    rated = [rates(c, step_ref, turn_ref, alog_ref, alog_turn_ref, lower) for c in range(blocks)]
    for ref in (dcross_ref, dbmat_ref, dcmat_ref, col_ref, scol_ref, row_ref, srow_ref):
        ref[...] = jnp.zeros_like(ref)
    width = 2 * hsize
    lane = lax.broadcasted_iota(jnp.int32, (1, width), 1)
    masks = [(lane < hsize).astype(f32), (lane >= hsize).astype(f32)]
    head_lane = lax.broadcasted_iota(jnp.int32, (1, heads), 1)
    head_row = lax.broadcasted_iota(jnp.int32, (heads, 1), 0)
    last_row = lax.broadcasted_iota(jnp.int32, (SPAN, 1), 0) == SPAN - 1
    for g in range(inner // width):
        cols = slice(g * width, (g + 1) * width)
        x = x_ref[:, cols].astype(f32)
        acc, sig = conv_act(x, wx_ref[:, cols], bx_ref[:, cols])
        vals = acc * sig
        states, tails, decays = [None], [], []
        for c in range(blocks):
            span = slice(c * SPAN, (c + 1) * SPAN)
            within = rated[c][1]
            w0, w1 = within[:, 2 * g : 2 * g + 1], within[:, 2 * g + 1 : 2 * g + 2]
            e0, e1 = w0[SPAN - 1 :], w1[SPAN - 1 :]
            if c < blocks - 1:
                tails.append(
                    lanes_of(
                        hsize,
                        jnp.exp(e0 - w0) * step_ref[span, 2 * g : 2 * g + 1],
                        jnp.exp(e1 - w1) * step_ref[span, 2 * g + 1 : 2 * g + 2],
                    )
                )
                decays.append(lanes_of(hsize, jnp.exp(e0), jnp.exp(e1)))
                fresh = dot(b_blk[c], (tails[c] * vals[span]).astype(bf16), ((0,), (0,)))
                if states[c] is not None:
                    fresh = fresh + decays[c] * states[c]
                states.append(fresh)
        d_state = None
        d_vals = [None] * blocks
        d_skip = jnp.zeros((1, width), f32)
        for c in reversed(range(blocks)):
            span = slice(c * SPAN, (c + 1) * SPAN)
            _, within, within_turn = rated[c]
            v = vals[span]
            v_low = v.astype(bf16)
            dy = dy_ref[span, cols].astype(f32)
            ws = [within[:, 2 * g + i : 2 * g + i + 1] for i in range(2)]
            mix, split, d_w = [], [], []
            d_cross = None
            for i in range(2):
                h = 2 * g + i
                turn = turn_ref[h : h + 1, span]
                decay = jnp.exp(jnp.where(causal, ws[i] - within_turn[h : h + 1, :], -10000.0))
                scored = decay * cross[c]
                mix.append((scored * turn).astype(bf16))
                d_half = (dy * masks[i]).astype(bf16)
                split.append(d_half)
                d_mix = dot(d_half, v_low, ((1,), (1,)))
                raw = d_mix * scored
                part = d_mix * decay * turn
                d_cross = part if d_cross is None else d_cross + part
                d_w.append(jnp.sum(raw * turn, axis=1, keepdims=True))
                raw_sum = jnp.sum(raw, axis=0, keepdims=True)
                row_ref[c] += jnp.where(head_row == h, -raw_sum * turn, 0.0)
                srow_ref[c] += jnp.where(head_row == h, raw_sum, 0.0)
            dcross_ref[c] += d_cross
            d_v = dot(jnp.concatenate(mix, axis=0), jnp.concatenate(split, axis=0), ((0,), (0,)))
            d_v = d_v + skip_ref[:, cols] * dy
            d_skip = d_skip + jnp.sum(dy * v, axis=0, keepdims=True)
            d_enter = None
            if states[c] is not None:
                st = states[c].astype(bf16)
                lifted = lanes_of(hsize, jnp.exp(ws[0]), jnp.exp(ws[1])) * dy
                lift_low = lifted.astype(bf16)
                dcmat_ref[span] += dot(lift_low, st, ((1,), (1,)))
                d_enter = dot(c_blk[c], lift_low, ((0,), (0,)))
                prod = lifted * dot(c_blk[c], st)
                for i in range(2):
                    d_w[i] = d_w[i] + jnp.sum(prod * masks[i], axis=1, keepdims=True)
            if d_state is not None:
                ds_low = d_state.astype(bf16)
                back = dot(b_blk[c], ds_low)
                d_v = d_v + tails[c] * back
                dbmat_ref[span] += dot((tails[c] * v).astype(bf16), ds_low, ((1,), (1,)))
                along = v * back
                if states[c] is not None:
                    held = decays[c] * d_state * states[c]
                for i in range(2):
                    h = 2 * g + i
                    d_tail = jnp.sum(along * masks[i], axis=1, keepdims=True)
                    reach = jnp.exp(ws[i][SPAN - 1 :] - ws[i])
                    scol_ref[c] += jnp.where(head_lane == h, d_tail * reach, 0.0)
                    fall = d_tail * reach * step_ref[span, h : h + 1]
                    d_end = jnp.sum(fall, axis=0, keepdims=True)
                    if states[c] is not None:
                        d_end = d_end + jnp.sum(
                            jnp.sum(held * masks[i], axis=1, keepdims=True), axis=0, keepdims=True
                        )
                    d_w[i] = d_w[i] - fall + jnp.where(last_row, d_end, 0.0)
                if d_enter is not None:
                    d_enter = d_enter + decays[c] * d_state
            for i in range(2):
                col_ref[c] += jnp.where(head_lane == 2 * g + i, d_w[i], 0.0)
            d_state = d_enter
            d_vals[c] = d_v
        d_acc = jnp.concatenate(d_vals, axis=0) * (sig + vals * (1.0 - sig))
        d_x, d_taps, d_bias = conv_back(x, wx_ref[:, cols], d_acc)
        dx_ref[:, cols] = d_x.astype(bf16)
        for k in range(K):
            dwx_ref[k : k + 1, cols] = d_taps[k]
        dbx_ref[:, cols] = d_bias
        dskip_ref[:, cols] = d_skip
    d_alog = jnp.zeros((1, heads), f32)
    d_dtb = jnp.zeros((1, heads), f32)
    for c in range(blocks):
        span = slice(c * SPAN, (c + 1) * SPAN)
        d_w = col_ref[c] + fine(eye, row_ref[c], ((1,), (1,)))
        d_step = scol_ref[c] + fine(eye, srow_ref[c], ((1,), (1,)))
        d_rate = fine(lower, d_w, ((0,), (0,)))
        d_alog = d_alog + jnp.sum(rated[c][0] * d_rate, axis=0, keepdims=True)
        d_dt = (d_step - jnp.exp(alog_ref[...]) * d_rate) * slope_ref[span, :]
        ddt_ref[span, :] = d_dt
        d_dtb = d_dtb + jnp.sum(d_dt, axis=0, keepdims=True)
        low = dcross_ref[c].astype(bf16)
        dcmat_ref[span] += dot(low, b_blk[c])
        dbmat_ref[span] += dot(low, c_blk[c], ((0,), (0,)))
    dhead_ref[0:1, :] = d_alog
    dhead_ref[1:2, :] = d_dtb
    d_bc = jnp.concatenate([dbmat_ref[...], dcmat_ref[...]], axis=1)
    d_acc = d_bc * (bc_sig + bc_acc * bc_sig * (1.0 - bc_sig))
    d_x, d_taps, d_bias = conv_back(bc_in, wb_ref[...], d_acc)
    dbc_ref[...] = d_x
    for k in range(K):
        dwb_ref[k : k + 1, :] = d_taps[k]
    dbb_ref[...] = d_bias


def vmem_specs(count):
    return [pl.BlockSpec(memory_space=pltpu.VMEM)] * count


def ssd_forward(hsize, args):
    return pl.pallas_call(
        functools.partial(ssd_forward_kernel, hsize),
        out_shape=jax.ShapeDtypeStruct(args[0].shape, f32),
        in_specs=vmem_specs(len(args)),
        out_specs=vmem_specs(1)[0],
        name="ssd_forward",
    )(*args)


def ssd_backward(hsize, args):
    rows, inner = args[0].shape
    heads = args[6].shape[1]
    blocks = rows // SPAN
    shapes = [
        ((rows, inner), bf16),
        ((rows, 2 * N), f32),
        ((rows, heads), f32),
        ((K, inner), f32),
        ((1, inner), f32),
        ((K, 2 * N), f32),
        ((1, 2 * N), f32),
        ((2, heads), f32),
        ((1, inner), f32),
    ]
    return pl.pallas_call(
        functools.partial(ssd_backward_kernel, hsize),
        out_shape=[jax.ShapeDtypeStruct(a, b) for a, b in shapes],
        in_specs=vmem_specs(len(args)),
        out_specs=vmem_specs(len(shapes)),
        scratch_shapes=[
            pltpu.VMEM((blocks, SPAN, SPAN), f32),
            pltpu.VMEM((rows, N), f32),
            pltpu.VMEM((rows, N), f32),
            pltpu.VMEM((blocks, SPAN, heads), f32),
            pltpu.VMEM((blocks, SPAN, heads), f32),
            pltpu.VMEM((blocks, heads, SPAN), f32),
            pltpu.VMEM((blocks, heads, SPAN), f32),
        ],
        name="ssd_backward",
    )(*args)


def adamw(param_vec, grad_vec, first, second):
    first_new = beta_one * first + (1.0 - beta_one) * grad_vec
    second_new = beta_two * second + (1.0 - beta_two) * grad_vec * grad_vec
    first_hat = first_new / (1.0 - beta_one**adam_step)
    second_hat = second_new / (1.0 - beta_two**adam_step)
    updated = param_vec - learn_rate * (
        first_hat / (jnp.sqrt(second_hat) + adam_eps) + weight_decay * param_vec
    )
    return (updated, first_new, second_new)


class Plan:
    def __init__(self, dp, seq, flat):
        self.dp, self.seq, self.flat = dp, seq, flat
        self.total = dp * seq
        count = self.total
        self.mix = IN // flat
        last_in = -(-IN // flat)
        rows_in = max(
            -(-(((k * flat) % PROJ) + min(flat, IN - k * flat)) // PROJ) for k in range(last_in)
        )
        rows_out = max(
            -(-(((k * flat - IN) % D) + flat) // D) for k in range(self.mix, count)
        )
        self.rows = ceil_to(max(rows_in, -(-rows_out // 4)), 8)
        self.in_len = IN - self.mix * flat
        self.mix_in = -(-(((self.mix * flat) % PROJ) + self.in_len) // PROJ)
        self.mix_out = -(-(flat - self.in_len) // D)
        self.mix_free = self.rows - self.mix_in
        assert 4 * self.mix_free >= self.mix_out
        rows = self.rows
        self.j_in = self.mix // seq + 1
        self.j_out = self.mix // seq
        n_in, n_out = self.j_in, dp - self.j_out
        self.in_map = np.full((seq, n_in, rows), -1, np.int32)
        self.out_map = np.full((seq, n_out, 4, rows), -1, np.int32)
        m = np.arange(rows)
        for s in range(seq):
            for j in range(n_in):
                k = j * seq + s
                if k > self.mix:
                    continue
                first = (k * flat) // PROJ
                used = min(rows, D - first)
                if k == self.mix:
                    used = self.mix_in
                self.in_map[s, j, :used] = first + m[:used]
            for j in range(n_out):
                k = (j + self.j_out) * seq + s
                if k < self.mix:
                    continue
                for b in range(4):
                    if k == self.mix:
                        q = b * self.mix_free + (m - self.mix_in)
                        ok = (m >= self.mix_in) & (q < self.mix_out)
                    else:
                        q = (k * flat - IN) // D + b * rows + m
                        ok = q < min(DI, -(-((k + 1) * flat - IN) // D))
                    self.out_map[s, j, b] = np.where(ok, q, -1)

    def pack(self, flat, k):
        rows, size = self.rows, self.flat
        shift = (k * size) % PROJ
        span = rows * PROJ
        buf = jnp.pad(flat, (PROJ, span - size))
        win = lax.dynamic_slice(buf, (PROJ - shift,), (span,)).reshape(rows, PROJ)
        win = jnp.pad(win, ((0, 0), (0, WIDE - PROJ)))
        off = (k * size - IN) % D
        span = 4 * rows * D
        buf = jnp.pad(flat, (D, span - size))
        out = lax.dynamic_slice(buf, (D - off,), (span,)).reshape(4, rows, D)
        out = jnp.concatenate([out[b] for b in range(4)] + [jnp.zeros((rows, WIDE - 4 * D), flat.dtype)], axis=1)
        head = flat[self.in_len :]
        free = self.mix_free
        head = jnp.pad(head, (0, 4 * free * D - head.shape[0])).reshape(4, free, D)
        low = jnp.concatenate([head[b] for b in range(4)] + [jnp.zeros((free, WIDE - 4 * D), flat.dtype)], axis=1)
        mixed = jnp.concatenate([win[: self.mix_in], low], axis=0)
        return jnp.where(k < self.mix, win, jnp.where(k > self.mix, out, mixed))

    def unpack(self, chunk, k):
        rows, size = self.rows, self.flat
        shift = (k * size) % PROJ
        line = chunk[:, :PROJ].reshape(-1)
        line = jnp.pad(line, (0, max(0, PROJ + size - rows * PROJ)))
        win = lax.dynamic_slice(line, (shift,), (size,))
        off = (k * size - IN) % D
        line = jnp.concatenate([chunk[:, b * D : (b + 1) * D] for b in range(4)], axis=0).reshape(-1)
        line = jnp.pad(line, (0, max(0, D + size - 4 * rows * D)))
        out = lax.dynamic_slice(line, (off,), (size,))
        low = chunk[self.mix_in :]
        low = jnp.concatenate([low[:, b * D : (b + 1) * D] for b in range(4)], axis=0)
        mixed = jnp.concatenate([win[: self.in_len], low.reshape(-1)[: size - self.in_len]])
        return jnp.where(k < self.mix, win, jnp.where(k > self.mix, out, mixed))


def make(dp, seq):
    za, yb, cc = factors(dp)

    def place(z, y, c):
        return ((z % za) * yb + (y % yb)) * cc + (c % cc)

    def perm(dz, dy, dc):
        return [
            (place(z, y, c), place(z + dz, y + dy, c + dc))
            for z in range(za)
            for y in range(yb)
            for c in range(cc)
        ]

    z_next, y_next, c_next = perm(1, 0, 0), perm(0, 1, 0), perm(0, 0, 1)

    def gather_dp(chunk):
        j = lax.axis_index("dp")
        z, y, c = j // (yb * cc), (j // cc) % yb, j % cc
        whole = jnp.zeros((dp,) + chunk.shape, chunk.dtype)
        slots = []
        cur = chunk
        for r in range(za):
            if r:
                cur = lax.ppermute(cur, "dp", z_next)
            side = cur
            for t in range(yb):
                if t:
                    side = lax.ppermute(side, "dp", y_next)
                slots.append((z - r, y - t, c, side))
                if cc == 2:
                    slots.append((z - r, y - t, c + 1, lax.ppermute(side, "dp", c_next)))
        for zi, yi, ci, data in slots:
            at = (((zi + za) % za) * yb + (yi + yb) % yb) * cc + ci % cc
            whole = lax.dynamic_update_index_in_dim(whole, data, at, 0)
        return whole

    def scatter_dp(parts):
        j = lax.axis_index("dp")
        z, y, c = j // (yb * cc), (j // cc) % yb, j % cc

        def pick(zi, yi, ci):
            at = (((zi + za) % za) * yb + (yi + yb) % yb) * cc + ci % cc
            return lax.dynamic_index_in_dim(parts, at, 0, False)

        def core_sum(zi, yi):
            own = pick(zi, yi, c)
            if cc == 2:
                got = lax.ppermute(pick(zi, yi, c + 1), "dp", c_next)
                own = (own.astype(f32) + got.astype(f32)).astype(bf16)
            return own

        def mid_sum(zi):
            acc = None
            for r in range(1, yb + 1):
                mine = core_sum(zi, y - r)
                if acc is not None:
                    acc = (acc.astype(f32) + mine.astype(f32)).astype(bf16)
                else:
                    acc = mine
                if r < yb:
                    acc = lax.ppermute(acc, "dp", y_next)
            return acc

        acc = None
        for r in range(1, za + 1):
            mine = mid_sum(z - r)
            if acc is not None:
                acc = acc.astype(f32) + mine.astype(f32)
            else:
                acc = mine
            if r < za:
                acc = lax.ppermute(acc.astype(bf16), "dp", z_next)
        return acc.astype(f32)

    def swap_seq(a):
        return lax.ppermute(a, "seq", [(0, 1), (1, 0)])

    def halves(a, axis):
        n = a.shape[axis] // 2
        return lax.slice_in_dim(a, 0, n, axis=axis), lax.slice_in_dim(a, n, 2 * n, axis=axis)

    def gather_seq(a, axis):
        if seq != 2:
            return lax.all_gather(a, "seq", axis=axis, tiled=True)
        first = lax.axis_index("seq") == 0
        other = swap_seq(a)
        return jnp.concatenate([jnp.where(first, a, other), jnp.where(first, other, a)], axis=axis)

    def scatter_seq(a, axis):
        if seq != 2:
            return lax.psum_scatter(a, "seq", scatter_dimension=axis, tiled=True)
        first = lax.axis_index("seq") == 0
        low, high = halves(a, axis)
        got = swap_seq(jnp.where(first, high, low).astype(bf16))
        return jnp.where(first, low, high) + got.astype(f32)

    def sum_seq(a):
        if seq != 2:
            return lax.psum(a, "seq")
        a = a.astype(bf16)
        return a.astype(f32) + swap_seq(a).astype(f32)

    def sum_seq_wide(a):
        if seq != 2:
            return lax.psum(a, "seq")
        return a + swap_seq(a)

    def own_seq(a, axis):
        n = a.shape[axis] // seq
        return lax.dynamic_slice_in_dim(a, lax.axis_index("seq") * n, n, axis)

    def sum_all(a):
        for axis, count in (("seq", seq), ("dp", dp)):
            step = 1
            while step < count:
                a = a + lax.ppermute(a, axis, [(i, i ^ step) for i in range(count)])
                step *= 2
        return a

    def on_device(x_in, cotangent, params, moment_one, moment_two):
        size = params.shape[0]
        plan = Plan(dp, seq, size)
        rows = plan.rows
        s = lax.axis_index("seq")
        k = lax.axis_index("dp") * seq + s
        halfs = params.astype(bf16)

        x_own = x_in[0]
        cot_own = cotangent[0]
        tokens = gather_seq(x_own, 0)
        cot = gather_seq(cot_own, 0)

        base = IN + OUT
        at = base - k * size
        padded = jnp.pad(halfs, (SMALL, SMALL))
        tail = lax.dynamic_slice(padded, (jnp.clip(at + SMALL, 0, size + SMALL),), (SMALL,))
        tail = jnp.pad(tail, (0, -SMALL % D)).reshape(-1, D)
        small = sum_all(tail).reshape(-1)
        pieces = []
        offset = 0
        for length in (K * CONV, CONV, D, DI, H, H, H):
            pieces.append(small[offset : offset + length].astype(f32))
            offset += length
        conv_w, conv_b, norm_g, gate_g, a_log, dt_bias, skip_gain = pieces
        conv_w = conv_w.reshape(K, CONV)

        chunk = plan.pack(halfs, k)
        whole = gather_dp(chunk)
        n_in, n_out = plan.j_in, dp - plan.j_out
        w_in = whole[:n_in].reshape(n_in * rows, WIDE)
        w_out = [
            whole[plan.j_out :, :, b * D : (b + 1) * D].reshape(n_out * rows, D) for b in range(4)
        ]
        in_map = lax.dynamic_index_in_dim(jnp.asarray(plan.in_map.reshape(seq, -1)), s, 0, False)
        out_map = lax.dynamic_index_in_dim(
            jnp.asarray(plan.out_map.transpose(0, 2, 1, 3).reshape(seq, 4, -1)), s, 0, False
        )
        pick_in = (jnp.arange(D)[:, None] == in_map[None, :]).astype(bf16)
        pick_out = [(jnp.arange(DI)[:, None] == out_map[b][None, :]).astype(bf16) for b in range(4)]

        wide = tokens.astype(f32)
        scale = lax.rsqrt(jnp.mean(wide * wide, axis=-1, keepdims=True) + norm_eps)
        normed = (wide * scale * norm_g[None, :]).astype(bf16)
        normed_k = dot(normed, pick_in).astype(bf16)
        partial = dot(normed_k, w_in)

        x_part = scatter_seq(partial[:, DI : 2 * DI], 1)
        bcdt = sum_seq(partial[:, 2 * DI : PROJ])
        z_part = scatter_seq(partial[:, :DI], 1)
        gate_in = z_part.astype(bf16).astype(f32)
        x_pre = x_part.astype(bf16)
        bc_pre = bcdt[:, : 2 * N].astype(bf16)
        dt_raw = own_seq(bcdt[:, 2 * N :], 1).astype(bf16).astype(f32)
        inner = DI // seq
        hsize = DI // H
        dt_in = dt_raw + own_seq(dt_bias, 0)[None, :]
        step_size = jax.nn.softplus(dt_in)
        alog = own_seq(a_log, 0)[None, :]
        ssd_args = (
            x_pre,
            bc_pre,
            own_seq(conv_w[:, :DI], 1),
            own_seq(conv_b[:DI], 0)[None, :],
            conv_w[:, DI:],
            conv_b[None, DI:],
            step_size,
            step_size.T,
            alog,
            alog.T,
            jnp.repeat(own_seq(skip_gain, 0), hsize)[None, :],
        )
        ssd_out = ssd_forward(hsize, ssd_args)

        d_gated = None
        for b in range(4):
            piece = dot(cot, w_out[b], ((1,), (1,))).astype(bf16)
            piece = dot(piece, pick_out[b], ((1,), (1,)))
            d_gated = piece if d_gated is None else d_gated + piece
        d_gated = scatter_seq(d_gated, 1)

        gain = own_seq(gate_g, 0)[None, :]
        sig = jax.nn.sigmoid(gate_in)
        swish = gate_in * sig
        gated = ssd_out * swish
        weighted = d_gated * gain
        sums = jnp.stack([jnp.sum(gated * gated, axis=1), jnp.sum(weighted * gated, axis=1)])
        sums = sum_seq_wide(sums)
        g_scale = lax.rsqrt(sums[0] / DI + norm_eps)[:, None]
        cross = (sums[1] / DI)[:, None]
        gated_norm = (gated * g_scale * gain).astype(bf16)
        d_gate_g = jnp.sum(d_gated * gated * g_scale, axis=0)
        d_pre = g_scale * weighted - gated * g_scale**3 * cross
        d_ssd = d_pre * swish
        d_gate_in = d_pre * ssd_out * (sig + swish * (1.0 - sig))

        gn_full = gather_seq(gated_norm, 1)
        gn_k = [dot(gn_full, pick_out[b]).astype(bf16) for b in range(4)]
        y_part = None
        for b in range(4):
            piece = dot(gn_k[b], w_out[b])
            y_part = piece if y_part is None else y_part + piece
        y_own = scatter_seq(y_part, 0) + x_own.astype(f32)

        d_x, d_bcpre, d_dtraw, d_wx, d_bx, d_wb, d_bb, d_head, d_skip = ssd_backward(
            hsize, ssd_args + (jax.nn.sigmoid(dt_in), d_ssd)
        )
        d_alog, d_dtbias = d_head[0], d_head[1]
        d_skip = jnp.sum(d_skip.reshape(-1, hsize), axis=1)
        d_z_full = gather_seq(d_gate_in.astype(bf16), 1)
        d_x_full = gather_seq(d_x, 1)
        d_bc = sum_seq(d_bcpre).astype(bf16)
        d_dt_full = gather_seq(d_dtraw.astype(bf16), 1)
        pad = jnp.zeros((d_bc.shape[0], WIDE - PROJ), bf16)
        d_mixed = jnp.concatenate([d_z_full, d_x_full, d_bc, d_dt_full, pad], axis=1)

        g_in = dot(normed_k, d_mixed, ((0,), (0,))).astype(bf16).reshape(n_in, rows, WIDE)
        g_out = jnp.concatenate(
            [dot(gn_k[b], cot, ((0,), (0,))).astype(bf16).reshape(n_out, rows, D) for b in range(4)]
            + [jnp.zeros((n_out, rows, WIDE - 4 * D), bf16)],
            axis=2,
        )
        both = n_in + n_out - dp
        parts = jnp.concatenate(
            [g_in[: n_in - both], g_in[n_in - both :] + g_out[:both], g_out[both:]], axis=0
        )

        dn_k = dot(d_mixed, w_in, ((1,), (1,))).astype(bf16)
        d_normed = scatter_seq(dot(dn_k, pick_in, ((1,), (1,))), 0)
        wide_own = x_own.astype(f32)
        scale_own = lax.rsqrt(jnp.mean(wide_own * wide_own, axis=-1, keepdims=True) + norm_eps)
        a_own = d_normed * norm_g[None, :]
        d_norm_g = jnp.sum(d_normed * wide_own * scale_own, axis=0)
        d_wide = scale_own * a_own - wide_own * scale_own**3 * jnp.mean(
            a_own * wide_own, axis=-1, keepdims=True
        )
        input_grad = (cot_own.astype(f32) + d_wide).astype(bf16)

        def spread(a, width):
            full = jnp.zeros(a.shape[:-1] + (width,), f32)
            start = (0,) * (a.ndim - 1) + (s * a.shape[-1],)
            return lax.dynamic_update_slice(full, a, start)

        small_grad = jnp.concatenate(
            [
                jnp.concatenate([spread(d_wx, DI), d_wb], axis=1).reshape(-1),
                spread(d_bx[0], DI),
                d_bb[0],
                d_norm_g,
                spread(d_gate_g, DI),
                spread(d_alog, H),
                spread(d_dtbias, H),
                spread(d_skip, H),
            ]
        )
        small_grad = jnp.pad(small_grad, (0, -SMALL % D)).reshape(-1, D)
        small_grad = sum_all(small_grad).reshape(-1)[:SMALL]

        grad_chunk = scatter_dp(parts)
        shard = plan.unpack(grad_chunk, k)
        wing = jnp.pad(small_grad, (size, size))
        shard = shard + lax.dynamic_slice(
            wing, (jnp.clip(size - at, 0, size + SMALL),), (size,)
        )
        updated, first_new, second_new = adamw(params, shard, moment_one, moment_two)
        return (y_own.astype(bf16)[None], input_grad[None], shard, updated, first_new, second_new)

    return on_device


def solution(mesh):
    return jax.shard_map(
        make(mesh.shape["dp"], mesh.shape["seq"]),
        mesh=mesh,
        in_specs=(
            P("dp", "seq", None),
            P("dp", "seq", None),
            P(("dp", "seq")),
            P(("dp", "seq")),
            P(("dp", "seq")),
        ),
        out_specs=(
            P("dp", "seq", None),
            P("dp", "seq", None),
            P(("dp", "seq")),
            P(("dp", "seq")),
            P(("dp", "seq")),
            P(("dp", "seq")),
        ),
        check_vma=False,
    )
```

```python
import functools
import jax
import jax.numpy as jnp
import numpy as np
from jax import lax
from jax.experimental import pallas as pl
from jax.experimental.pallas import tpu as pltpu
from jax.sharding import PartitionSpec as P

D = 1024
DI = 2048
N = 128
K = 4
SPAN = 128
H = 32
CONV = 2304
PROJ = 4384
WIDE = 4480
IN = D * PROJ
OUT = DI * D
SMALL = K * CONV + CONV + D + DI + 3 * H

norm_eps = 1e-05
learn_rate = 0.005
beta_one = 0.9
beta_two = 0.95
adam_eps = 1e-08
weight_decay = 0.1
adam_step = 10

bf16 = jnp.bfloat16
f32 = jnp.float32


def ceil_to(value, unit):
    return -(-value // unit) * unit


def factors(count):
    core = 2 if count % 2 == 0 else 1
    rest = count // core
    mid = 1
    while rest % (mid * 2) == 0 and (mid * 2) ** 2 <= rest * 1:
        mid *= 2
    return rest // mid, mid, core


def dot(a, b, dims=((1,), (0,))):
    return lax.dot_general(a, b, (dims, ((), ())), preferred_element_type=f32)


def col_roll(a, steps):
    rows = a.shape[0]
    at = lax.broadcasted_iota(jnp.int32, a.shape, 0)
    if steps >= 0:
        return jnp.where(at >= steps, pltpu.roll(a, steps, 0), 0.0)
    return jnp.where(at < rows + steps, pltpu.roll(a, rows + steps, 0), 0.0)


def conv_act(x, taps, bias):
    acc = bias + taps[K - 1 : K] * x
    for k in range(1, K):
        acc = acc + taps[K - 1 - k : K - k] * col_roll(x, k)
    sig = 1.0 / (1.0 + jnp.exp(-acc))
    return acc, sig


def conv_back(x, taps, d_acc):
    d_x = taps[K - 1 : K] * d_acc
    d_taps = [jnp.sum(d_acc * x, axis=0, keepdims=True)]
    for k in range(1, K):
        d_x = d_x + taps[K - 1 - k : K - k] * col_roll(d_acc, -k)
        d_taps.insert(0, jnp.sum(d_acc * col_roll(x, k), axis=0, keepdims=True))
    return d_x, d_taps, jnp.sum(d_acc, axis=0, keepdims=True)


def fine(a, b, dims):
    return lax.dot_general(
        a, b, (dims, ((), ())), precision=lax.Precision.HIGHEST, preferred_element_type=f32
    )


def tri_parts():
    row = lax.broadcasted_iota(jnp.int32, (SPAN, SPAN), 0)
    col = lax.broadcasted_iota(jnp.int32, (SPAN, SPAN), 1)
    return row >= col, row == col


def rates(c, step_ref, turn_ref, alog_ref, alog_turn_ref, lower):
    span = slice(c * SPAN, (c + 1) * SPAN)
    rate = step_ref[span, :] * -jnp.exp(alog_ref[...])
    rate_turn = turn_ref[:, span] * -jnp.exp(alog_turn_ref[...])
    within = fine(lower, rate, ((1,), (0,)))
    within_turn = fine(rate_turn, lower, ((1,), (1,)))
    return rate, within, within_turn


def lanes_of(pair, first, second):
    lane = lax.broadcasted_iota(jnp.int32, (1, 2 * pair), 1)
    return jnp.where(lane < pair, first, second)


def ssd_forward_kernel(
    hsize, x_ref, bc_ref, wx_ref, bx_ref, wb_ref, bb_ref, step_ref, turn_ref, alog_ref, alog_turn_ref, skip_ref, out_ref
):
    rows, inner = x_ref.shape
    blocks = rows // SPAN
    causal, _ = tri_parts()
    lower = causal.astype(f32)
    acc, sig = conv_act(bc_ref[...].astype(f32), wb_ref[...], bb_ref[...])
    bc = (acc * sig).astype(bf16)
    b_blk = [bc[c * SPAN : (c + 1) * SPAN, :N] for c in range(blocks)]
    c_blk = [bc[c * SPAN : (c + 1) * SPAN, N:] for c in range(blocks)]
    cross = [dot(c_blk[c], b_blk[c], ((1,), (1,))) for c in range(blocks)]
    rated = [rates(c, step_ref, turn_ref, alog_ref, alog_turn_ref, lower) for c in range(blocks)]
    width = 2 * hsize
    lane = lax.broadcasted_iota(jnp.int32, (1, width), 1)
    masks = [(lane < hsize).astype(f32), (lane >= hsize).astype(f32)]
    for g in range(inner // width):
        cols = slice(g * width, (g + 1) * width)
        acc, sig = conv_act(x_ref[:, cols].astype(f32), wx_ref[:, cols], bx_ref[:, cols])
        vals = acc * sig
        state = None
        for c in range(blocks):
            span = slice(c * SPAN, (c + 1) * SPAN)
            _, within, within_turn = rated[c]
            v = vals[span]
            mix, split = [], []
            for i in range(2):
                h = 2 * g + i
                gap = within[:, h : h + 1] - within_turn[h : h + 1, :]
                mix.append(
                    (jnp.exp(jnp.where(causal, gap, -10000.0)) * cross[c] * turn_ref[h : h + 1, span]).astype(bf16)
                )
                split.append((v * masks[i]).astype(bf16))
            out = dot(jnp.concatenate(mix, axis=1), jnp.concatenate(split, axis=0))
            w0, w1 = within[:, 2 * g : 2 * g + 1], within[:, 2 * g + 1 : 2 * g + 2]
            if state is not None:
                out = out + lanes_of(hsize, jnp.exp(w0), jnp.exp(w1)) * dot(c_blk[c], state.astype(bf16))
            out_ref[span, cols] = out + skip_ref[:, cols] * v
            if c < blocks - 1:
                e0, e1 = w0[SPAN - 1 :], w1[SPAN - 1 :]
                tail = lanes_of(
                    hsize,
                    jnp.exp(e0 - w0) * step_ref[span, 2 * g : 2 * g + 1],
                    jnp.exp(e1 - w1) * step_ref[span, 2 * g + 1 : 2 * g + 2],
                )
                fresh = dot(b_blk[c], (tail * v).astype(bf16), ((0,), (0,)))
                if state is not None:
                    fresh = fresh + lanes_of(hsize, jnp.exp(e0), jnp.exp(e1)) * state
                state = fresh


def ssd_backward_kernel(
    hsize, x_ref, bc_ref, wx_ref, bx_ref, wb_ref, bb_ref, step_ref, turn_ref, alog_ref, alog_turn_ref, skip_ref,
    slope_ref, dy_ref, dx_ref, dbc_ref, ddt_ref, dwx_ref, dbx_ref, dwb_ref, dbb_ref, dhead_ref, dskip_ref,
    dcross_ref, dbmat_ref, dcmat_ref, col_ref, scol_ref, row_ref, srow_ref,
):
    rows, inner = x_ref.shape
    heads = step_ref.shape[1]
    blocks = rows // SPAN
    causal, eye = tri_parts()
    lower = causal.astype(f32)
    eye = eye.astype(f32)
    bc_in = bc_ref[...].astype(f32)
    bc_acc, bc_sig = conv_act(bc_in, wb_ref[...], bb_ref[...])
    bc = (bc_acc * bc_sig).astype(bf16)
    b_blk = [bc[c * SPAN : (c + 1) * SPAN, :N] for c in range(blocks)]
    c_blk = [bc[c * SPAN : (c + 1) * SPAN, N:] for c in range(blocks)]
    cross = [dot(c_blk[c], b_blk[c], ((1,), (1,))) for c in range(blocks)]
    rated = [rates(c, step_ref, turn_ref, alog_ref, alog_turn_ref, lower) for c in range(blocks)]
    for ref in (dcross_ref, dbmat_ref, dcmat_ref, col_ref, scol_ref, row_ref, srow_ref):
        ref[...] = jnp.zeros_like(ref)
    width = 2 * hsize
    lane = lax.broadcasted_iota(jnp.int32, (1, width), 1)
    masks = [(lane < hsize).astype(f32), (lane >= hsize).astype(f32)]
    head_lane = lax.broadcasted_iota(jnp.int32, (1, heads), 1)
    head_row = lax.broadcasted_iota(jnp.int32, (heads, 1), 0)
    last_row = lax.broadcasted_iota(jnp.int32, (SPAN, 1), 0) == SPAN - 1
    for g in range(inner // width):
        cols = slice(g * width, (g + 1) * width)
        x = x_ref[:, cols].astype(f32)
        acc, sig = conv_act(x, wx_ref[:, cols], bx_ref[:, cols])
        vals = acc * sig
        states, tails, decays = [None], [], []
        for c in range(blocks):
            span = slice(c * SPAN, (c + 1) * SPAN)
            within = rated[c][1]
            w0, w1 = within[:, 2 * g : 2 * g + 1], within[:, 2 * g + 1 : 2 * g + 2]
            e0, e1 = w0[SPAN - 1 :], w1[SPAN - 1 :]
            if c < blocks - 1:
                tails.append(
                    lanes_of(
                        hsize,
                        jnp.exp(e0 - w0) * step_ref[span, 2 * g : 2 * g + 1],
                        jnp.exp(e1 - w1) * step_ref[span, 2 * g + 1 : 2 * g + 2],
                    )
                )
                decays.append(lanes_of(hsize, jnp.exp(e0), jnp.exp(e1)))
                fresh = dot(b_blk[c], (tails[c] * vals[span]).astype(bf16), ((0,), (0,)))
                if states[c] is not None:
                    fresh = fresh + decays[c] * states[c]
                states.append(fresh)
        d_state = None
        d_vals = [None] * blocks
        d_skip = jnp.zeros((1, width), f32)
        for c in reversed(range(blocks)):
            span = slice(c * SPAN, (c + 1) * SPAN)
            _, within, within_turn = rated[c]
            v = vals[span]
            v_low = v.astype(bf16)
            dy = dy_ref[span, cols].astype(f32)
            ws = [within[:, 2 * g + i : 2 * g + i + 1] for i in range(2)]
            mix, split, d_w = [], [], []
            d_cross = None
            for i in range(2):
                h = 2 * g + i
                turn = turn_ref[h : h + 1, span]
                decay = jnp.exp(jnp.where(causal, ws[i] - within_turn[h : h + 1, :], -10000.0))
                scored = decay * cross[c]
                mix.append((scored * turn).astype(bf16))
                d_half = (dy * masks[i]).astype(bf16)
                split.append(d_half)
                d_mix = dot(d_half, v_low, ((1,), (1,)))
                raw = d_mix * scored
                part = d_mix * decay * turn
                d_cross = part if d_cross is None else d_cross + part
                d_w.append(jnp.sum(raw * turn, axis=1, keepdims=True))
                raw_sum = jnp.sum(raw, axis=0, keepdims=True)
                row_ref[c] += jnp.where(head_row == h, -raw_sum * turn, 0.0)
                srow_ref[c] += jnp.where(head_row == h, raw_sum, 0.0)
            dcross_ref[c] += d_cross
            d_v = dot(jnp.concatenate(mix, axis=0), jnp.concatenate(split, axis=0), ((0,), (0,)))
            d_v = d_v + skip_ref[:, cols] * dy
            d_skip = d_skip + jnp.sum(dy * v, axis=0, keepdims=True)
            d_enter = None
            if states[c] is not None:
                st = states[c].astype(bf16)
                lifted = lanes_of(hsize, jnp.exp(ws[0]), jnp.exp(ws[1])) * dy
                lift_low = lifted.astype(bf16)
                dcmat_ref[span] += dot(lift_low, st, ((1,), (1,)))
                d_enter = dot(c_blk[c], lift_low, ((0,), (0,)))
                prod = lifted * dot(c_blk[c], st)
                for i in range(2):
                    d_w[i] = d_w[i] + jnp.sum(prod * masks[i], axis=1, keepdims=True)
            if d_state is not None:
                ds_low = d_state.astype(bf16)
                back = dot(b_blk[c], ds_low)
                d_v = d_v + tails[c] * back
                dbmat_ref[span] += dot((tails[c] * v).astype(bf16), ds_low, ((1,), (1,)))
                along = v * back
                if states[c] is not None:
                    held = decays[c] * d_state * states[c]
                for i in range(2):
                    h = 2 * g + i
                    d_tail = jnp.sum(along * masks[i], axis=1, keepdims=True)
                    reach = jnp.exp(ws[i][SPAN - 1 :] - ws[i])
                    scol_ref[c] += jnp.where(head_lane == h, d_tail * reach, 0.0)
                    fall = d_tail * reach * step_ref[span, h : h + 1]
                    d_end = jnp.sum(fall, axis=0, keepdims=True)
                    if states[c] is not None:
                        d_end = d_end + jnp.sum(
                            jnp.sum(held * masks[i], axis=1, keepdims=True), axis=0, keepdims=True
                        )
                    d_w[i] = d_w[i] - fall + jnp.where(last_row, d_end, 0.0)
                if d_enter is not None:
                    d_enter = d_enter + decays[c] * d_state
            for i in range(2):
                col_ref[c] += jnp.where(head_lane == 2 * g + i, d_w[i], 0.0)
            d_state = d_enter
            d_vals[c] = d_v
        d_acc = jnp.concatenate(d_vals, axis=0) * (sig + vals * (1.0 - sig))
        d_x, d_taps, d_bias = conv_back(x, wx_ref[:, cols], d_acc)
        dx_ref[:, cols] = d_x.astype(bf16)
        for k in range(K):
            dwx_ref[k : k + 1, cols] = d_taps[k]
        dbx_ref[:, cols] = d_bias
        dskip_ref[:, cols] = d_skip
    d_alog = jnp.zeros((1, heads), f32)
    d_dtb = jnp.zeros((1, heads), f32)
    for c in range(blocks):
        span = slice(c * SPAN, (c + 1) * SPAN)
        d_w = col_ref[c] + fine(eye, row_ref[c], ((1,), (1,)))
        d_step = scol_ref[c] + fine(eye, srow_ref[c], ((1,), (1,)))
        d_rate = fine(lower, d_w, ((0,), (0,)))
        d_alog = d_alog + jnp.sum(rated[c][0] * d_rate, axis=0, keepdims=True)
        d_dt = (d_step - jnp.exp(alog_ref[...]) * d_rate) * slope_ref[span, :]
        ddt_ref[span, :] = d_dt
        d_dtb = d_dtb + jnp.sum(d_dt, axis=0, keepdims=True)
        low = dcross_ref[c].astype(bf16)
        dcmat_ref[span] += dot(low, b_blk[c])
        dbmat_ref[span] += dot(low, c_blk[c], ((0,), (0,)))
    dhead_ref[0:1, :] = d_alog
    dhead_ref[1:2, :] = d_dtb
    d_bc = jnp.concatenate([dbmat_ref[...], dcmat_ref[...]], axis=1)
    d_acc = d_bc * (bc_sig + bc_acc * bc_sig * (1.0 - bc_sig))
    d_x, d_taps, d_bias = conv_back(bc_in, wb_ref[...], d_acc)
    dbc_ref[...] = d_x
    for k in range(K):
        dwb_ref[k : k + 1, :] = d_taps[k]
    dbb_ref[...] = d_bias


def vmem_specs(count):
    return [pl.BlockSpec(memory_space=pltpu.VMEM)] * count


def ssd_forward(hsize, args):
    return pl.pallas_call(
        functools.partial(ssd_forward_kernel, hsize),
        out_shape=jax.ShapeDtypeStruct(args[0].shape, f32),
        in_specs=vmem_specs(len(args)),
        out_specs=vmem_specs(1)[0],
        cost_estimate=pl.CostEstimate(flops=int(2.5e9), transcendentals=0, bytes_accessed=int(1e7)),
        name="ssd_forward",
    )(*args)


def ssd_backward(hsize, args):
    rows, inner = args[0].shape
    heads = args[6].shape[1]
    blocks = rows // SPAN
    shapes = [
        ((rows, inner), bf16),
        ((rows, 2 * N), f32),
        ((rows, heads), f32),
        ((K, inner), f32),
        ((1, inner), f32),
        ((K, 2 * N), f32),
        ((1, 2 * N), f32),
        ((2, heads), f32),
        ((1, inner), f32),
    ]
    return pl.pallas_call(
        functools.partial(ssd_backward_kernel, hsize),
        out_shape=[jax.ShapeDtypeStruct(a, b) for a, b in shapes],
        in_specs=vmem_specs(len(args)),
        out_specs=vmem_specs(len(shapes)),
        scratch_shapes=[
            pltpu.VMEM((blocks, SPAN, SPAN), f32),
            pltpu.VMEM((rows, N), f32),
            pltpu.VMEM((rows, N), f32),
            pltpu.VMEM((blocks, SPAN, heads), f32),
            pltpu.VMEM((blocks, SPAN, heads), f32),
            pltpu.VMEM((blocks, heads, SPAN), f32),
            pltpu.VMEM((blocks, heads, SPAN), f32),
        ],
        cost_estimate=pl.CostEstimate(flops=int(6e9), transcendentals=0, bytes_accessed=int(2.4e7)),
        name="ssd_backward",
    )(*args)


def adamw(param_vec, grad_vec, first, second):
    first_new = beta_one * first + (1.0 - beta_one) * grad_vec
    second_new = beta_two * second + (1.0 - beta_two) * grad_vec * grad_vec
    first_hat = first_new / (1.0 - beta_one**adam_step)
    second_hat = second_new / (1.0 - beta_two**adam_step)
    updated = param_vec - learn_rate * (
        first_hat / (jnp.sqrt(second_hat) + adam_eps) + weight_decay * param_vec
    )
    return (updated, first_new, second_new)


class Plan:
    def __init__(self, dp, seq, flat):
        self.dp, self.seq, self.flat = dp, seq, flat
        self.total = dp * seq
        count = self.total
        self.mix = IN // flat
        last_in = -(-IN // flat)
        rows_in = max(
            -(-(((k * flat) % PROJ) + min(flat, IN - k * flat)) // PROJ) for k in range(last_in)
        )
        rows_out = max(
            -(-(((k * flat - IN) % D) + flat) // D) for k in range(self.mix, count)
        )
        self.rows = ceil_to(max(rows_in, -(-rows_out // 4)), 8)
        self.in_len = IN - self.mix * flat
        self.mix_in = -(-(((self.mix * flat) % PROJ) + self.in_len) // PROJ)
        self.mix_out = -(-(flat - self.in_len) // D)
        self.mix_free = self.rows - self.mix_in
        assert 4 * self.mix_free >= self.mix_out
        rows = self.rows
        self.j_in = self.mix // seq + 1
        self.j_out = self.mix // seq
        n_in, n_out = self.j_in, dp - self.j_out
        self.in_map = np.full((seq, n_in, rows), -1, np.int32)
        self.out_map = np.full((seq, n_out, 4, rows), -1, np.int32)
        m = np.arange(rows)
        for s in range(seq):
            for j in range(n_in):
                k = j * seq + s
                if k > self.mix:
                    continue
                first = (k * flat) // PROJ
                used = min(rows, D - first)
                if k == self.mix:
                    used = self.mix_in
                self.in_map[s, j, :used] = first + m[:used]
            for j in range(n_out):
                k = (j + self.j_out) * seq + s
                if k < self.mix:
                    continue
                for b in range(4):
                    if k == self.mix:
                        q = b * self.mix_free + (m - self.mix_in)
                        ok = (m >= self.mix_in) & (q < self.mix_out)
                    else:
                        q = (k * flat - IN) // D + b * rows + m
                        ok = q < min(DI, -(-((k + 1) * flat - IN) // D))
                    self.out_map[s, j, b] = np.where(ok, q, -1)

    def pack(self, flat, k):
        rows, size = self.rows, self.flat
        shift = (k * size) % PROJ
        span = rows * PROJ
        buf = jnp.pad(flat, (PROJ, span - size))
        win = lax.dynamic_slice(buf, (PROJ - shift,), (span,)).reshape(rows, PROJ)
        win = jnp.pad(win, ((0, 0), (0, WIDE - PROJ)))
        off = (k * size - IN) % D
        span = 4 * rows * D
        buf = jnp.pad(flat, (D, span - size))
        out = lax.dynamic_slice(buf, (D - off,), (span,)).reshape(4, rows, D)
        out = jnp.concatenate([out[b] for b in range(4)] + [jnp.zeros((rows, WIDE - 4 * D), flat.dtype)], axis=1)
        head = flat[self.in_len :]
        free = self.mix_free
        head = jnp.pad(head, (0, 4 * free * D - head.shape[0])).reshape(4, free, D)
        low = jnp.concatenate([head[b] for b in range(4)] + [jnp.zeros((free, WIDE - 4 * D), flat.dtype)], axis=1)
        mixed = jnp.concatenate([win[: self.mix_in], low], axis=0)
        return jnp.where(k < self.mix, win, jnp.where(k > self.mix, out, mixed))

    def unpack(self, chunk, k):
        rows, size = self.rows, self.flat
        shift = (k * size) % PROJ
        line = chunk[:, :PROJ].reshape(-1)
        line = jnp.pad(line, (0, max(0, PROJ + size - rows * PROJ)))
        win = lax.dynamic_slice(line, (shift,), (size,))
        off = (k * size - IN) % D
        line = jnp.concatenate([chunk[:, b * D : (b + 1) * D] for b in range(4)], axis=0).reshape(-1)
        line = jnp.pad(line, (0, max(0, D + size - 4 * rows * D)))
        out = lax.dynamic_slice(line, (off,), (size,))
        low = chunk[self.mix_in :]
        low = jnp.concatenate([low[:, b * D : (b + 1) * D] for b in range(4)], axis=0)
        mixed = jnp.concatenate([win[: self.in_len], low.reshape(-1)[: size - self.in_len]])
        return jnp.where(k < self.mix, win, jnp.where(k > self.mix, out, mixed))


def make_general(dp, seq):
    za, yb, cc = factors(dp)

    def place(z, y, c):
        return ((z % za) * yb + (y % yb)) * cc + (c % cc)

    def perm(dz, dy, dc):
        return [
            (place(z, y, c), place(z + dz, y + dy, c + dc))
            for z in range(za)
            for y in range(yb)
            for c in range(cc)
        ]

    z_next, y_next, c_next = perm(1, 0, 0), perm(0, 1, 0), perm(0, 0, 1)

    def gather_dp(chunk):
        j = lax.axis_index("dp")
        z, y, c = j // (yb * cc), (j // cc) % yb, j % cc
        whole = jnp.zeros((dp,) + chunk.shape, chunk.dtype)
        slots = []
        cur = chunk
        for r in range(za):
            if r:
                cur = lax.ppermute(cur, "dp", z_next)
            side = cur
            for t in range(yb):
                if t:
                    side = lax.ppermute(side, "dp", y_next)
                slots.append((z - r, y - t, c, side))
                if cc == 2:
                    slots.append((z - r, y - t, c + 1, lax.ppermute(side, "dp", c_next)))
        for zi, yi, ci, data in slots:
            at = (((zi + za) % za) * yb + (yi + yb) % yb) * cc + ci % cc
            whole = lax.dynamic_update_index_in_dim(whole, data, at, 0)
        return whole

    def scatter_dp(parts):
        j = lax.axis_index("dp")
        z, y, c = j // (yb * cc), (j // cc) % yb, j % cc

        def pick(zi, yi, ci):
            at = (((zi + za) % za) * yb + (yi + yb) % yb) * cc + ci % cc
            return lax.dynamic_index_in_dim(parts, at, 0, False)

        def core_sum(zi, yi):
            own = pick(zi, yi, c)
            if cc == 2:
                got = lax.ppermute(pick(zi, yi, c + 1), "dp", c_next)
                own = (own.astype(f32) + got.astype(f32)).astype(bf16)
            return own

        def mid_sum(zi):
            acc = None
            for r in range(1, yb + 1):
                mine = core_sum(zi, y - r)
                if acc is not None:
                    acc = (acc.astype(f32) + mine.astype(f32)).astype(bf16)
                else:
                    acc = mine
                if r < yb:
                    acc = lax.ppermute(acc, "dp", y_next)
            return acc

        acc = None
        for r in range(1, za + 1):
            mine = mid_sum(z - r)
            if acc is not None:
                acc = acc.astype(f32) + mine.astype(f32)
            else:
                acc = mine
            if r < za:
                acc = lax.ppermute(acc.astype(bf16), "dp", z_next)
        return acc.astype(f32)

    def swap_seq(a):
        return lax.ppermute(a, "seq", [(0, 1), (1, 0)])

    def halves(a, axis):
        n = a.shape[axis] // 2
        return lax.slice_in_dim(a, 0, n, axis=axis), lax.slice_in_dim(a, n, 2 * n, axis=axis)

    def gather_seq(a, axis):
        if seq != 2:
            return lax.all_gather(a, "seq", axis=axis, tiled=True)
        first = lax.axis_index("seq") == 0
        other = swap_seq(a)
        return jnp.concatenate([jnp.where(first, a, other), jnp.where(first, other, a)], axis=axis)

    def scatter_seq(a, axis):
        if seq != 2:
            return lax.psum_scatter(a, "seq", scatter_dimension=axis, tiled=True)
        first = lax.axis_index("seq") == 0
        low, high = halves(a, axis)
        got = swap_seq(jnp.where(first, high, low).astype(bf16))
        return jnp.where(first, low, high) + got.astype(f32)

    def sum_seq(a):
        if seq != 2:
            return lax.psum(a, "seq")
        a = a.astype(bf16)
        return a.astype(f32) + swap_seq(a).astype(f32)

    def sum_seq_wide(a):
        if seq != 2:
            return lax.psum(a, "seq")
        return a + swap_seq(a)

    def own_seq(a, axis):
        n = a.shape[axis] // seq
        return lax.dynamic_slice_in_dim(a, lax.axis_index("seq") * n, n, axis)

    def sum_all(a):
        for axis, count in (("seq", seq), ("dp", dp)):
            step = 1
            while step < count:
                a = a + lax.ppermute(a, axis, [(i, i ^ step) for i in range(count)])
                step *= 2
        return a

    def on_device(x_in, cotangent, params, moment_one, moment_two):
        size = params.shape[0]
        plan = Plan(dp, seq, size)
        rows = plan.rows
        s = lax.axis_index("seq")
        k = lax.axis_index("dp") * seq + s
        halfs = params.astype(bf16)

        x_own = x_in[0]
        cot_own = cotangent[0]
        tokens = gather_seq(x_own, 0)
        cot = gather_seq(cot_own, 0)

        base = IN + OUT
        at = base - k * size
        padded = jnp.pad(halfs, (SMALL, SMALL))
        tail = lax.dynamic_slice(padded, (jnp.clip(at + SMALL, 0, size + SMALL),), (SMALL,))
        tail = jnp.pad(tail, (0, -SMALL % D)).reshape(-1, D)
        small = sum_all(tail).reshape(-1)
        pieces = []
        offset = 0
        for length in (K * CONV, CONV, D, DI, H, H, H):
            pieces.append(small[offset : offset + length].astype(f32))
            offset += length
        conv_w, conv_b, norm_g, gate_g, a_log, dt_bias, skip_gain = pieces
        conv_w = conv_w.reshape(K, CONV)

        chunk = plan.pack(halfs, k)
        whole = gather_dp(chunk)
        n_in, n_out = plan.j_in, dp - plan.j_out
        w_in = whole[:n_in].reshape(n_in * rows, WIDE)
        w_out = [
            whole[plan.j_out :, :, b * D : (b + 1) * D].reshape(n_out * rows, D) for b in range(4)
        ]
        in_map = lax.dynamic_index_in_dim(jnp.asarray(plan.in_map.reshape(seq, -1)), s, 0, False)
        out_map = lax.dynamic_index_in_dim(
            jnp.asarray(plan.out_map.transpose(0, 2, 1, 3).reshape(seq, 4, -1)), s, 0, False
        )
        pick_in = (jnp.arange(D)[:, None] == in_map[None, :]).astype(bf16)
        pick_out = [(jnp.arange(DI)[:, None] == out_map[b][None, :]).astype(bf16) for b in range(4)]

        wide = tokens.astype(f32)
        scale = lax.rsqrt(jnp.mean(wide * wide, axis=-1, keepdims=True) + norm_eps)
        normed = (wide * scale * norm_g[None, :]).astype(bf16)
        normed_k = dot(normed, pick_in).astype(bf16)
        partial = dot(normed_k, w_in)

        x_part = scatter_seq(partial[:, DI : 2 * DI], 1)
        bcdt = sum_seq(partial[:, 2 * DI : PROJ])
        z_part = scatter_seq(partial[:, :DI], 1)
        gate_in = z_part.astype(bf16).astype(f32)
        x_pre = x_part.astype(bf16)
        bc_pre = bcdt[:, : 2 * N].astype(bf16)
        dt_raw = own_seq(bcdt[:, 2 * N :], 1).astype(bf16).astype(f32)
        inner = DI // seq
        hsize = DI // H
        dt_in = dt_raw + own_seq(dt_bias, 0)[None, :]
        step_size = jax.nn.softplus(dt_in)
        alog = own_seq(a_log, 0)[None, :]
        ssd_args = (
            x_pre,
            bc_pre,
            own_seq(conv_w[:, :DI], 1),
            own_seq(conv_b[:DI], 0)[None, :],
            conv_w[:, DI:],
            conv_b[None, DI:],
            step_size,
            step_size.T,
            alog,
            alog.T,
            jnp.repeat(own_seq(skip_gain, 0), hsize)[None, :],
        )
        ssd_out = ssd_forward(hsize, ssd_args)

        d_gated = None
        for b in range(4):
            piece = dot(cot, w_out[b], ((1,), (1,))).astype(bf16)
            piece = dot(piece, pick_out[b], ((1,), (1,)))
            d_gated = piece if d_gated is None else d_gated + piece
        d_gated = scatter_seq(d_gated, 1)

        gain = own_seq(gate_g, 0)[None, :]
        sig = jax.nn.sigmoid(gate_in)
        swish = gate_in * sig
        gated = ssd_out * swish
        weighted = d_gated * gain
        sums = jnp.stack([jnp.sum(gated * gated, axis=1), jnp.sum(weighted * gated, axis=1)])
        sums = sum_seq_wide(sums)
        g_scale = lax.rsqrt(sums[0] / DI + norm_eps)[:, None]
        cross = (sums[1] / DI)[:, None]
        gated_norm = (gated * g_scale * gain).astype(bf16)
        d_gate_g = jnp.sum(d_gated * gated * g_scale, axis=0)
        d_pre = g_scale * weighted - gated * g_scale**3 * cross
        d_ssd = d_pre * swish
        d_gate_in = d_pre * ssd_out * (sig + swish * (1.0 - sig))

        gn_full = gather_seq(gated_norm, 1)
        gn_k = [dot(gn_full, pick_out[b]).astype(bf16) for b in range(4)]
        y_part = None
        for b in range(4):
            piece = dot(gn_k[b], w_out[b])
            y_part = piece if y_part is None else y_part + piece
        y_own = scatter_seq(y_part, 0) + x_own.astype(f32)

        d_x, d_bcpre, d_dtraw, d_wx, d_bx, d_wb, d_bb, d_head, d_skip = ssd_backward(
            hsize, ssd_args + (jax.nn.sigmoid(dt_in), d_ssd)
        )
        d_alog, d_dtbias = d_head[0], d_head[1]
        d_skip = jnp.sum(d_skip.reshape(-1, hsize), axis=1)
        d_z_full = gather_seq(d_gate_in.astype(bf16), 1)
        d_x_full = gather_seq(d_x, 1)
        d_bc = sum_seq(d_bcpre).astype(bf16)
        d_dt_full = gather_seq(d_dtraw.astype(bf16), 1)
        pad = jnp.zeros((d_bc.shape[0], WIDE - PROJ), bf16)
        d_mixed = jnp.concatenate([d_z_full, d_x_full, d_bc, d_dt_full, pad], axis=1)

        g_in = dot(normed_k, d_mixed, ((0,), (0,))).astype(bf16).reshape(n_in, rows, WIDE)
        g_out = jnp.concatenate(
            [dot(gn_k[b], cot, ((0,), (0,))).astype(bf16).reshape(n_out, rows, D) for b in range(4)]
            + [jnp.zeros((n_out, rows, WIDE - 4 * D), bf16)],
            axis=2,
        )
        both = n_in + n_out - dp
        parts = jnp.concatenate(
            [g_in[: n_in - both], g_in[n_in - both :] + g_out[:both], g_out[both:]], axis=0
        )

        dn_k = dot(d_mixed, w_in, ((1,), (1,))).astype(bf16)
        d_normed = scatter_seq(dot(dn_k, pick_in, ((1,), (1,))), 0)
        wide_own = x_own.astype(f32)
        scale_own = lax.rsqrt(jnp.mean(wide_own * wide_own, axis=-1, keepdims=True) + norm_eps)
        a_own = d_normed * norm_g[None, :]
        d_norm_g = jnp.sum(d_normed * wide_own * scale_own, axis=0)
        d_wide = scale_own * a_own - wide_own * scale_own**3 * jnp.mean(
            a_own * wide_own, axis=-1, keepdims=True
        )
        input_grad = (cot_own.astype(f32) + d_wide).astype(bf16)

        def spread(a, width):
            full = jnp.zeros(a.shape[:-1] + (width,), f32)
            start = (0,) * (a.ndim - 1) + (s * a.shape[-1],)
            return lax.dynamic_update_slice(full, a, start)

        small_grad = jnp.concatenate(
            [
                jnp.concatenate([spread(d_wx, DI), d_wb], axis=1).reshape(-1),
                spread(d_bx[0], DI),
                d_bb[0],
                d_norm_g,
                spread(d_gate_g, DI),
                spread(d_alog, H),
                spread(d_dtbias, H),
                spread(d_skip, H),
            ]
        )
        small_grad = jnp.pad(small_grad, (0, -SMALL % D)).reshape(-1, D)
        small_grad = sum_all(small_grad).reshape(-1)[:SMALL]

        grad_chunk = scatter_dp(parts)
        shard = plan.unpack(grad_chunk, k)
        wing = jnp.pad(small_grad, (size, size))
        shard = shard + lax.dynamic_slice(
            wing, (jnp.clip(size - at, 0, size + SMALL),), (size,)
        )
        updated, first_new, second_new = adamw(params, shard, moment_one, moment_two)
        return (y_own.astype(bf16)[None], input_grad[None], shard, updated, first_new, second_new)

    return on_device


def matmul_cost(flops, size):
    return pl.CostEstimate(flops=flops, transcendentals=0, bytes_accessed=size)


def call(kernel, name, shapes, args, micros, **scratch):
    return pl.pallas_call(
        kernel,
        out_shape=[jax.ShapeDtypeStruct(a, b) for a, b in shapes],
        in_specs=vmem_specs(len(args)),
        out_specs=vmem_specs(len(shapes)),
        cost_estimate=matmul_cost(int(micros * 5e8), int(micros * 2e6)),
        name=name,
        **scratch,
    )(*args)


def front_kernel(depth, nk_ref, w_ref, own_ref, other_ref, rest_ref=None):
    half = own_ref.shape[1]
    nk = nk_ref[...]
    own_ref[...] = dot(nk, w_ref[:depth, :half])
    other_ref[...] = dot(nk, w_ref[:depth, half : 2 * half]).astype(bf16)
    if rest_ref is not None:
        rest_ref[...] = dot(nk, w_ref[:depth, 2 * half :]).astype(bf16)


def gate_grad_kernel(base, cot_ref, wb_ref, wa_ref, pick_ref, own_ref, other_ref):
    half = own_ref.shape[1]
    total = None
    for b in range(4):
        ref = wb_ref if b < 2 else wa_ref
        c = b % 2
        piece = dot(cot_ref[...], ref[base:, c * D : (c + 1) * D], ((1,), (1,))).astype(bf16)
        piece = dot(piece, pick_ref[b], ((1,), (1,)))
        total = piece if total is None else total + piece
    own_ref[...] = total[:, :half]
    other_ref[...] = total[:, half:].astype(bf16)


def out_kernel(base, own_ref, other_ref, wb_ref, wa_ref, pick_ref, gk_ref, y_ref):
    half = own_ref.shape[1]
    total = None
    for b in range(4):
        ref = wb_ref if b < 2 else wa_ref
        c = b % 2
        gk = dot(own_ref[...], pick_ref[b, :half]) + dot(other_ref[...], pick_ref[b, half:])
        gk = gk.astype(bf16)
        gk_ref[b] = gk
        piece = dot(gk, ref[base:, c * D : (c + 1) * D])
        total = piece if total is None else total + piece
    y_ref[...] = total


def weight_grad_kernel(depth, base, first, nk_ref, d_ref, gk_ref, cot_ref, out_ref):
    cols = out_ref.shape[1]
    nk = nk_ref[...]
    for n in range(0, cols, D):
        stop = min(n + D, cols)
        top = dot(nk, d_ref[:, n:stop], ((0,), (0,)))
        out_ref[:base, n:stop] = top[:base].astype(bf16)
        if n + D <= 2 * D:
            low = dot(gk_ref[first + n // D], cot_ref[...], ((0,), (0,)))
            out_ref[base:depth, n:stop] = (top[base:] + low[: depth - base]).astype(bf16)
            out_ref[depth:, n:stop] = low[depth - base :].astype(bf16)
        else:
            out_ref[base:depth, n:stop] = top[base:].astype(bf16)
            out_ref[depth:, n:stop] = jnp.zeros((out_ref.shape[0] - depth, stop - n), bf16)


def input_grad_kernel(depth, db_ref, da_ref, wb_ref, wa_ref, pick_ref, out_ref):
    dn = dot(db_ref[...], wb_ref[:depth], ((1,), (1,))) + dot(da_ref[...], wa_ref[:depth], ((1,), (1,)))
    out_ref[...] = dot(dn.astype(bf16), pick_ref[...], ((1,), (1,)))


def small_fits(dp, plan):
    return plan.rows * (WIDE - 4 * D) >= SMALL and (dp - 1) * plan.seq > plan.mix


def make_pair(dp, flat):
    seq = 2
    plan = Plan(dp, seq, flat)
    rows = plan.rows
    za, yb, cc = factors(dp)
    inner = DI // seq
    hsize = DI // H
    side = WIDE - 4 * D
    n_in, n_out = plan.j_in, dp - plan.j_out
    depth, base = n_in * rows, plan.j_out * rows

    def place(z, y, c):
        return ((z % za) * yb + (y % yb)) * cc + (c % cc)

    def perm(dz, dy, dc):
        return [
            (place(z, y, c), place(z + dz, y + dy, c + dc))
            for z in range(za)
            for y in range(yb)
            for c in range(cc)
        ]

    z_next, y_next, c_next = perm(1, 0, 0), perm(0, 1, 0), perm(0, 0, 1)

    def position():
        j = lax.axis_index("dp")
        return j // (yb * cc), (j // cc) % yb, j % cc

    def index(z, y, c):
        return (((z + za) % za) * yb + (y + yb) % yb) * cc + c % cc

    def gather_dp(chunk):
        z, y, c = position()
        slots = []
        cur = chunk
        for r in range(za):
            if r:
                cur = lax.ppermute(cur, "dp", z_next)
            beside = cur
            for t in range(yb):
                if t:
                    beside = lax.ppermute(beside, "dp", y_next)
                if cc == 2:
                    slots.append((index(z - r, y - t, c + 1), lax.ppermute(beside, "dp", c_next)))
                slots.append((index(z - r, y - t, c), beside))
        whole = jnp.zeros((dp,) + chunk.shape, chunk.dtype)
        for at, data in slots:
            whole = lax.dynamic_update_index_in_dim(whole, data, at, 0)
        return whole.reshape(dp * rows, chunk.shape[1]), cur

    def scatter_dp(parts):
        parts = parts.reshape(dp, rows, -1)
        z, y, c = position()

        def pick(zi, yi, ci):
            return lax.dynamic_index_in_dim(parts, index(zi, yi, ci), 0, False)

        def add(a, b):
            return (a.astype(f32) + b.astype(f32)).astype(bf16)

        def core_sum(zi, yi):
            own = pick(zi, yi, c)
            if cc == 2:
                own = add(own, lax.ppermute(pick(zi, yi, c + 1), "dp", c_next))
            return own

        def mid_sum(zi):
            acc = core_sum(zi, y - 1)
            for r in range(2, yb + 1):
                acc = add(lax.ppermute(acc, "dp", y_next), core_sum(zi, y - r))
            return acc

        acc = mid_sum(z - 1)
        for r in range(2, za + 1):
            acc = add(lax.ppermute(acc, "dp", z_next), mid_sum(z - r))
        return acc

    def swap(a):
        return lax.ppermute(a, "seq", [(0, 1), (1, 0)])

    def sum_all(a):
        for axis, count in (("seq", seq), ("dp", dp)):
            step = 1
            while step < count:
                a = a + lax.ppermute(a, axis, [(i, i ^ step) for i in range(count)])
                step *= 2
        return a

    def own_seq(a, axis):
        n = a.shape[axis] // seq
        return lax.dynamic_slice_in_dim(a, lax.axis_index("seq") * n, n, axis)

    def on_device(x_in, cotangent, params, moment_one, moment_two):
        s = lax.axis_index("seq")
        first = s == 0
        k = lax.axis_index("dp") * seq + s
        halfs = params.astype(bf16)

        def ordered(a, other):
            return jnp.concatenate([jnp.where(first, a, other), jnp.where(first, other, a)], axis=0)

        def flip(a, cut):
            return jnp.where(first, a, jnp.concatenate([a[:, cut:], a[:, :cut]], axis=1))

        at = IN + OUT - k * flat
        padded = jnp.pad(halfs, (SMALL, SMALL))
        tail = lax.dynamic_slice(padded, (jnp.clip(at + SMALL, 0, flat + SMALL),), (SMALL,))
        tail = jnp.pad(tail, (0, rows * side - SMALL)).reshape(rows, side)
        tail = tail + swap(tail)

        chunk = plan.pack(halfs, k)
        input_rows = k <= plan.mix
        part_b = jnp.where(input_rows, flip(chunk[:, :DI], inner), chunk[:, :DI])
        mid = chunk[:, DI : 2 * DI]
        part_a = jnp.concatenate(
            [
                jnp.where(input_rows, flip(mid, inner), mid),
                jnp.where(input_rows, chunk[:, 4 * D :], tail),
            ],
            axis=1,
        )
        if plan.mix_out:
            keep = (k == plan.mix) & (jnp.arange(rows) >= plan.mix_in)[:, None]
            part_b = jnp.where(keep, chunk[:, :DI], part_b)
            part_a = jnp.where(keep, chunk[:, DI:], part_a)
        w_a, last = gather_dp(part_a)
        part_b, last = lax.optimization_barrier((part_b, last))
        w_b, _ = gather_dp(part_b)

        x_own = x_in[0]
        cot_own = cotangent[0]
        tokens = ordered(x_own, swap(x_own))
        cot = ordered(cot_own, swap(cot_own))
        count = tokens.shape[0]

        in_map = lax.dynamic_index_in_dim(jnp.asarray(plan.in_map.reshape(seq, -1)), s, 0, False)
        turned = plan.out_map.copy()
        turned[1] = np.where(turned[1] >= 0, (turned[1] + inner) % DI, -1)
        out_map = lax.dynamic_index_in_dim(
            jnp.asarray(turned.transpose(0, 2, 1, 3).reshape(seq, 4, -1)), s, 0, False
        )
        pick_in = (jnp.arange(D)[:, None] == in_map[None, :]).astype(bf16)
        pick_out = (jnp.arange(DI)[None, :, None] == out_map[:, None, :]).astype(bf16)

        small = w_a[(dp - 1) * rows :, 2 * D :].reshape(-1)
        pieces = []
        offset = 0
        for length in (K * CONV, CONV, D, DI, H, H, H):
            pieces.append(small[offset : offset + length].astype(f32))
            offset += length
        conv_w, conv_b, norm_g, gate_g, a_log, dt_bias, skip_gain = pieces
        conv_w = conv_w.reshape(K, CONV)

        wide = tokens.astype(f32)
        scale = lax.rsqrt(jnp.mean(wide * wide, axis=-1, keepdims=True) + norm_eps)
        normed = (wide * scale * norm_g[None, :]).astype(bf16)
        normed_k = dot(normed, pick_in).astype(bf16)

        x_own_part, x_other, bcdt = call(
            functools.partial(front_kernel, depth),
            "front_a",
            [((count, inner), f32), ((count, inner), bf16), ((count, side), bf16)],
            (normed_k, w_a),
            4.0,
        )
        bcdt = bcdt.astype(f32) + swap(bcdt).astype(f32)
        x_pre = (x_own_part + swap(x_other).astype(f32)).astype(bf16)
        bc_pre = bcdt[:, : 2 * N].astype(bf16)
        dt_raw = own_seq(bcdt[:, 2 * N : 2 * N + H], 1).astype(bf16).astype(f32)
        dt_in = dt_raw + own_seq(dt_bias, 0)[None, :]
        step_size = jax.nn.softplus(dt_in)
        alog = own_seq(a_log, 0)[None, :]
        ssd_args = (
            x_pre,
            bc_pre,
            own_seq(conv_w[:, :DI], 1),
            own_seq(conv_b[:DI], 0)[None, :],
            conv_w[:, DI:],
            conv_b[None, DI:],
            step_size,
            step_size.T,
            alog,
            alog.T,
            jnp.repeat(own_seq(skip_gain, 0), hsize)[None, :],
        )
        ssd_out = ssd_forward(hsize, ssd_args)

        z_own_part, z_other = call(
            functools.partial(front_kernel, depth),
            "front_b",
            [((count, inner), f32), ((count, inner), bf16)],
            (normed_k, w_b),
            3.0,
        )
        gate_in = (z_own_part + swap(z_other).astype(f32)).astype(bf16).astype(f32)
        dg_own, dg_other = call(
            functools.partial(gate_grad_kernel, base),
            "gate_grad",
            [((count, inner), f32), ((count, inner), bf16)],
            (cot, w_b, w_a, pick_out),
            6.0,
        )
        d_gated = dg_own + swap(dg_other).astype(f32)

        gain = own_seq(gate_g, 0)[None, :]
        sig = jax.nn.sigmoid(gate_in)
        swish = gate_in * sig
        gated = ssd_out * swish
        weighted = d_gated * gain
        sums = jnp.stack([jnp.sum(gated * gated, axis=1), jnp.sum(weighted * gated, axis=1)])
        sums = sums + swap(sums)
        g_scale = lax.rsqrt(sums[0] / DI + norm_eps)[:, None]
        cross = (sums[1] / DI)[:, None]
        gn_own = (gated * g_scale * gain).astype(bf16)
        d_gate_g = jnp.sum(d_gated * gated * g_scale, axis=0)
        d_pre = g_scale * weighted - gated * g_scale**3 * cross
        d_ssd = d_pre * swish
        dz_own = (d_pre * ssd_out * (sig + swish * (1.0 - sig))).astype(bf16)
        gn_own, dz_own, d_ssd = lax.optimization_barrier((gn_own, dz_own, d_ssd))
        gn_other = swap(gn_own)
        dz_other = swap(dz_own)

        d_x, d_bcpre, d_dtraw, d_wx, d_bx, d_wb, d_bb, d_head, d_skip = ssd_backward(
            hsize, ssd_args + (jax.nn.sigmoid(dt_in), d_ssd)
        )
        d_alog, d_dtbias = d_head[0], d_head[1]
        d_skip = jnp.sum(d_skip.reshape(-1, hsize), axis=1)

        gn_k, y_part = call(
            functools.partial(out_kernel, base),
            "out_front",
            [((4, count, n_out * rows), bf16), ((count, D), f32)],
            (gn_own, gn_other, w_b, w_a, pick_out),
            6.0,
        )
        d_b = jnp.concatenate([dz_own, dz_other], axis=1)
        parts_b = call(
            functools.partial(weight_grad_kernel, depth, base, 0),
            "grad_b",
            [((dp * rows, DI), bf16)],
            (normed_k, d_b, gn_k, cot),
            5.0,
        )[0]
        grad_b = scatter_dp(parts_b)

        bcdt_own = jnp.concatenate([d_bcpre, d_dtraw], axis=1).astype(bf16)
        dx_other, bcdt_other = swap(d_x), swap(bcdt_own)
        d_bc = (bcdt_own[:, : 2 * N].astype(f32) + bcdt_other[:, : 2 * N].astype(f32)).astype(bf16)
        dt_pair = jnp.where(
            first,
            jnp.concatenate([bcdt_own[:, 2 * N :], bcdt_other[:, 2 * N :]], axis=1),
            jnp.concatenate([bcdt_other[:, 2 * N :], bcdt_own[:, 2 * N :]], axis=1),
        )
        blank = jnp.zeros((count, WIDE - PROJ), bf16)
        d_a = jnp.concatenate([d_x, dx_other, d_bc, dt_pair, blank], axis=1)
        parts_a = call(
            functools.partial(weight_grad_kernel, depth, base, 2),
            "grad_a",
            [((dp * rows, 2 * D + side), bf16)],
            (normed_k, d_a, gn_k, cot),
            5.0,
        )[0]
        grad_a = scatter_dp(parts_a)

        d_normed = call(
            functools.partial(input_grad_kernel, depth),
            "grad_x",
            [((count, D), f32)],
            (d_b, d_a, w_b, w_a, pick_in),
            5.0,
        )[0]

        def own_tokens(a):
            half = count // 2
            low, high = a[:half], a[half:]
            got = swap(jnp.where(first, high, low).astype(bf16))
            return jnp.where(first, low, high) + got.astype(f32)

        d_norm_g = jnp.sum(d_normed * wide * scale, axis=0)
        d_own = own_tokens(d_normed)
        y_own = own_tokens(y_part) + x_own.astype(f32)
        wide_own = x_own.astype(f32)
        scale_own = lax.rsqrt(jnp.mean(wide_own * wide_own, axis=-1, keepdims=True) + norm_eps)
        a_own = d_own * norm_g[None, :]
        d_wide = scale_own * a_own - wide_own * scale_own**3 * jnp.mean(
            a_own * wide_own, axis=-1, keepdims=True
        )
        input_grad = (cot_own.astype(f32) + d_wide).astype(bf16)

        def spread(a, width):
            full = jnp.zeros(a.shape[:-1] + (width,), f32)
            start = (0,) * (a.ndim - 1) + (s * a.shape[-1],)
            return lax.dynamic_update_slice(full, a, start)

        small_grad = jnp.concatenate(
            [
                jnp.concatenate([spread(d_wx, DI), d_wb], axis=1).reshape(-1),
                spread(d_bx[0], DI),
                d_bb[0],
                d_norm_g,
                spread(d_gate_g, DI),
                spread(d_alog, H),
                spread(d_dtbias, H),
                spread(d_skip, H),
            ]
        )
        small_grad = jnp.pad(small_grad, (0, -SMALL % D)).reshape(-1, D)
        small_grad = sum_all(small_grad).reshape(-1)[:SMALL]

        def unflip(a, cut):
            keep = k > plan.mix
            if plan.mix_out:
                keep = keep | ((k == plan.mix) & (jnp.arange(rows) >= plan.mix_in)[:, None])
            return jnp.where(keep, a, flip(a, cut))

        grad_a, grad_b = grad_a.astype(f32), grad_b.astype(f32)
        grad_chunk = jnp.concatenate(
            [unflip(grad_b, inner), unflip(grad_a[:, : 2 * D], inner), grad_a[:, 2 * D :]], axis=1
        )
        shard = plan.unpack(grad_chunk, k)
        wing = jnp.pad(small_grad, (flat, flat))
        shard = shard + lax.dynamic_slice(wing, (jnp.clip(flat - at, 0, flat + SMALL),), (flat,))
        updated, first_new, second_new = adamw(params, shard, moment_one, moment_two)
        return (y_own.astype(bf16)[None], input_grad[None], shard, updated, first_new, second_new)

    return on_device


def make(dp, seq):
    def on_device(x_in, cotangent, params, moment_one, moment_two):
        flat = params.shape[0]
        if seq == 2 and small_fits(dp, Plan(dp, seq, flat)):
            step = make_pair(dp, flat)
        else:
            step = make_general(dp, seq)
        return step(x_in, cotangent, params, moment_one, moment_two)

    return on_device


def solution(mesh):
    return jax.shard_map(
        make(mesh.shape["dp"], mesh.shape["seq"]),
        mesh=mesh,
        in_specs=(
            P("dp", "seq", None),
            P("dp", "seq", None),
            P(("dp", "seq")),
            P(("dp", "seq")),
            P(("dp", "seq")),
        ),
        out_specs=(
            P("dp", "seq", None),
            P("dp", "seq", None),
            P(("dp", "seq")),
            P(("dp", "seq")),
            P(("dp", "seq")),
            P(("dp", "seq")),
        ),
        check_vma=False,
    )
```

```python
import functools
import jax
import jax.numpy as jnp
import numpy as np
from jax import lax
from jax.experimental import pallas as pl
from jax.experimental.pallas import tpu as pltpu
from jax.sharding import PartitionSpec as P

D = 1024
DI = 2048
N = 128
K = 4
SPAN = 128
H = 32
CONV = 2304
PROJ = 4384
WIDE = 4480
IN = D * PROJ
OUT = DI * D
SMALL = K * CONV + CONV + D + DI + 3 * H

norm_eps = 1e-05
learn_rate = 0.005
beta_one = 0.9
beta_two = 0.95
adam_eps = 1e-08
weight_decay = 0.1
adam_step = 10

bf16 = jnp.bfloat16
f32 = jnp.float32


def ceil_to(value, unit):
    return -(-value // unit) * unit


def factors(count):
    core = 2 if count % 2 == 0 else 1
    rest = count // core
    mid = 1
    while rest % (mid * 2) == 0 and (mid * 2) ** 2 <= rest * 1:
        mid *= 2
    return rest // mid, mid, core


def dot(a, b, dims=((1,), (0,))):
    return lax.dot_general(a, b, (dims, ((), ())), preferred_element_type=f32)


def col_roll(a, steps):
    rows = a.shape[0]
    at = lax.broadcasted_iota(jnp.int32, a.shape, 0)
    if steps >= 0:
        return jnp.where(at >= steps, pltpu.roll(a, steps, 0), 0.0)
    return jnp.where(at < rows + steps, pltpu.roll(a, rows + steps, 0), 0.0)


def conv_act(x, taps, bias):
    acc = bias + taps[K - 1 : K] * x
    for k in range(1, K):
        acc = acc + taps[K - 1 - k : K - k] * col_roll(x, k)
    sig = 1.0 / (1.0 + jnp.exp(-acc))
    return acc, sig


def conv_back(x, taps, d_acc):
    d_x = taps[K - 1 : K] * d_acc
    d_taps = [jnp.sum(d_acc * x, axis=0, keepdims=True)]
    for k in range(1, K):
        d_x = d_x + taps[K - 1 - k : K - k] * col_roll(d_acc, -k)
        d_taps.insert(0, jnp.sum(d_acc * col_roll(x, k), axis=0, keepdims=True))
    return d_x, d_taps, jnp.sum(d_acc, axis=0, keepdims=True)


def fine(a, b, dims):
    return lax.dot_general(
        a, b, (dims, ((), ())), precision=lax.Precision.HIGHEST, preferred_element_type=f32
    )


def tri_parts():
    row = lax.broadcasted_iota(jnp.int32, (SPAN, SPAN), 0)
    col = lax.broadcasted_iota(jnp.int32, (SPAN, SPAN), 1)
    return row >= col, row == col


def rates(c, step_ref, turn_ref, alog_ref, alog_turn_ref, lower):
    span = slice(c * SPAN, (c + 1) * SPAN)
    rate = step_ref[span, :] * -jnp.exp(alog_ref[...])
    rate_turn = turn_ref[:, span] * -jnp.exp(alog_turn_ref[...])
    within = fine(lower, rate, ((1,), (0,)))
    within_turn = fine(rate_turn, lower, ((1,), (1,)))
    return rate, within, within_turn


def lanes_of(pair, first, second):
    lane = lax.broadcasted_iota(jnp.int32, (1, 2 * pair), 1)
    return jnp.where(lane < pair, first, second)


def ssd_forward_kernel(
    hsize, x_ref, bc_ref, wx_ref, bx_ref, wb_ref, bb_ref, step_ref, turn_ref, alog_ref, alog_turn_ref, skip_ref, out_ref
):
    rows, inner = x_ref.shape
    blocks = rows // SPAN
    causal, _ = tri_parts()
    lower = causal.astype(f32)
    acc, sig = conv_act(bc_ref[...].astype(f32), wb_ref[...], bb_ref[...])
    bc = (acc * sig).astype(bf16)
    b_blk = [bc[c * SPAN : (c + 1) * SPAN, :N] for c in range(blocks)]
    c_blk = [bc[c * SPAN : (c + 1) * SPAN, N:] for c in range(blocks)]
    cross = [dot(c_blk[c], b_blk[c], ((1,), (1,))) for c in range(blocks)]
    rated = [rates(c, step_ref, turn_ref, alog_ref, alog_turn_ref, lower) for c in range(blocks)]
    width = 2 * hsize
    lane = lax.broadcasted_iota(jnp.int32, (1, width), 1)
    masks = [(lane < hsize).astype(f32), (lane >= hsize).astype(f32)]
    for g in range(inner // width):
        cols = slice(g * width, (g + 1) * width)
        acc, sig = conv_act(x_ref[:, cols].astype(f32), wx_ref[:, cols], bx_ref[:, cols])
        vals = acc * sig
        state = None
        for c in range(blocks):
            span = slice(c * SPAN, (c + 1) * SPAN)
            _, within, within_turn = rated[c]
            v = vals[span]
            mix, split = [], []
            for i in range(2):
                h = 2 * g + i
                gap = within[:, h : h + 1] - within_turn[h : h + 1, :]
                mix.append(
                    (jnp.exp(jnp.where(causal, gap, -10000.0)) * cross[c] * turn_ref[h : h + 1, span]).astype(bf16)
                )
                split.append((v * masks[i]).astype(bf16))
            out = dot(jnp.concatenate(mix, axis=1), jnp.concatenate(split, axis=0))
            w0, w1 = within[:, 2 * g : 2 * g + 1], within[:, 2 * g + 1 : 2 * g + 2]
            if state is not None:
                out = out + lanes_of(hsize, jnp.exp(w0), jnp.exp(w1)) * dot(c_blk[c], state.astype(bf16))
            out_ref[span, cols] = out + skip_ref[:, cols] * v
            if c < blocks - 1:
                e0, e1 = w0[SPAN - 1 :], w1[SPAN - 1 :]
                tail = lanes_of(
                    hsize,
                    jnp.exp(e0 - w0) * step_ref[span, 2 * g : 2 * g + 1],
                    jnp.exp(e1 - w1) * step_ref[span, 2 * g + 1 : 2 * g + 2],
                )
                fresh = dot(b_blk[c], (tail * v).astype(bf16), ((0,), (0,)))
                if state is not None:
                    fresh = fresh + lanes_of(hsize, jnp.exp(e0), jnp.exp(e1)) * state
                state = fresh


def ssd_backward_kernel(
    hsize, x_ref, bc_ref, wx_ref, bx_ref, wb_ref, bb_ref, step_ref, turn_ref, alog_ref, alog_turn_ref, skip_ref,
    slope_ref, dy_ref, dx_ref, dbc_ref, ddt_ref, dwx_ref, dbx_ref, dwb_ref, dbb_ref, dhead_ref, dskip_ref,
    dcross_ref, dbmat_ref, dcmat_ref, col_ref, scol_ref, row_ref, srow_ref,
):
    rows, inner = x_ref.shape
    heads = step_ref.shape[1]
    blocks = rows // SPAN
    causal, eye = tri_parts()
    lower = causal.astype(f32)
    eye = eye.astype(f32)
    bc_in = bc_ref[...].astype(f32)
    bc_acc, bc_sig = conv_act(bc_in, wb_ref[...], bb_ref[...])
    bc = (bc_acc * bc_sig).astype(bf16)
    b_blk = [bc[c * SPAN : (c + 1) * SPAN, :N] for c in range(blocks)]
    c_blk = [bc[c * SPAN : (c + 1) * SPAN, N:] for c in range(blocks)]
    cross = [dot(c_blk[c], b_blk[c], ((1,), (1,))) for c in range(blocks)]
    rated = [rates(c, step_ref, turn_ref, alog_ref, alog_turn_ref, lower) for c in range(blocks)]
    for ref in (dcross_ref, dbmat_ref, dcmat_ref, col_ref, scol_ref, row_ref, srow_ref):
        ref[...] = jnp.zeros_like(ref)
    width = 2 * hsize
    lane = lax.broadcasted_iota(jnp.int32, (1, width), 1)
    masks = [(lane < hsize).astype(f32), (lane >= hsize).astype(f32)]
    head_lane = lax.broadcasted_iota(jnp.int32, (1, heads), 1)
    head_row = lax.broadcasted_iota(jnp.int32, (heads, 1), 0)
    last_row = lax.broadcasted_iota(jnp.int32, (SPAN, 1), 0) == SPAN - 1
    for g in range(inner // width):
        cols = slice(g * width, (g + 1) * width)
        x = x_ref[:, cols].astype(f32)
        acc, sig = conv_act(x, wx_ref[:, cols], bx_ref[:, cols])
        vals = acc * sig
        states, tails, decays = [None], [], []
        for c in range(blocks):
            span = slice(c * SPAN, (c + 1) * SPAN)
            within = rated[c][1]
            w0, w1 = within[:, 2 * g : 2 * g + 1], within[:, 2 * g + 1 : 2 * g + 2]
            e0, e1 = w0[SPAN - 1 :], w1[SPAN - 1 :]
            if c < blocks - 1:
                tails.append(
                    lanes_of(
                        hsize,
                        jnp.exp(e0 - w0) * step_ref[span, 2 * g : 2 * g + 1],
                        jnp.exp(e1 - w1) * step_ref[span, 2 * g + 1 : 2 * g + 2],
                    )
                )
                decays.append(lanes_of(hsize, jnp.exp(e0), jnp.exp(e1)))
                fresh = dot(b_blk[c], (tails[c] * vals[span]).astype(bf16), ((0,), (0,)))
                if states[c] is not None:
                    fresh = fresh + decays[c] * states[c]
                states.append(fresh)
        d_state = None
        d_vals = [None] * blocks
        d_skip = jnp.zeros((1, width), f32)
        for c in reversed(range(blocks)):
            span = slice(c * SPAN, (c + 1) * SPAN)
            _, within, within_turn = rated[c]
            v = vals[span]
            v_low = v.astype(bf16)
            dy = dy_ref[span, cols].astype(f32)
            ws = [within[:, 2 * g + i : 2 * g + i + 1] for i in range(2)]
            mix, split, d_w = [], [], []
            d_cross = None
            for i in range(2):
                h = 2 * g + i
                turn = turn_ref[h : h + 1, span]
                decay = jnp.exp(jnp.where(causal, ws[i] - within_turn[h : h + 1, :], -10000.0))
                scored = decay * cross[c]
                mix.append((scored * turn).astype(bf16))
                d_half = (dy * masks[i]).astype(bf16)
                split.append(d_half)
                d_mix = dot(d_half, v_low, ((1,), (1,)))
                raw = d_mix * scored
                part = d_mix * decay * turn
                d_cross = part if d_cross is None else d_cross + part
                d_w.append(jnp.sum(raw * turn, axis=1, keepdims=True))
                raw_sum = jnp.sum(raw, axis=0, keepdims=True)
                row_ref[c] += jnp.where(head_row == h, -raw_sum * turn, 0.0)
                srow_ref[c] += jnp.where(head_row == h, raw_sum, 0.0)
            dcross_ref[c] += d_cross
            d_v = dot(jnp.concatenate(mix, axis=0), jnp.concatenate(split, axis=0), ((0,), (0,)))
            d_v = d_v + skip_ref[:, cols] * dy
            d_skip = d_skip + jnp.sum(dy * v, axis=0, keepdims=True)
            d_enter = None
            if states[c] is not None:
                st = states[c].astype(bf16)
                lifted = lanes_of(hsize, jnp.exp(ws[0]), jnp.exp(ws[1])) * dy
                lift_low = lifted.astype(bf16)
                dcmat_ref[span] += dot(lift_low, st, ((1,), (1,)))
                d_enter = dot(c_blk[c], lift_low, ((0,), (0,)))
                prod = lifted * dot(c_blk[c], st)
                for i in range(2):
                    d_w[i] = d_w[i] + jnp.sum(prod * masks[i], axis=1, keepdims=True)
            if d_state is not None:
                ds_low = d_state.astype(bf16)
                back = dot(b_blk[c], ds_low)
                d_v = d_v + tails[c] * back
                dbmat_ref[span] += dot((tails[c] * v).astype(bf16), ds_low, ((1,), (1,)))
                along = v * back
                if states[c] is not None:
                    held = decays[c] * d_state * states[c]
                for i in range(2):
                    h = 2 * g + i
                    d_tail = jnp.sum(along * masks[i], axis=1, keepdims=True)
                    reach = jnp.exp(ws[i][SPAN - 1 :] - ws[i])
                    scol_ref[c] += jnp.where(head_lane == h, d_tail * reach, 0.0)
                    fall = d_tail * reach * step_ref[span, h : h + 1]
                    d_end = jnp.sum(fall, axis=0, keepdims=True)
                    if states[c] is not None:
                        d_end = d_end + jnp.sum(
                            jnp.sum(held * masks[i], axis=1, keepdims=True), axis=0, keepdims=True
                        )
                    d_w[i] = d_w[i] - fall + jnp.where(last_row, d_end, 0.0)
                if d_enter is not None:
                    d_enter = d_enter + decays[c] * d_state
            for i in range(2):
                col_ref[c] += jnp.where(head_lane == 2 * g + i, d_w[i], 0.0)
            d_state = d_enter
            d_vals[c] = d_v
        d_acc = jnp.concatenate(d_vals, axis=0) * (sig + vals * (1.0 - sig))
        d_x, d_taps, d_bias = conv_back(x, wx_ref[:, cols], d_acc)
        dx_ref[:, cols] = d_x.astype(bf16)
        for k in range(K):
            dwx_ref[k : k + 1, cols] = d_taps[k]
        dbx_ref[:, cols] = d_bias
        dskip_ref[:, cols] = d_skip
    d_alog = jnp.zeros((1, heads), f32)
    d_dtb = jnp.zeros((1, heads), f32)
    for c in range(blocks):
        span = slice(c * SPAN, (c + 1) * SPAN)
        d_w = col_ref[c] + fine(eye, row_ref[c], ((1,), (1,)))
        d_step = scol_ref[c] + fine(eye, srow_ref[c], ((1,), (1,)))
        d_rate = fine(lower, d_w, ((0,), (0,)))
        d_alog = d_alog + jnp.sum(rated[c][0] * d_rate, axis=0, keepdims=True)
        d_dt = (d_step - jnp.exp(alog_ref[...]) * d_rate) * slope_ref[span, :]
        ddt_ref[span, :] = d_dt
        d_dtb = d_dtb + jnp.sum(d_dt, axis=0, keepdims=True)
        low = dcross_ref[c].astype(bf16)
        dcmat_ref[span] += dot(low, b_blk[c])
        dbmat_ref[span] += dot(low, c_blk[c], ((0,), (0,)))
    dhead_ref[0:1, :] = d_alog
    dhead_ref[1:2, :] = d_dtb
    d_bc = jnp.concatenate([dbmat_ref[...], dcmat_ref[...]], axis=1)
    d_acc = d_bc * (bc_sig + bc_acc * bc_sig * (1.0 - bc_sig))
    d_x, d_taps, d_bias = conv_back(bc_in, wb_ref[...], d_acc)
    dbc_ref[...] = d_x
    for k in range(K):
        dwb_ref[k : k + 1, :] = d_taps[k]
    dbb_ref[...] = d_bias


def vmem_specs(count):
    return [pl.BlockSpec(memory_space=pltpu.VMEM)] * count


def ssd_forward(hsize, args):
    return pl.pallas_call(
        functools.partial(ssd_forward_kernel, hsize),
        out_shape=jax.ShapeDtypeStruct(args[0].shape, f32),
        in_specs=vmem_specs(len(args)),
        out_specs=vmem_specs(1)[0],
        cost_estimate=pl.CostEstimate(flops=int(2.5e9), transcendentals=0, bytes_accessed=int(1e7)),
        name="ssd_forward",
    )(*args)


def ssd_backward(hsize, args):
    rows, inner = args[0].shape
    heads = args[6].shape[1]
    blocks = rows // SPAN
    shapes = [
        ((rows, inner), bf16),
        ((rows, 2 * N), f32),
        ((rows, heads), f32),
        ((K, inner), f32),
        ((1, inner), f32),
        ((K, 2 * N), f32),
        ((1, 2 * N), f32),
        ((2, heads), f32),
        ((1, inner), f32),
    ]
    return pl.pallas_call(
        functools.partial(ssd_backward_kernel, hsize),
        out_shape=[jax.ShapeDtypeStruct(a, b) for a, b in shapes],
        in_specs=vmem_specs(len(args)),
        out_specs=vmem_specs(len(shapes)),
        scratch_shapes=[
            pltpu.VMEM((blocks, SPAN, SPAN), f32),
            pltpu.VMEM((rows, N), f32),
            pltpu.VMEM((rows, N), f32),
            pltpu.VMEM((blocks, SPAN, heads), f32),
            pltpu.VMEM((blocks, SPAN, heads), f32),
            pltpu.VMEM((blocks, heads, SPAN), f32),
            pltpu.VMEM((blocks, heads, SPAN), f32),
        ],
        cost_estimate=pl.CostEstimate(flops=int(6e9), transcendentals=0, bytes_accessed=int(2.4e7)),
        name="ssd_backward",
    )(*args)


def adamw(param_vec, grad_vec, first, second):
    first_new = beta_one * first + (1.0 - beta_one) * grad_vec
    second_new = beta_two * second + (1.0 - beta_two) * grad_vec * grad_vec
    first_hat = first_new / (1.0 - beta_one**adam_step)
    second_hat = second_new / (1.0 - beta_two**adam_step)
    updated = param_vec - learn_rate * (
        first_hat / (jnp.sqrt(second_hat) + adam_eps) + weight_decay * param_vec
    )
    return (updated, first_new, second_new)


class Plan:
    def __init__(self, dp, seq, flat):
        self.dp, self.seq, self.flat = dp, seq, flat
        self.total = dp * seq
        count = self.total
        self.mix = IN // flat
        last_in = -(-IN // flat)
        rows_in = max(
            -(-(((k * flat) % PROJ) + min(flat, IN - k * flat)) // PROJ) for k in range(last_in)
        )
        rows_out = max(
            -(-(((k * flat - IN) % D) + flat) // D) for k in range(self.mix, count)
        )
        self.rows = ceil_to(max(rows_in, -(-rows_out // 4)), 8)
        self.in_len = IN - self.mix * flat
        self.mix_in = -(-(((self.mix * flat) % PROJ) + self.in_len) // PROJ)
        self.mix_out = -(-(flat - self.in_len) // D)
        self.mix_free = self.rows - self.mix_in
        assert 4 * self.mix_free >= self.mix_out
        rows = self.rows
        self.j_in = self.mix // seq + 1
        self.j_out = self.mix // seq
        n_in, n_out = self.j_in, dp - self.j_out
        self.in_map = np.full((seq, n_in, rows), -1, np.int32)
        self.out_map = np.full((seq, n_out, 4, rows), -1, np.int32)
        m = np.arange(rows)
        for s in range(seq):
            for j in range(n_in):
                k = j * seq + s
                if k > self.mix:
                    continue
                first = (k * flat) // PROJ
                used = min(rows, D - first)
                if k == self.mix:
                    used = self.mix_in
                self.in_map[s, j, :used] = first + m[:used]
            for j in range(n_out):
                k = (j + self.j_out) * seq + s
                if k < self.mix:
                    continue
                for b in range(4):
                    if k == self.mix:
                        q = b * self.mix_free + (m - self.mix_in)
                        ok = (m >= self.mix_in) & (q < self.mix_out)
                    else:
                        q = (k * flat - IN) // D + b * rows + m
                        ok = q < min(DI, -(-((k + 1) * flat - IN) // D))
                    self.out_map[s, j, b] = np.where(ok, q, -1)

    def pack(self, flat, k):
        rows, size = self.rows, self.flat
        shift = (k * size) % PROJ
        span = rows * PROJ
        buf = jnp.pad(flat, (PROJ, span - size))
        win = lax.dynamic_slice(buf, (PROJ - shift,), (span,)).reshape(rows, PROJ)
        win = jnp.pad(win, ((0, 0), (0, WIDE - PROJ)))
        off = (k * size - IN) % D
        span = 4 * rows * D
        buf = jnp.pad(flat, (D, span - size))
        out = lax.dynamic_slice(buf, (D - off,), (span,)).reshape(4, rows, D)
        out = jnp.concatenate([out[b] for b in range(4)] + [jnp.zeros((rows, WIDE - 4 * D), flat.dtype)], axis=1)
        head = flat[self.in_len :]
        free = self.mix_free
        head = jnp.pad(head, (0, 4 * free * D - head.shape[0])).reshape(4, free, D)
        low = jnp.concatenate([head[b] for b in range(4)] + [jnp.zeros((free, WIDE - 4 * D), flat.dtype)], axis=1)
        mixed = jnp.concatenate([win[: self.mix_in], low], axis=0)
        return jnp.where(k < self.mix, win, jnp.where(k > self.mix, out, mixed))

    def unpack(self, chunk, k):
        rows, size = self.rows, self.flat
        shift = (k * size) % PROJ
        line = chunk[:, :PROJ].reshape(-1)
        line = jnp.pad(line, (0, max(0, PROJ + size - rows * PROJ)))
        win = lax.dynamic_slice(line, (shift,), (size,))
        off = (k * size - IN) % D
        line = jnp.concatenate([chunk[:, b * D : (b + 1) * D] for b in range(4)], axis=0).reshape(-1)
        line = jnp.pad(line, (0, max(0, D + size - 4 * rows * D)))
        out = lax.dynamic_slice(line, (off,), (size,))
        low = chunk[self.mix_in :]
        low = jnp.concatenate([low[:, b * D : (b + 1) * D] for b in range(4)], axis=0)
        mixed = jnp.concatenate([win[: self.in_len], low.reshape(-1)[: size - self.in_len]])
        return jnp.where(k < self.mix, win, jnp.where(k > self.mix, out, mixed))


def make_general(dp, seq):
    za, yb, cc = factors(dp)

    def place(z, y, c):
        return ((z % za) * yb + (y % yb)) * cc + (c % cc)

    def perm(dz, dy, dc):
        return [
            (place(z, y, c), place(z + dz, y + dy, c + dc))
            for z in range(za)
            for y in range(yb)
            for c in range(cc)
        ]

    z_next, y_next, c_next = perm(1, 0, 0), perm(0, 1, 0), perm(0, 0, 1)

    def gather_dp(chunk):
        j = lax.axis_index("dp")
        z, y, c = j // (yb * cc), (j // cc) % yb, j % cc
        whole = jnp.zeros((dp,) + chunk.shape, chunk.dtype)
        slots = []
        cur = chunk
        for r in range(za):
            if r:
                cur = lax.ppermute(cur, "dp", z_next)
            side = cur
            for t in range(yb):
                if t:
                    side = lax.ppermute(side, "dp", y_next)
                slots.append((z - r, y - t, c, side))
                if cc == 2:
                    slots.append((z - r, y - t, c + 1, lax.ppermute(side, "dp", c_next)))
        for zi, yi, ci, data in slots:
            at = (((zi + za) % za) * yb + (yi + yb) % yb) * cc + ci % cc
            whole = lax.dynamic_update_index_in_dim(whole, data, at, 0)
        return whole

    def scatter_dp(parts):
        j = lax.axis_index("dp")
        z, y, c = j // (yb * cc), (j // cc) % yb, j % cc

        def pick(zi, yi, ci):
            at = (((zi + za) % za) * yb + (yi + yb) % yb) * cc + ci % cc
            return lax.dynamic_index_in_dim(parts, at, 0, False)

        def core_sum(zi, yi):
            own = pick(zi, yi, c)
            if cc == 2:
                got = lax.ppermute(pick(zi, yi, c + 1), "dp", c_next)
                own = (own.astype(f32) + got.astype(f32)).astype(bf16)
            return own

        def mid_sum(zi):
            acc = None
            for r in range(1, yb + 1):
                mine = core_sum(zi, y - r)
                if acc is not None:
                    acc = (acc.astype(f32) + mine.astype(f32)).astype(bf16)
                else:
                    acc = mine
                if r < yb:
                    acc = lax.ppermute(acc, "dp", y_next)
            return acc

        acc = None
        for r in range(1, za + 1):
            mine = mid_sum(z - r)
            if acc is not None:
                acc = acc.astype(f32) + mine.astype(f32)
            else:
                acc = mine
            if r < za:
                acc = lax.ppermute(acc.astype(bf16), "dp", z_next)
        return acc.astype(f32)

    def swap_seq(a):
        return lax.ppermute(a, "seq", [(0, 1), (1, 0)])

    def halves(a, axis):
        n = a.shape[axis] // 2
        return lax.slice_in_dim(a, 0, n, axis=axis), lax.slice_in_dim(a, n, 2 * n, axis=axis)

    def gather_seq(a, axis):
        if seq != 2:
            return lax.all_gather(a, "seq", axis=axis, tiled=True)
        first = lax.axis_index("seq") == 0
        other = swap_seq(a)
        return jnp.concatenate([jnp.where(first, a, other), jnp.where(first, other, a)], axis=axis)

    def scatter_seq(a, axis):
        if seq != 2:
            return lax.psum_scatter(a, "seq", scatter_dimension=axis, tiled=True)
        first = lax.axis_index("seq") == 0
        low, high = halves(a, axis)
        got = swap_seq(jnp.where(first, high, low).astype(bf16))
        return jnp.where(first, low, high) + got.astype(f32)

    def sum_seq(a):
        if seq != 2:
            return lax.psum(a, "seq")
        a = a.astype(bf16)
        return a.astype(f32) + swap_seq(a).astype(f32)

    def sum_seq_wide(a):
        if seq != 2:
            return lax.psum(a, "seq")
        return a + swap_seq(a)

    def own_seq(a, axis):
        n = a.shape[axis] // seq
        return lax.dynamic_slice_in_dim(a, lax.axis_index("seq") * n, n, axis)

    def sum_all(a):
        for axis, count in (("seq", seq), ("dp", dp)):
            step = 1
            while step < count:
                a = a + lax.ppermute(a, axis, [(i, i ^ step) for i in range(count)])
                step *= 2
        return a

    def on_device(x_in, cotangent, params, moment_one, moment_two):
        size = params.shape[0]
        plan = Plan(dp, seq, size)
        rows = plan.rows
        s = lax.axis_index("seq")
        k = lax.axis_index("dp") * seq + s
        halfs = params.astype(bf16)

        x_own = x_in[0]
        cot_own = cotangent[0]
        tokens = gather_seq(x_own, 0)
        cot = gather_seq(cot_own, 0)

        base = IN + OUT
        at = base - k * size
        padded = jnp.pad(halfs, (SMALL, SMALL))
        tail = lax.dynamic_slice(padded, (jnp.clip(at + SMALL, 0, size + SMALL),), (SMALL,))
        tail = jnp.pad(tail, (0, -SMALL % D)).reshape(-1, D)
        small = sum_all(tail).reshape(-1)
        pieces = []
        offset = 0
        for length in (K * CONV, CONV, D, DI, H, H, H):
            pieces.append(small[offset : offset + length].astype(f32))
            offset += length
        conv_w, conv_b, norm_g, gate_g, a_log, dt_bias, skip_gain = pieces
        conv_w = conv_w.reshape(K, CONV)

        chunk = plan.pack(halfs, k)
        whole = gather_dp(chunk)
        n_in, n_out = plan.j_in, dp - plan.j_out
        w_in = whole[:n_in].reshape(n_in * rows, WIDE)
        w_out = [
            whole[plan.j_out :, :, b * D : (b + 1) * D].reshape(n_out * rows, D) for b in range(4)
        ]
        in_map = lax.dynamic_index_in_dim(jnp.asarray(plan.in_map.reshape(seq, -1)), s, 0, False)
        out_map = lax.dynamic_index_in_dim(
            jnp.asarray(plan.out_map.transpose(0, 2, 1, 3).reshape(seq, 4, -1)), s, 0, False
        )
        pick_in = (jnp.arange(D)[:, None] == in_map[None, :]).astype(bf16)
        pick_out = [(jnp.arange(DI)[:, None] == out_map[b][None, :]).astype(bf16) for b in range(4)]

        wide = tokens.astype(f32)
        scale = lax.rsqrt(jnp.mean(wide * wide, axis=-1, keepdims=True) + norm_eps)
        normed = (wide * scale * norm_g[None, :]).astype(bf16)
        normed_k = dot(normed, pick_in).astype(bf16)
        partial = dot(normed_k, w_in)

        x_part = scatter_seq(partial[:, DI : 2 * DI], 1)
        bcdt = sum_seq(partial[:, 2 * DI : PROJ])
        z_part = scatter_seq(partial[:, :DI], 1)
        gate_in = z_part.astype(bf16).astype(f32)
        x_pre = x_part.astype(bf16)
        bc_pre = bcdt[:, : 2 * N].astype(bf16)
        dt_raw = own_seq(bcdt[:, 2 * N :], 1).astype(bf16).astype(f32)
        hsize = DI // H
        dt_in = dt_raw + own_seq(dt_bias, 0)[None, :]
        step_size = jax.nn.softplus(dt_in)
        alog = own_seq(a_log, 0)[None, :]
        ssd_args = (
            x_pre,
            bc_pre,
            own_seq(conv_w[:, :DI], 1),
            own_seq(conv_b[:DI], 0)[None, :],
            conv_w[:, DI:],
            conv_b[None, DI:],
            step_size,
            step_size.T,
            alog,
            alog.T,
            jnp.repeat(own_seq(skip_gain, 0), hsize)[None, :],
        )
        ssd_out = ssd_forward(hsize, ssd_args)

        d_gated = None
        for b in range(4):
            piece = dot(cot, w_out[b], ((1,), (1,))).astype(bf16)
            piece = dot(piece, pick_out[b], ((1,), (1,)))
            d_gated = piece if d_gated is None else d_gated + piece
        d_gated = scatter_seq(d_gated, 1)

        gain = own_seq(gate_g, 0)[None, :]
        sig = jax.nn.sigmoid(gate_in)
        swish = gate_in * sig
        gated = ssd_out * swish
        weighted = d_gated * gain
        sums = jnp.stack([jnp.sum(gated * gated, axis=1), jnp.sum(weighted * gated, axis=1)])
        sums = sum_seq_wide(sums)
        g_scale = lax.rsqrt(sums[0] / DI + norm_eps)[:, None]
        cross = (sums[1] / DI)[:, None]
        gated_norm = (gated * g_scale * gain).astype(bf16)
        d_gate_g = jnp.sum(d_gated * gated * g_scale, axis=0)
        d_pre = g_scale * weighted - gated * g_scale**3 * cross
        d_ssd = d_pre * swish
        d_gate_in = d_pre * ssd_out * (sig + swish * (1.0 - sig))

        gn_full = gather_seq(gated_norm, 1)
        gn_k = [dot(gn_full, pick_out[b]).astype(bf16) for b in range(4)]
        y_part = None
        for b in range(4):
            piece = dot(gn_k[b], w_out[b])
            y_part = piece if y_part is None else y_part + piece
        y_own = scatter_seq(y_part, 0) + x_own.astype(f32)

        d_x, d_bcpre, d_dtraw, d_wx, d_bx, d_wb, d_bb, d_head, d_skip = ssd_backward(
            hsize, ssd_args + (jax.nn.sigmoid(dt_in), d_ssd)
        )
        d_alog, d_dtbias = d_head[0], d_head[1]
        d_skip = jnp.sum(d_skip.reshape(-1, hsize), axis=1)
        d_z_full = gather_seq(d_gate_in.astype(bf16), 1)
        d_x_full = gather_seq(d_x, 1)
        d_bc = sum_seq(d_bcpre).astype(bf16)
        d_dt_full = gather_seq(d_dtraw.astype(bf16), 1)
        pad = jnp.zeros((d_bc.shape[0], WIDE - PROJ), bf16)
        d_mixed = jnp.concatenate([d_z_full, d_x_full, d_bc, d_dt_full, pad], axis=1)

        g_in = dot(normed_k, d_mixed, ((0,), (0,))).astype(bf16).reshape(n_in, rows, WIDE)
        g_out = jnp.concatenate(
            [dot(gn_k[b], cot, ((0,), (0,))).astype(bf16).reshape(n_out, rows, D) for b in range(4)]
            + [jnp.zeros((n_out, rows, WIDE - 4 * D), bf16)],
            axis=2,
        )
        both = n_in + n_out - dp
        parts = jnp.concatenate(
            [g_in[: n_in - both], g_in[n_in - both :] + g_out[:both], g_out[both:]], axis=0
        )

        dn_k = dot(d_mixed, w_in, ((1,), (1,))).astype(bf16)
        d_normed = scatter_seq(dot(dn_k, pick_in, ((1,), (1,))), 0)
        wide_own = x_own.astype(f32)
        scale_own = lax.rsqrt(jnp.mean(wide_own * wide_own, axis=-1, keepdims=True) + norm_eps)
        a_own = d_normed * norm_g[None, :]
        d_norm_g = jnp.sum(d_normed * wide_own * scale_own, axis=0)
        d_wide = scale_own * a_own - wide_own * scale_own**3 * jnp.mean(
            a_own * wide_own, axis=-1, keepdims=True
        )
        input_grad = (cot_own.astype(f32) + d_wide).astype(bf16)

        def spread(a, width):
            full = jnp.zeros(a.shape[:-1] + (width,), f32)
            start = (0,) * (a.ndim - 1) + (s * a.shape[-1],)
            return lax.dynamic_update_slice(full, a, start)

        small_grad = jnp.concatenate(
            [
                jnp.concatenate([spread(d_wx, DI), d_wb], axis=1).reshape(-1),
                spread(d_bx[0], DI),
                d_bb[0],
                d_norm_g,
                spread(d_gate_g, DI),
                spread(d_alog, H),
                spread(d_dtbias, H),
                spread(d_skip, H),
            ]
        )
        small_grad = jnp.pad(small_grad, (0, -SMALL % D)).reshape(-1, D)
        small_grad = sum_all(small_grad).reshape(-1)[:SMALL]

        grad_chunk = scatter_dp(parts)
        shard = plan.unpack(grad_chunk, k)
        wing = jnp.pad(small_grad, (size, size))
        shard = shard + lax.dynamic_slice(
            wing, (jnp.clip(size - at, 0, size + SMALL),), (size,)
        )
        updated, first_new, second_new = adamw(params, shard, moment_one, moment_two)
        return (y_own.astype(bf16)[None], input_grad[None], shard, updated, first_new, second_new)

    return on_device


def matmul_cost(flops, size):
    return pl.CostEstimate(flops=flops, transcendentals=0, bytes_accessed=size)


def call(kernel, shapes, args, micros, **scratch):
    return pl.pallas_call(
        kernel,
        out_shape=[jax.ShapeDtypeStruct(a, b) for a, b in shapes],
        in_specs=vmem_specs(len(args)),
        out_specs=vmem_specs(len(shapes)),
        cost_estimate=matmul_cost(int(micros * 5e8), int(micros * 2e6)),
        **scratch,
    )(*args)


def front_kernel(depth, nk_ref, w_ref, own_ref, other_ref, rest_ref=None):
    half = own_ref.shape[1]
    nk = nk_ref[...]
    own_ref[...] = dot(nk, w_ref[:depth, :half])
    other_ref[...] = dot(nk, w_ref[:depth, half : 2 * half]).astype(bf16)
    if rest_ref is not None:
        rest_ref[...] = dot(nk, w_ref[:depth, 2 * half :]).astype(bf16)


def gate_grad_kernel(base, cot_ref, wb_ref, wa_ref, pick_ref, own_ref, other_ref):
    half = own_ref.shape[1]
    total = None
    for b in range(4):
        ref = wb_ref if b < 2 else wa_ref
        c = b % 2
        piece = dot(cot_ref[...], ref[base:, c * D : (c + 1) * D], ((1,), (1,))).astype(bf16)
        piece = dot(piece, pick_ref[b], ((1,), (1,)))
        total = piece if total is None else total + piece
    own_ref[...] = total[:, :half]
    other_ref[...] = total[:, half:].astype(bf16)


def pick_kernel(own_ref, other_ref, pick_ref, gk_ref):
    half = own_ref.shape[1]
    for b in range(4):
        gk = dot(own_ref[...], pick_ref[b, :half]) + dot(other_ref[...], pick_ref[b, half:])
        gk_ref[b] = gk.astype(bf16)


def out_kernel(base, gk_ref, wb_ref, wa_ref, y_ref):
    total = None
    for b in range(4):
        ref = wb_ref if b < 2 else wa_ref
        c = b % 2
        piece = dot(gk_ref[b], ref[base:, c * D : (c + 1) * D])
        total = piece if total is None else total + piece
    y_ref[...] = total


def weight_grad_kernel(depth, base, first, nk_ref, d_ref, gk_ref, cot_ref, out_ref):
    cols = out_ref.shape[1]
    nk = nk_ref[...]
    for n in range(0, cols, D):
        stop = min(n + D, cols)
        top = dot(nk, d_ref[:, n:stop], ((0,), (0,)))
        out_ref[:base, n:stop] = top[:base].astype(bf16)
        if n + D <= 2 * D:
            low = dot(gk_ref[first + n // D], cot_ref[...], ((0,), (0,)))
            out_ref[base:depth, n:stop] = (top[base:] + low[: depth - base]).astype(bf16)
            out_ref[depth:, n:stop] = low[depth - base :].astype(bf16)
        else:
            out_ref[base:depth, n:stop] = top[base:].astype(bf16)
            out_ref[depth:, n:stop] = jnp.zeros((out_ref.shape[0] - depth, stop - n), bf16)


def input_grad_kernel(depth, db_ref, da_ref, wb_ref, wa_ref, pick_ref, out_ref):
    dn = dot(db_ref[...], wb_ref[:depth], ((1,), (1,))) + dot(da_ref[...], wa_ref[:depth], ((1,), (1,)))
    out_ref[...] = dot(dn.astype(bf16), pick_ref[...], ((1,), (1,)))


def tie(value, token):
    return lax.optimization_barrier((value, token))[0]


def small_fits(dp, plan):
    return plan.rows * (WIDE - 4 * D) >= SMALL and (dp - 1) * plan.seq > plan.mix


def make_pair(dp, flat):
    seq = 2
    plan = Plan(dp, seq, flat)
    rows = plan.rows
    za, yb, cc = factors(dp)
    inner = DI // seq
    hsize = DI // H
    side = WIDE - 4 * D
    n_in, n_out = plan.j_in, dp - plan.j_out
    depth, base = n_in * rows, plan.j_out * rows

    def place(z, y, c):
        return ((z % za) * yb + (y % yb)) * cc + (c % cc)

    def perm(dz, dy, dc):
        return [
            (place(z, y, c), place(z + dz, y + dy, c + dc))
            for z in range(za)
            for y in range(yb)
            for c in range(cc)
        ]

    z_next, y_next, c_next = perm(1, 0, 0), perm(0, 1, 0), perm(0, 0, 1)

    def position():
        j = lax.axis_index("dp")
        return j // (yb * cc), (j // cc) % yb, j % cc

    def index(z, y, c):
        return (((z + za) % za) * yb + (y + yb) % yb) * cc + c % cc

    def gather_dp(chunk, token=None):
        z, y, c = position()
        slots = []
        cur = chunk
        early = None
        for r in range(za):
            if r:
                if r == za - 1 and token is not None:
                    cur = tie(cur, token)
                cur = lax.ppermute(cur, "dp", z_next)
            if r == 1:
                early = cur
            beside = cur
            for t in range(yb):
                if t:
                    beside = lax.ppermute(beside, "dp", y_next)
                if cc == 2:
                    slots.append((index(z - r, y - t, c + 1), lax.ppermute(beside, "dp", c_next)))
                slots.append((index(z - r, y - t, c), beside))
        whole = jnp.zeros((dp,) + chunk.shape, chunk.dtype)
        for at, data in slots:
            whole = lax.dynamic_update_index_in_dim(whole, data, at, 0)
        return whole.reshape(dp * rows, chunk.shape[1]), early, cur

    def scatter_dp(parts):
        parts = parts.reshape(dp, rows, -1)
        z, y, c = position()

        def pick(zi, yi, ci):
            return lax.dynamic_index_in_dim(parts, index(zi, yi, ci), 0, False)

        def add(a, b):
            return (a.astype(f32) + b.astype(f32)).astype(bf16)

        def core_sum(zi, yi):
            own = pick(zi, yi, c)
            if cc == 2:
                own = add(own, lax.ppermute(pick(zi, yi, c + 1), "dp", c_next))
            return own

        def mid_sum(zi):
            acc = core_sum(zi, y - 1)
            for r in range(2, yb + 1):
                acc = lax.ppermute(acc, "dp", y_next)
                acc = add(acc, core_sum(zi, y - r))
            return acc

        acc = mid_sum(z - 1)
        marks = [acc]
        for r in range(2, za + 1):
            acc = add(lax.ppermute(acc, "dp", z_next), mid_sum(z - r))
            marks.append(acc)
        return acc, marks

    def swap(a):
        return lax.ppermute(a, "seq", [(0, 1), (1, 0)])

    def sum_all(a):
        for axis, count in (("seq", seq), ("dp", dp)):
            step = 1
            while step < count:
                a = a + lax.ppermute(a, axis, [(i, i ^ step) for i in range(count)])
                step *= 2
        return a

    def own_seq(a, axis):
        n = a.shape[axis] // seq
        return lax.dynamic_slice_in_dim(a, lax.axis_index("seq") * n, n, axis)

    def on_device(x_in, cotangent, params, moment_one, moment_two):
        s = lax.axis_index("seq")
        first = s == 0
        k = lax.axis_index("dp") * seq + s
        halfs = params.astype(bf16)

        def ordered(a, other):
            return jnp.concatenate([jnp.where(first, a, other), jnp.where(first, other, a)], axis=0)

        def flip(a, cut):
            return jnp.where(first, a, jnp.concatenate([a[:, cut:], a[:, :cut]], axis=1))

        at = IN + OUT - k * flat
        padded = jnp.pad(halfs, (SMALL, SMALL))
        tail = lax.dynamic_slice(padded, (jnp.clip(at + SMALL, 0, flat + SMALL),), (SMALL,))
        tail = jnp.pad(tail, (0, rows * side - SMALL)).reshape(rows, side)
        tail = tail + swap(tail)

        chunk = plan.pack(halfs, k)
        input_rows = k <= plan.mix
        part_b = jnp.where(input_rows, flip(chunk[:, :DI], inner), chunk[:, :DI])
        mid = chunk[:, DI : 2 * DI]
        part_a = jnp.concatenate(
            [
                jnp.where(input_rows, flip(mid, inner), mid),
                jnp.where(input_rows, chunk[:, 4 * D :], tail),
            ],
            axis=1,
        )
        if plan.mix_out:
            keep = (k == plan.mix) & (jnp.arange(rows) >= plan.mix_in)[:, None]
            part_b = jnp.where(keep, chunk[:, :DI], part_b)
            part_a = jnp.where(keep, chunk[:, DI:], part_a)
        w_a, early, last_a = gather_dp(part_a)
        part_b = tie(part_b, last_a)

        x_own = x_in[0]
        cot_own = cotangent[0]
        tokens = ordered(x_own, swap(x_own))
        cot = ordered(cot_own, swap(cot_own))
        count = tokens.shape[0]

        in_map = lax.dynamic_index_in_dim(jnp.asarray(plan.in_map.reshape(seq, -1)), tie(s, early), 0, False)
        turned = plan.out_map.copy()
        turned[1] = np.where(turned[1] >= 0, (turned[1] + inner) % DI, -1)
        out_map = lax.dynamic_index_in_dim(
            jnp.asarray(turned.transpose(0, 2, 1, 3).reshape(seq, 4, -1)), tie(s, early), 0, False
        )
        pick_in = (jnp.arange(D)[:, None] == in_map[None, :]).astype(bf16)
        pick_out = (jnp.arange(DI)[None, :, None] == out_map[:, None, :]).astype(bf16)

        small = w_a[(dp - 1) * rows :, 2 * D :].reshape(-1)
        pieces = []
        offset = 0
        for length in (K * CONV, CONV, D, DI, H, H, H):
            pieces.append(small[offset : offset + length].astype(f32))
            offset += length
        conv_w, conv_b, norm_g, gate_g, a_log, dt_bias, skip_gain = pieces
        conv_w = conv_w.reshape(K, CONV)

        wide = tokens.astype(f32)
        scale = lax.rsqrt(jnp.mean(wide * wide, axis=-1, keepdims=True) + norm_eps)
        normed = (wide * scale * norm_g[None, :]).astype(bf16)
        normed_k = dot(normed, pick_in).astype(bf16)

        x_own_part, x_other, bcdt = call(
            functools.partial(front_kernel, depth),
            [((count, inner), f32), ((count, inner), bf16), ((count, side), bf16)],
            (normed_k, w_a),
            4.0,
        )
        w_b, _, _ = gather_dp(part_b, x_other)
        bcdt = bcdt.astype(f32) + swap(bcdt).astype(f32)
        x_pre = (x_own_part + swap(x_other).astype(f32)).astype(bf16)
        bc_pre = bcdt[:, : 2 * N].astype(bf16)
        dt_raw = own_seq(bcdt[:, 2 * N : 2 * N + H], 1).astype(bf16).astype(f32)
        dt_in = dt_raw + own_seq(dt_bias, 0)[None, :]
        step_size = jax.nn.softplus(dt_in)
        alog = own_seq(a_log, 0)[None, :]
        ssd_args = (
            x_pre,
            bc_pre,
            own_seq(conv_w[:, :DI], 1),
            own_seq(conv_b[:DI], 0)[None, :],
            conv_w[:, DI:],
            conv_b[None, DI:],
            step_size,
            step_size.T,
            alog,
            alog.T,
            jnp.repeat(own_seq(skip_gain, 0), hsize)[None, :],
        )
        ssd_out = ssd_forward(hsize, ssd_args)

        z_own_part, z_other = call(
            functools.partial(front_kernel, depth),
            [((count, inner), f32), ((count, inner), bf16)],
            (normed_k, w_b),
            3.0,
        )
        gate_in = (z_own_part + swap(z_other).astype(f32)).astype(bf16).astype(f32)
        dg_own, dg_other = call(
            functools.partial(gate_grad_kernel, base),
            [((count, inner), f32), ((count, inner), bf16)],
            (cot, w_b, w_a, pick_out),
            6.0,
        )
        d_gated = dg_own + swap(dg_other).astype(f32)

        gain = own_seq(gate_g, 0)[None, :]
        sig = jax.nn.sigmoid(gate_in)
        swish = gate_in * sig
        gated = ssd_out * swish
        weighted = d_gated * gain
        sums = jnp.stack([jnp.sum(gated * gated, axis=1), jnp.sum(weighted * gated, axis=1)])
        sums = sums + swap(sums)
        g_scale = lax.rsqrt(sums[0] / DI + norm_eps)[:, None]
        cross = (sums[1] / DI)[:, None]
        gn_own = (gated * g_scale * gain).astype(bf16)
        d_gate_g = jnp.sum(d_gated * gated * g_scale, axis=0)
        d_pre = g_scale * weighted - gated * g_scale**3 * cross
        d_ssd = d_pre * swish
        dz_own = (d_pre * ssd_out * (sig + swish * (1.0 - sig))).astype(bf16)
        gn_own, dz_own, d_ssd = lax.optimization_barrier((gn_own, dz_own, d_ssd))
        gn_other = swap(gn_own)
        dz_other = swap(dz_own)

        d_x, d_bcpre, d_dtraw, d_wx, d_bx, d_wb, d_bb, d_head, d_skip = ssd_backward(
            hsize, ssd_args + (jax.nn.sigmoid(dt_in), d_ssd)
        )
        d_alog, d_dtbias = d_head[0], d_head[1]
        d_skip = jnp.sum(d_skip.reshape(-1, hsize), axis=1)

        gn_k = call(
            pick_kernel, [((4, count, n_out * rows), bf16)], (gn_own, gn_other, pick_out), 3.0
        )[0]
        d_b = jnp.concatenate([dz_own, dz_other], axis=1)
        parts_b = call(
            functools.partial(weight_grad_kernel, depth, base, 0),
            [((dp * rows, DI), bf16)],
            (normed_k, d_b, gn_k, cot),
            5.0,
        )[0]
        grad_b, marks_b = scatter_dp(parts_b)

        bcdt_own = jnp.concatenate([d_bcpre, d_dtraw], axis=1).astype(bf16)
        dx_other, bcdt_other = swap(d_x), swap(bcdt_own)
        d_bc = (bcdt_own[:, : 2 * N].astype(f32) + bcdt_other[:, : 2 * N].astype(f32)).astype(bf16)
        dt_pair = jnp.where(
            first,
            jnp.concatenate([bcdt_own[:, 2 * N :], bcdt_other[:, 2 * N :]], axis=1),
            jnp.concatenate([bcdt_other[:, 2 * N :], bcdt_own[:, 2 * N :]], axis=1),
        )
        blank = jnp.zeros((count, WIDE - PROJ), bf16)
        d_a = jnp.concatenate([d_x, dx_other, d_bc, dt_pair, blank], axis=1)
        parts_a = call(
            functools.partial(weight_grad_kernel, depth, base, 2),
            [((dp * rows, 2 * D + side), bf16)],
            (normed_k, d_a, gn_k, cot),
            5.0,
        )[0]
        grad_a, marks_a = scatter_dp(parts_a)

        y_part = call(
            functools.partial(out_kernel, base),
            [((count, D), f32)],
            (tie(gn_k, marks_b[0]), w_b, w_a),
            4.0,
        )[0]
        d_normed = call(
            functools.partial(input_grad_kernel, depth),
            [((count, D), f32)],
            (d_b, tie(d_a, marks_a[0]), w_b, w_a, pick_in),
            5.0,
        )[0]

        def own_tokens(a):
            half = count // 2
            low, high = a[:half], a[half:]
            got = swap(jnp.where(first, high, low).astype(bf16))
            return jnp.where(first, low, high) + got.astype(f32)

        d_norm_g = jnp.sum(d_normed * wide * scale, axis=0)
        d_own = own_tokens(d_normed)
        y_own = own_tokens(y_part) + x_own.astype(f32)
        wide_own = x_own.astype(f32)
        scale_own = lax.rsqrt(jnp.mean(wide_own * wide_own, axis=-1, keepdims=True) + norm_eps)
        a_own = d_own * norm_g[None, :]
        d_wide = scale_own * a_own - wide_own * scale_own**3 * jnp.mean(
            a_own * wide_own, axis=-1, keepdims=True
        )
        input_grad = (cot_own.astype(f32) + d_wide).astype(bf16)

        def spread(a, width):
            full = jnp.zeros(a.shape[:-1] + (width,), f32)
            start = (0,) * (a.ndim - 1) + (s * a.shape[-1],)
            return lax.dynamic_update_slice(full, a, start)

        small_grad = jnp.concatenate(
            [
                jnp.concatenate([spread(d_wx, DI), d_wb], axis=1).reshape(-1),
                spread(d_bx[0], DI),
                d_bb[0],
                d_norm_g,
                spread(d_gate_g, DI),
                spread(d_alog, H),
                spread(d_dtbias, H),
                spread(d_skip, H),
            ]
        )
        small_grad = jnp.pad(small_grad, (0, -SMALL % D)).reshape(-1, D)
        small_grad = sum_all(small_grad).reshape(-1)[:SMALL]

        def unflip(a, cut):
            keep = k > plan.mix
            if plan.mix_out:
                keep = keep | ((k == plan.mix) & (jnp.arange(rows) >= plan.mix_in)[:, None])
            return jnp.where(keep, a, flip(a, cut))

        grad_a, grad_b = grad_a.astype(f32), grad_b.astype(f32)
        grad_chunk = jnp.concatenate(
            [unflip(grad_b, inner), unflip(grad_a[:, : 2 * D], inner), grad_a[:, 2 * D :]], axis=1
        )
        shard = plan.unpack(grad_chunk, k)
        wing = jnp.pad(small_grad, (flat, flat))
        shard = shard + lax.dynamic_slice(wing, (jnp.clip(flat - at, 0, flat + SMALL),), (flat,))
        updated, first_new, second_new = adamw(params, shard, moment_one, moment_two)
        return (y_own.astype(bf16)[None], input_grad[None], shard, updated, first_new, second_new)

    return on_device


def make(dp, seq):
    def on_device(x_in, cotangent, params, moment_one, moment_two):
        flat = params.shape[0]
        if seq == 2 and small_fits(dp, Plan(dp, seq, flat)):
            return make_pair(dp, flat)(x_in, cotangent, params, moment_one, moment_two)
        return make_general(dp, seq)(x_in, cotangent, params, moment_one, moment_two)

    return on_device


def solution(mesh):
    return jax.shard_map(
        make(mesh.shape["dp"], mesh.shape["seq"]),
        mesh=mesh,
        in_specs=(
            P("dp", "seq", None),
            P("dp", "seq", None),
            P(("dp", "seq")),
            P(("dp", "seq")),
            P(("dp", "seq")),
        ),
        out_specs=(
            P("dp", "seq", None),
            P("dp", "seq", None),
            P(("dp", "seq")),
            P(("dp", "seq")),
            P(("dp", "seq")),
            P(("dp", "seq")),
        ),
        check_vma=False,
    )
```

```python
import functools
import jax
import jax.numpy as jnp
import numpy as np
from jax import lax
from jax.experimental import pallas as pl
from jax.experimental.pallas import tpu as pltpu
from jax.sharding import PartitionSpec as P

D = 1024
DI = 2048
N = 128
K = 4
SPAN = 128
H = 32
CONV = 2304
PROJ = 4384
WIDE = 4480
IN = D * PROJ
OUT = DI * D
SMALL = K * CONV + CONV + D + DI + 3 * H

norm_eps = 1e-05
learn_rate = 0.005
beta_one = 0.9
beta_two = 0.95
adam_eps = 1e-08
weight_decay = 0.1
adam_step = 10

bf16 = jnp.bfloat16
f32 = jnp.float32


def ceil_to(value, unit):
    return -(-value // unit) * unit


def factors(count):
    core = 2 if count % 2 == 0 else 1
    rest = count // core
    mid = 1
    while rest % (mid * 2) == 0 and (mid * 2) ** 2 <= rest * 1:
        mid *= 2
    return rest // mid, mid, core


def dot(a, b, dims=((1,), (0,))):
    return lax.dot_general(a, b, (dims, ((), ())), preferred_element_type=f32)


def col_roll(a, steps):
    rows = a.shape[0]
    at = lax.broadcasted_iota(jnp.int32, a.shape, 0)
    if steps >= 0:
        return jnp.where(at >= steps, pltpu.roll(a, steps, 0), 0.0)
    return jnp.where(at < rows + steps, pltpu.roll(a, rows + steps, 0), 0.0)


def conv_act(x, taps, bias):
    acc = bias + taps[K - 1 : K] * x
    for k in range(1, K):
        acc = acc + taps[K - 1 - k : K - k] * col_roll(x, k)
    sig = 1.0 / (1.0 + jnp.exp(-acc))
    return acc, sig


def conv_back(x, taps, d_acc):
    d_x = taps[K - 1 : K] * d_acc
    d_taps = [jnp.sum(d_acc * x, axis=0, keepdims=True)]
    for k in range(1, K):
        d_x = d_x + taps[K - 1 - k : K - k] * col_roll(d_acc, -k)
        d_taps.insert(0, jnp.sum(d_acc * col_roll(x, k), axis=0, keepdims=True))
    return d_x, d_taps, jnp.sum(d_acc, axis=0, keepdims=True)


def fine(a, b, dims):
    return lax.dot_general(
        a, b, (dims, ((), ())), precision=lax.Precision.HIGHEST, preferred_element_type=f32
    )


def tri_parts():
    row = lax.broadcasted_iota(jnp.int32, (SPAN, SPAN), 0)
    col = lax.broadcasted_iota(jnp.int32, (SPAN, SPAN), 1)
    return row >= col, row == col


def rates(c, step_ref, turn_ref, alog_ref, alog_turn_ref, lower):
    span = slice(c * SPAN, (c + 1) * SPAN)
    rate = step_ref[span, :] * -jnp.exp(alog_ref[...])
    rate_turn = turn_ref[:, span] * -jnp.exp(alog_turn_ref[...])
    within = fine(lower, rate, ((1,), (0,)))
    within_turn = fine(rate_turn, lower, ((1,), (1,)))
    return rate, within, within_turn


def lanes_of(pair, first, second):
    lane = lax.broadcasted_iota(jnp.int32, (1, 2 * pair), 1)
    return jnp.where(lane < pair, first, second)


def ssd_forward_kernel(
    hsize, x_ref, bc_ref, wx_ref, bx_ref, wb_ref, bb_ref, step_ref, turn_ref, alog_ref, alog_turn_ref, skip_ref, out_ref
):
    rows, inner = x_ref.shape
    blocks = rows // SPAN
    causal, _ = tri_parts()
    lower = causal.astype(f32)
    acc, sig = conv_act(bc_ref[...].astype(f32), wb_ref[...], bb_ref[...])
    bc = (acc * sig).astype(bf16)
    b_blk = [bc[c * SPAN : (c + 1) * SPAN, :N] for c in range(blocks)]
    c_blk = [bc[c * SPAN : (c + 1) * SPAN, N:] for c in range(blocks)]
    cross = [dot(c_blk[c], b_blk[c], ((1,), (1,))) for c in range(blocks)]
    rated = [rates(c, step_ref, turn_ref, alog_ref, alog_turn_ref, lower) for c in range(blocks)]
    width = 2 * hsize
    lane = lax.broadcasted_iota(jnp.int32, (1, width), 1)
    masks = [(lane < hsize).astype(f32), (lane >= hsize).astype(f32)]
    for g in range(inner // width):
        cols = slice(g * width, (g + 1) * width)
        acc, sig = conv_act(x_ref[:, cols].astype(f32), wx_ref[:, cols], bx_ref[:, cols])
        vals = acc * sig
        state = None
        for c in range(blocks):
            span = slice(c * SPAN, (c + 1) * SPAN)
            _, within, within_turn = rated[c]
            v = vals[span]
            mix, split = [], []
            for i in range(2):
                h = 2 * g + i
                gap = within[:, h : h + 1] - within_turn[h : h + 1, :]
                mix.append(
                    (jnp.exp(jnp.where(causal, gap, -10000.0)) * cross[c] * turn_ref[h : h + 1, span]).astype(bf16)
                )
                split.append((v * masks[i]).astype(bf16))
            out = dot(jnp.concatenate(mix, axis=1), jnp.concatenate(split, axis=0))
            w0, w1 = within[:, 2 * g : 2 * g + 1], within[:, 2 * g + 1 : 2 * g + 2]
            if state is not None:
                out = out + lanes_of(hsize, jnp.exp(w0), jnp.exp(w1)) * dot(c_blk[c], state.astype(bf16))
            out_ref[span, cols] = out + skip_ref[:, cols] * v
            if c < blocks - 1:
                e0, e1 = w0[SPAN - 1 :], w1[SPAN - 1 :]
                tail = lanes_of(
                    hsize,
                    jnp.exp(e0 - w0) * step_ref[span, 2 * g : 2 * g + 1],
                    jnp.exp(e1 - w1) * step_ref[span, 2 * g + 1 : 2 * g + 2],
                )
                fresh = dot(b_blk[c], (tail * v).astype(bf16), ((0,), (0,)))
                if state is not None:
                    fresh = fresh + lanes_of(hsize, jnp.exp(e0), jnp.exp(e1)) * state
                state = fresh


def ssd_backward_kernel(
    hsize, x_ref, bc_ref, wx_ref, bx_ref, wb_ref, bb_ref, step_ref, turn_ref, alog_ref, alog_turn_ref, skip_ref,
    slope_ref, dy_ref, dx_ref, dbc_ref, ddt_ref, dwx_ref, dbx_ref, dwb_ref, dbb_ref, dhead_ref, dskip_ref,
    dcross_ref, dbmat_ref, dcmat_ref, col_ref, scol_ref, row_ref, srow_ref,
):
    rows, inner = x_ref.shape
    heads = step_ref.shape[1]
    blocks = rows // SPAN
    causal, eye = tri_parts()
    lower = causal.astype(f32)
    eye = eye.astype(f32)
    bc_in = bc_ref[...].astype(f32)
    bc_acc, bc_sig = conv_act(bc_in, wb_ref[...], bb_ref[...])
    bc = (bc_acc * bc_sig).astype(bf16)
    b_blk = [bc[c * SPAN : (c + 1) * SPAN, :N] for c in range(blocks)]
    c_blk = [bc[c * SPAN : (c + 1) * SPAN, N:] for c in range(blocks)]
    cross = [dot(c_blk[c], b_blk[c], ((1,), (1,))) for c in range(blocks)]
    rated = [rates(c, step_ref, turn_ref, alog_ref, alog_turn_ref, lower) for c in range(blocks)]
    for ref in (dcross_ref, dbmat_ref, dcmat_ref, col_ref, scol_ref, row_ref, srow_ref):
        ref[...] = jnp.zeros_like(ref)
    width = 2 * hsize
    lane = lax.broadcasted_iota(jnp.int32, (1, width), 1)
    masks = [(lane < hsize).astype(f32), (lane >= hsize).astype(f32)]
    head_lane = lax.broadcasted_iota(jnp.int32, (1, heads), 1)
    head_row = lax.broadcasted_iota(jnp.int32, (heads, 1), 0)
    last_row = lax.broadcasted_iota(jnp.int32, (SPAN, 1), 0) == SPAN - 1
    for g in range(inner // width):
        cols = slice(g * width, (g + 1) * width)
        x = x_ref[:, cols].astype(f32)
        acc, sig = conv_act(x, wx_ref[:, cols], bx_ref[:, cols])
        vals = acc * sig
        states, tails, decays = [None], [], []
        for c in range(blocks):
            span = slice(c * SPAN, (c + 1) * SPAN)
            within = rated[c][1]
            w0, w1 = within[:, 2 * g : 2 * g + 1], within[:, 2 * g + 1 : 2 * g + 2]
            e0, e1 = w0[SPAN - 1 :], w1[SPAN - 1 :]
            if c < blocks - 1:
                tails.append(
                    lanes_of(
                        hsize,
                        jnp.exp(e0 - w0) * step_ref[span, 2 * g : 2 * g + 1],
                        jnp.exp(e1 - w1) * step_ref[span, 2 * g + 1 : 2 * g + 2],
                    )
                )
                decays.append(lanes_of(hsize, jnp.exp(e0), jnp.exp(e1)))
                fresh = dot(b_blk[c], (tails[c] * vals[span]).astype(bf16), ((0,), (0,)))
                if states[c] is not None:
                    fresh = fresh + decays[c] * states[c]
                states.append(fresh)
        d_state = None
        d_vals = [None] * blocks
        d_skip = jnp.zeros((1, width), f32)
        for c in reversed(range(blocks)):
            span = slice(c * SPAN, (c + 1) * SPAN)
            _, within, within_turn = rated[c]
            v = vals[span]
            v_low = v.astype(bf16)
            dy = dy_ref[span, cols].astype(f32)
            ws = [within[:, 2 * g + i : 2 * g + i + 1] for i in range(2)]
            mix, split, d_w = [], [], []
            d_cross = None
            for i in range(2):
                h = 2 * g + i
                turn = turn_ref[h : h + 1, span]
                decay = jnp.exp(jnp.where(causal, ws[i] - within_turn[h : h + 1, :], -10000.0))
                scored = decay * cross[c]
                mix.append((scored * turn).astype(bf16))
                d_half = (dy * masks[i]).astype(bf16)
                split.append(d_half)
                d_mix = dot(d_half, v_low, ((1,), (1,)))
                raw = d_mix * scored
                part = d_mix * decay * turn
                d_cross = part if d_cross is None else d_cross + part
                d_w.append(jnp.sum(raw * turn, axis=1, keepdims=True))
                raw_sum = jnp.sum(raw, axis=0, keepdims=True)
                row_ref[c] += jnp.where(head_row == h, -raw_sum * turn, 0.0)
                srow_ref[c] += jnp.where(head_row == h, raw_sum, 0.0)
            dcross_ref[c] += d_cross
            d_v = dot(jnp.concatenate(mix, axis=0), jnp.concatenate(split, axis=0), ((0,), (0,)))
            d_v = d_v + skip_ref[:, cols] * dy
            d_skip = d_skip + jnp.sum(dy * v, axis=0, keepdims=True)
            d_enter = None
            if states[c] is not None:
                st = states[c].astype(bf16)
                lifted = lanes_of(hsize, jnp.exp(ws[0]), jnp.exp(ws[1])) * dy
                lift_low = lifted.astype(bf16)
                dcmat_ref[span] += dot(lift_low, st, ((1,), (1,)))
                d_enter = dot(c_blk[c], lift_low, ((0,), (0,)))
                prod = lifted * dot(c_blk[c], st)
                for i in range(2):
                    d_w[i] = d_w[i] + jnp.sum(prod * masks[i], axis=1, keepdims=True)
            if d_state is not None:
                ds_low = d_state.astype(bf16)
                back = dot(b_blk[c], ds_low)
                d_v = d_v + tails[c] * back
                dbmat_ref[span] += dot((tails[c] * v).astype(bf16), ds_low, ((1,), (1,)))
                along = v * back
                if states[c] is not None:
                    held = decays[c] * d_state * states[c]
                for i in range(2):
                    h = 2 * g + i
                    d_tail = jnp.sum(along * masks[i], axis=1, keepdims=True)
                    reach = jnp.exp(ws[i][SPAN - 1 :] - ws[i])
                    scol_ref[c] += jnp.where(head_lane == h, d_tail * reach, 0.0)
                    fall = d_tail * reach * step_ref[span, h : h + 1]
                    d_end = jnp.sum(fall, axis=0, keepdims=True)
                    if states[c] is not None:
                        d_end = d_end + jnp.sum(
                            jnp.sum(held * masks[i], axis=1, keepdims=True), axis=0, keepdims=True
                        )
                    d_w[i] = d_w[i] - fall + jnp.where(last_row, d_end, 0.0)
                if d_enter is not None:
                    d_enter = d_enter + decays[c] * d_state
            for i in range(2):
                col_ref[c] += jnp.where(head_lane == 2 * g + i, d_w[i], 0.0)
            d_state = d_enter
            d_vals[c] = d_v
        d_acc = jnp.concatenate(d_vals, axis=0) * (sig + vals * (1.0 - sig))
        d_x, d_taps, d_bias = conv_back(x, wx_ref[:, cols], d_acc)
        dx_ref[:, cols] = d_x.astype(bf16)
        for k in range(K):
            dwx_ref[k : k + 1, cols] = d_taps[k]
        dbx_ref[:, cols] = d_bias
        dskip_ref[:, cols] = d_skip
    d_alog = jnp.zeros((1, heads), f32)
    d_dtb = jnp.zeros((1, heads), f32)
    for c in range(blocks):
        span = slice(c * SPAN, (c + 1) * SPAN)
        d_w = col_ref[c] + fine(eye, row_ref[c], ((1,), (1,)))
        d_step = scol_ref[c] + fine(eye, srow_ref[c], ((1,), (1,)))
        d_rate = fine(lower, d_w, ((0,), (0,)))
        d_alog = d_alog + jnp.sum(rated[c][0] * d_rate, axis=0, keepdims=True)
        d_dt = (d_step - jnp.exp(alog_ref[...]) * d_rate) * slope_ref[span, :]
        ddt_ref[span, :] = d_dt
        d_dtb = d_dtb + jnp.sum(d_dt, axis=0, keepdims=True)
        low = dcross_ref[c].astype(bf16)
        dcmat_ref[span] += dot(low, b_blk[c])
        dbmat_ref[span] += dot(low, c_blk[c], ((0,), (0,)))
    dhead_ref[0:1, :] = d_alog
    dhead_ref[1:2, :] = d_dtb
    d_bc = jnp.concatenate([dbmat_ref[...], dcmat_ref[...]], axis=1)
    d_acc = d_bc * (bc_sig + bc_acc * bc_sig * (1.0 - bc_sig))
    d_x, d_taps, d_bias = conv_back(bc_in, wb_ref[...], d_acc)
    dbc_ref[...] = d_x
    for k in range(K):
        dwb_ref[k : k + 1, :] = d_taps[k]
    dbb_ref[...] = d_bias


def vmem_specs(count):
    return [pl.BlockSpec(memory_space=pltpu.VMEM)] * count


def ssd_forward(hsize, args):
    return pl.pallas_call(
        functools.partial(ssd_forward_kernel, hsize),
        out_shape=jax.ShapeDtypeStruct(args[0].shape, f32),
        in_specs=vmem_specs(len(args)),
        out_specs=vmem_specs(1)[0],
        cost_estimate=pl.CostEstimate(flops=int(2.5e9), transcendentals=0, bytes_accessed=int(1e7)),
        name="ssd_forward",
    )(*args)


def ssd_backward(hsize, args):
    rows, inner = args[0].shape
    heads = args[6].shape[1]
    blocks = rows // SPAN
    shapes = [
        ((rows, inner), bf16),
        ((rows, 2 * N), f32),
        ((rows, heads), f32),
        ((K, inner), f32),
        ((1, inner), f32),
        ((K, 2 * N), f32),
        ((1, 2 * N), f32),
        ((2, heads), f32),
        ((1, inner), f32),
    ]
    return pl.pallas_call(
        functools.partial(ssd_backward_kernel, hsize),
        out_shape=[jax.ShapeDtypeStruct(a, b) for a, b in shapes],
        in_specs=vmem_specs(len(args)),
        out_specs=vmem_specs(len(shapes)),
        scratch_shapes=[
            pltpu.VMEM((blocks, SPAN, SPAN), f32),
            pltpu.VMEM((rows, N), f32),
            pltpu.VMEM((rows, N), f32),
            pltpu.VMEM((blocks, SPAN, heads), f32),
            pltpu.VMEM((blocks, SPAN, heads), f32),
            pltpu.VMEM((blocks, heads, SPAN), f32),
            pltpu.VMEM((blocks, heads, SPAN), f32),
        ],
        cost_estimate=pl.CostEstimate(flops=int(6e9), transcendentals=0, bytes_accessed=int(2.4e7)),
        name="ssd_backward",
    )(*args)


def adamw(param_vec, grad_vec, first, second):
    first_new = beta_one * first + (1.0 - beta_one) * grad_vec
    second_new = beta_two * second + (1.0 - beta_two) * grad_vec * grad_vec
    first_hat = first_new / (1.0 - beta_one**adam_step)
    second_hat = second_new / (1.0 - beta_two**adam_step)
    updated = param_vec - learn_rate * (
        first_hat / (jnp.sqrt(second_hat) + adam_eps) + weight_decay * param_vec
    )
    return (updated, first_new, second_new)


class Plan:
    def __init__(self, dp, seq, flat):
        self.dp, self.seq, self.flat = dp, seq, flat
        self.total = dp * seq
        count = self.total
        self.mix = IN // flat
        last_in = -(-IN // flat)
        rows_in = max(
            -(-(((k * flat) % PROJ) + min(flat, IN - k * flat)) // PROJ) for k in range(last_in)
        )
        rows_out = max(
            -(-(((k * flat - IN) % D) + flat) // D) for k in range(self.mix, count)
        )
        self.rows = ceil_to(max(rows_in, -(-rows_out // 4)), 8)
        self.in_len = IN - self.mix * flat
        self.mix_in = -(-(((self.mix * flat) % PROJ) + self.in_len) // PROJ)
        self.mix_out = -(-(flat - self.in_len) // D)
        self.mix_free = self.rows - self.mix_in
        assert 4 * self.mix_free >= self.mix_out
        rows = self.rows
        self.j_in = self.mix // seq + 1
        self.j_out = self.mix // seq
        n_in, n_out = self.j_in, dp - self.j_out
        self.in_map = np.full((seq, n_in, rows), -1, np.int32)
        self.out_map = np.full((seq, n_out, 4, rows), -1, np.int32)
        m = np.arange(rows)
        for s in range(seq):
            for j in range(n_in):
                k = j * seq + s
                if k > self.mix:
                    continue
                first = (k * flat) // PROJ
                used = min(rows, D - first)
                if k == self.mix:
                    used = self.mix_in
                self.in_map[s, j, :used] = first + m[:used]
            for j in range(n_out):
                k = (j + self.j_out) * seq + s
                if k < self.mix:
                    continue
                for b in range(4):
                    if k == self.mix:
                        q = b * self.mix_free + (m - self.mix_in)
                        ok = (m >= self.mix_in) & (q < self.mix_out)
                    else:
                        q = (k * flat - IN) // D + b * rows + m
                        ok = q < min(DI, -(-((k + 1) * flat - IN) // D))
                    self.out_map[s, j, b] = np.where(ok, q, -1)

    def pack(self, flat, k):
        rows, size = self.rows, self.flat
        shift = (k * size) % PROJ
        span = rows * PROJ
        buf = jnp.pad(flat, (PROJ, span - size))
        win = lax.dynamic_slice(buf, (PROJ - shift,), (span,)).reshape(rows, PROJ)
        win = jnp.pad(win, ((0, 0), (0, WIDE - PROJ)))
        off = (k * size - IN) % D
        span = 4 * rows * D
        buf = jnp.pad(flat, (D, span - size))
        out = lax.dynamic_slice(buf, (D - off,), (span,)).reshape(4, rows, D)
        out = jnp.concatenate([out[b] for b in range(4)] + [jnp.zeros((rows, WIDE - 4 * D), flat.dtype)], axis=1)
        head = flat[self.in_len :]
        free = self.mix_free
        head = jnp.pad(head, (0, 4 * free * D - head.shape[0])).reshape(4, free, D)
        low = jnp.concatenate([head[b] for b in range(4)] + [jnp.zeros((free, WIDE - 4 * D), flat.dtype)], axis=1)
        mixed = jnp.concatenate([win[: self.mix_in], low], axis=0)
        return jnp.where(k < self.mix, win, jnp.where(k > self.mix, out, mixed))

    def unpack(self, chunk, k):
        rows, size = self.rows, self.flat
        shift = (k * size) % PROJ
        line = chunk[:, :PROJ].reshape(-1)
        line = jnp.pad(line, (0, max(0, PROJ + size - rows * PROJ)))
        win = lax.dynamic_slice(line, (shift,), (size,))
        off = (k * size - IN) % D
        line = jnp.concatenate([chunk[:, b * D : (b + 1) * D] for b in range(4)], axis=0).reshape(-1)
        line = jnp.pad(line, (0, max(0, D + size - 4 * rows * D)))
        out = lax.dynamic_slice(line, (off,), (size,))
        low = chunk[self.mix_in :]
        low = jnp.concatenate([low[:, b * D : (b + 1) * D] for b in range(4)], axis=0)
        mixed = jnp.concatenate([win[: self.in_len], low.reshape(-1)[: size - self.in_len]])
        return jnp.where(k < self.mix, win, jnp.where(k > self.mix, out, mixed))


def make_general(dp, seq):
    za, yb, cc = factors(dp)

    def place(z, y, c):
        return ((z % za) * yb + (y % yb)) * cc + (c % cc)

    def perm(dz, dy, dc):
        return [
            (place(z, y, c), place(z + dz, y + dy, c + dc))
            for z in range(za)
            for y in range(yb)
            for c in range(cc)
        ]

    z_next, y_next, c_next = perm(1, 0, 0), perm(0, 1, 0), perm(0, 0, 1)

    def gather_dp(chunk):
        j = lax.axis_index("dp")
        z, y, c = j // (yb * cc), (j // cc) % yb, j % cc
        whole = jnp.zeros((dp,) + chunk.shape, chunk.dtype)
        slots = []
        cur = chunk
        for r in range(za):
            if r:
                cur = lax.ppermute(cur, "dp", z_next)
            side = cur
            for t in range(yb):
                if t:
                    side = lax.ppermute(side, "dp", y_next)
                slots.append((z - r, y - t, c, side))
                if cc == 2:
                    slots.append((z - r, y - t, c + 1, lax.ppermute(side, "dp", c_next)))
        for zi, yi, ci, data in slots:
            at = (((zi + za) % za) * yb + (yi + yb) % yb) * cc + ci % cc
            whole = lax.dynamic_update_index_in_dim(whole, data, at, 0)
        return whole

    def scatter_dp(parts):
        j = lax.axis_index("dp")
        z, y, c = j // (yb * cc), (j // cc) % yb, j % cc

        def pick(zi, yi, ci):
            at = (((zi + za) % za) * yb + (yi + yb) % yb) * cc + ci % cc
            return lax.dynamic_index_in_dim(parts, at, 0, False)

        def core_sum(zi, yi):
            own = pick(zi, yi, c)
            if cc == 2:
                got = lax.ppermute(pick(zi, yi, c + 1), "dp", c_next)
                own = (own.astype(f32) + got.astype(f32)).astype(bf16)
            return own

        def mid_sum(zi):
            acc = None
            for r in range(1, yb + 1):
                mine = core_sum(zi, y - r)
                if acc is not None:
                    acc = (acc.astype(f32) + mine.astype(f32)).astype(bf16)
                else:
                    acc = mine
                if r < yb:
                    acc = lax.ppermute(acc, "dp", y_next)
            return acc

        acc = None
        for r in range(1, za + 1):
            mine = mid_sum(z - r)
            if acc is not None:
                acc = acc.astype(f32) + mine.astype(f32)
            else:
                acc = mine
            if r < za:
                acc = lax.ppermute(acc.astype(bf16), "dp", z_next)
        return acc.astype(f32)

    def swap_seq(a):
        return lax.ppermute(a, "seq", [(0, 1), (1, 0)])

    def halves(a, axis):
        n = a.shape[axis] // 2
        return lax.slice_in_dim(a, 0, n, axis=axis), lax.slice_in_dim(a, n, 2 * n, axis=axis)

    def gather_seq(a, axis):
        if seq != 2:
            return lax.all_gather(a, "seq", axis=axis, tiled=True)
        first = lax.axis_index("seq") == 0
        other = swap_seq(a)
        return jnp.concatenate([jnp.where(first, a, other), jnp.where(first, other, a)], axis=axis)

    def scatter_seq(a, axis):
        if seq != 2:
            return lax.psum_scatter(a, "seq", scatter_dimension=axis, tiled=True)
        first = lax.axis_index("seq") == 0
        low, high = halves(a, axis)
        got = swap_seq(jnp.where(first, high, low).astype(bf16))
        return jnp.where(first, low, high) + got.astype(f32)

    def sum_seq(a):
        if seq != 2:
            return lax.psum(a, "seq")
        a = a.astype(bf16)
        return a.astype(f32) + swap_seq(a).astype(f32)

    def sum_seq_wide(a):
        if seq != 2:
            return lax.psum(a, "seq")
        return a + swap_seq(a)

    def own_seq(a, axis):
        n = a.shape[axis] // seq
        return lax.dynamic_slice_in_dim(a, lax.axis_index("seq") * n, n, axis)

    def sum_all(a):
        for axis, count in (("seq", seq), ("dp", dp)):
            step = 1
            while step < count:
                a = a + lax.ppermute(a, axis, [(i, i ^ step) for i in range(count)])
                step *= 2
        return a

    def on_device(x_in, cotangent, params, moment_one, moment_two):
        size = params.shape[0]
        plan = Plan(dp, seq, size)
        rows = plan.rows
        s = lax.axis_index("seq")
        k = lax.axis_index("dp") * seq + s
        halfs = params.astype(bf16)

        x_own = x_in[0]
        cot_own = cotangent[0]
        tokens = gather_seq(x_own, 0)
        cot = gather_seq(cot_own, 0)

        base = IN + OUT
        at = base - k * size
        padded = jnp.pad(halfs, (SMALL, SMALL))
        tail = lax.dynamic_slice(padded, (jnp.clip(at + SMALL, 0, size + SMALL),), (SMALL,))
        tail = jnp.pad(tail, (0, -SMALL % D)).reshape(-1, D)
        small = sum_all(tail).reshape(-1)
        pieces = []
        offset = 0
        for length in (K * CONV, CONV, D, DI, H, H, H):
            pieces.append(small[offset : offset + length].astype(f32))
            offset += length
        conv_w, conv_b, norm_g, gate_g, a_log, dt_bias, skip_gain = pieces
        conv_w = conv_w.reshape(K, CONV)

        chunk = plan.pack(halfs, k)
        whole = gather_dp(chunk)
        n_in, n_out = plan.j_in, dp - plan.j_out
        w_in = whole[:n_in].reshape(n_in * rows, WIDE)
        w_out = [
            whole[plan.j_out :, :, b * D : (b + 1) * D].reshape(n_out * rows, D) for b in range(4)
        ]
        in_map = lax.dynamic_index_in_dim(jnp.asarray(plan.in_map.reshape(seq, -1)), s, 0, False)
        out_map = lax.dynamic_index_in_dim(
            jnp.asarray(plan.out_map.transpose(0, 2, 1, 3).reshape(seq, 4, -1)), s, 0, False
        )
        pick_in = (jnp.arange(D)[:, None] == in_map[None, :]).astype(bf16)
        pick_out = [(jnp.arange(DI)[:, None] == out_map[b][None, :]).astype(bf16) for b in range(4)]

        wide = tokens.astype(f32)
        scale = lax.rsqrt(jnp.mean(wide * wide, axis=-1, keepdims=True) + norm_eps)
        normed = (wide * scale * norm_g[None, :]).astype(bf16)
        normed_k = dot(normed, pick_in).astype(bf16)
        partial = dot(normed_k, w_in)

        x_part = scatter_seq(partial[:, DI : 2 * DI], 1)
        bcdt = sum_seq(partial[:, 2 * DI : PROJ])
        z_part = scatter_seq(partial[:, :DI], 1)
        gate_in = z_part.astype(bf16).astype(f32)
        x_pre = x_part.astype(bf16)
        bc_pre = bcdt[:, : 2 * N].astype(bf16)
        dt_raw = own_seq(bcdt[:, 2 * N :], 1).astype(bf16).astype(f32)
        hsize = DI // H
        dt_in = dt_raw + own_seq(dt_bias, 0)[None, :]
        step_size = jax.nn.softplus(dt_in)
        alog = own_seq(a_log, 0)[None, :]
        ssd_args = (
            x_pre,
            bc_pre,
            own_seq(conv_w[:, :DI], 1),
            own_seq(conv_b[:DI], 0)[None, :],
            conv_w[:, DI:],
            conv_b[None, DI:],
            step_size,
            step_size.T,
            alog,
            alog.T,
            jnp.repeat(own_seq(skip_gain, 0), hsize)[None, :],
        )
        ssd_out = ssd_forward(hsize, ssd_args)

        d_gated = None
        for b in range(4):
            piece = dot(cot, w_out[b], ((1,), (1,))).astype(bf16)
            piece = dot(piece, pick_out[b], ((1,), (1,)))
            d_gated = piece if d_gated is None else d_gated + piece
        d_gated = scatter_seq(d_gated, 1)

        gain = own_seq(gate_g, 0)[None, :]
        sig = jax.nn.sigmoid(gate_in)
        swish = gate_in * sig
        gated = ssd_out * swish
        weighted = d_gated * gain
        sums = jnp.stack([jnp.sum(gated * gated, axis=1), jnp.sum(weighted * gated, axis=1)])
        sums = sum_seq_wide(sums)
        g_scale = lax.rsqrt(sums[0] / DI + norm_eps)[:, None]
        cross = (sums[1] / DI)[:, None]
        gated_norm = (gated * g_scale * gain).astype(bf16)
        d_gate_g = jnp.sum(d_gated * gated * g_scale, axis=0)
        d_pre = g_scale * weighted - gated * g_scale**3 * cross
        d_ssd = d_pre * swish
        d_gate_in = d_pre * ssd_out * (sig + swish * (1.0 - sig))

        gn_full = gather_seq(gated_norm, 1)
        gn_k = [dot(gn_full, pick_out[b]).astype(bf16) for b in range(4)]
        y_part = None
        for b in range(4):
            piece = dot(gn_k[b], w_out[b])
            y_part = piece if y_part is None else y_part + piece
        y_own = scatter_seq(y_part, 0) + x_own.astype(f32)

        d_x, d_bcpre, d_dtraw, d_wx, d_bx, d_wb, d_bb, d_head, d_skip = ssd_backward(
            hsize, ssd_args + (jax.nn.sigmoid(dt_in), d_ssd)
        )
        d_alog, d_dtbias = d_head[0], d_head[1]
        d_skip = jnp.sum(d_skip.reshape(-1, hsize), axis=1)
        d_z_full = gather_seq(d_gate_in.astype(bf16), 1)
        d_x_full = gather_seq(d_x, 1)
        d_bc = sum_seq(d_bcpre).astype(bf16)
        d_dt_full = gather_seq(d_dtraw.astype(bf16), 1)
        pad = jnp.zeros((d_bc.shape[0], WIDE - PROJ), bf16)
        d_mixed = jnp.concatenate([d_z_full, d_x_full, d_bc, d_dt_full, pad], axis=1)

        g_in = dot(normed_k, d_mixed, ((0,), (0,))).astype(bf16).reshape(n_in, rows, WIDE)
        g_out = jnp.concatenate(
            [dot(gn_k[b], cot, ((0,), (0,))).astype(bf16).reshape(n_out, rows, D) for b in range(4)]
            + [jnp.zeros((n_out, rows, WIDE - 4 * D), bf16)],
            axis=2,
        )
        both = n_in + n_out - dp
        parts = jnp.concatenate(
            [g_in[: n_in - both], g_in[n_in - both :] + g_out[:both], g_out[both:]], axis=0
        )

        dn_k = dot(d_mixed, w_in, ((1,), (1,))).astype(bf16)
        d_normed = scatter_seq(dot(dn_k, pick_in, ((1,), (1,))), 0)
        wide_own = x_own.astype(f32)
        scale_own = lax.rsqrt(jnp.mean(wide_own * wide_own, axis=-1, keepdims=True) + norm_eps)
        a_own = d_normed * norm_g[None, :]
        d_norm_g = jnp.sum(d_normed * wide_own * scale_own, axis=0)
        d_wide = scale_own * a_own - wide_own * scale_own**3 * jnp.mean(
            a_own * wide_own, axis=-1, keepdims=True
        )
        input_grad = (cot_own.astype(f32) + d_wide).astype(bf16)

        def spread(a, width):
            full = jnp.zeros(a.shape[:-1] + (width,), f32)
            start = (0,) * (a.ndim - 1) + (s * a.shape[-1],)
            return lax.dynamic_update_slice(full, a, start)

        small_grad = jnp.concatenate(
            [
                jnp.concatenate([spread(d_wx, DI), d_wb], axis=1).reshape(-1),
                spread(d_bx[0], DI),
                d_bb[0],
                d_norm_g,
                spread(d_gate_g, DI),
                spread(d_alog, H),
                spread(d_dtbias, H),
                spread(d_skip, H),
            ]
        )
        small_grad = jnp.pad(small_grad, (0, -SMALL % D)).reshape(-1, D)
        small_grad = sum_all(small_grad).reshape(-1)[:SMALL]

        grad_chunk = scatter_dp(parts)
        shard = plan.unpack(grad_chunk, k)
        wing = jnp.pad(small_grad, (size, size))
        shard = shard + lax.dynamic_slice(
            wing, (jnp.clip(size - at, 0, size + SMALL),), (size,)
        )
        updated, first_new, second_new = adamw(params, shard, moment_one, moment_two)
        return (y_own.astype(bf16)[None], input_grad[None], shard, updated, first_new, second_new)

    return on_device


def matmul_cost(flops, size):
    return pl.CostEstimate(flops=flops, transcendentals=0, bytes_accessed=size)


def call(kernel, shapes, args, micros, **scratch):
    return pl.pallas_call(
        kernel,
        out_shape=[jax.ShapeDtypeStruct(a, b) for a, b in shapes],
        in_specs=vmem_specs(len(args)),
        out_specs=vmem_specs(len(shapes)),
        cost_estimate=matmul_cost(int(micros * 5e8), int(micros * 2e6)),
        **scratch,
    )(*args)


def front_kernel(depth, nk_ref, w_ref, own_ref, other_ref, rest_ref=None):
    half = own_ref.shape[1]
    nk = nk_ref[...]
    own_ref[...] = dot(nk, w_ref[:depth, :half])
    other_ref[...] = dot(nk, w_ref[:depth, half : 2 * half]).astype(bf16)
    if rest_ref is not None:
        rest_ref[...] = dot(nk, w_ref[:depth, 2 * half :]).astype(bf16)


def gate_grad_kernel(base, cot_ref, wb_ref, wa_ref, pick_ref, own_ref, other_ref):
    half = own_ref.shape[1]
    total = None
    for b in range(4):
        ref = wb_ref if b < 2 else wa_ref
        c = b % 2
        piece = dot(cot_ref[...], ref[base:, c * D : (c + 1) * D], ((1,), (1,))).astype(bf16)
        piece = dot(piece, pick_ref[b], ((1,), (1,)))
        total = piece if total is None else total + piece
    own_ref[...] = total[:, :half]
    other_ref[...] = total[:, half:].astype(bf16)


def pick_kernel(own_ref, other_ref, pick_ref, gk_ref):
    half = own_ref.shape[1]
    for b in range(4):
        gk = dot(own_ref[...], pick_ref[b, :half]) + dot(other_ref[...], pick_ref[b, half:])
        gk_ref[b] = gk.astype(bf16)


def out_kernel(base, gk_ref, wb_ref, wa_ref, y_ref):
    total = None
    for b in range(4):
        ref = wb_ref if b < 2 else wa_ref
        c = b % 2
        piece = dot(gk_ref[b], ref[base:, c * D : (c + 1) * D])
        total = piece if total is None else total + piece
    y_ref[...] = total


def weight_grad_kernel(depth, base, first, nk_ref, d_ref, gk_ref, cot_ref, *rest):
    out_ref = rest[-1]
    cols = out_ref.shape[1]
    nk = nk_ref[...]
    for n in range(0, cols, D):
        stop = min(n + D, cols)
        top = dot(nk, d_ref[:, n:stop], ((0,), (0,)))
        out_ref[:base, n:stop] = top[:base].astype(bf16)
        if n + D <= 2 * D:
            low = dot(gk_ref[first + n // D], cot_ref[...], ((0,), (0,)))
            out_ref[base:depth, n:stop] = (top[base:] + low[: depth - base]).astype(bf16)
            out_ref[depth:, n:stop] = low[depth - base :].astype(bf16)
        else:
            out_ref[base:depth, n:stop] = top[base:].astype(bf16)
            out_ref[depth:, n:stop] = jnp.zeros((out_ref.shape[0] - depth, stop - n), bf16)
    if len(rest) > 1:
        tile = rest[0][...]
        out_ref[out_ref.shape[0] - tile.shape[0] :, 2 * D :] = tile


def input_grad_kernel(depth, db_ref, da_ref, wb_ref, wa_ref, pick_ref, out_ref):
    dn = dot(db_ref[...], wb_ref[:depth], ((1,), (1,))) + dot(da_ref[...], wa_ref[:depth], ((1,), (1,)))
    out_ref[...] = dot(dn.astype(bf16), pick_ref[...], ((1,), (1,)))


def tie(value, token):
    return lax.optimization_barrier((value, token))[0]


def small_fits(dp, plan):
    start = (dp - 1) * plan.seq
    return plan.rows * (WIDE - 4 * D) >= SMALL and start > plan.mix and start * plan.flat <= IN + OUT


def make_pair(dp, flat):
    seq = 2
    plan = Plan(dp, seq, flat)
    rows = plan.rows
    za, yb, cc = factors(dp)
    inner = DI // seq
    hsize = DI // H
    side = WIDE - 4 * D
    n_in, n_out = plan.j_in, dp - plan.j_out
    depth, base = n_in * rows, plan.j_out * rows

    def place(z, y, c):
        return ((z % za) * yb + (y % yb)) * cc + (c % cc)

    def perm(dz, dy, dc):
        return [
            (place(z, y, c), place(z + dz, y + dy, c + dc))
            for z in range(za)
            for y in range(yb)
            for c in range(cc)
        ]

    z_next, y_next, c_next = perm(1, 0, 0), perm(0, 1, 0), perm(0, 0, 1)

    def position():
        j = lax.axis_index("dp")
        return j // (yb * cc), (j // cc) % yb, j % cc

    def index(z, y, c):
        return (((z + za) % za) * yb + (y + yb) % yb) * cc + c % cc

    def gather_dp(chunk):
        z, y, c = position()
        slots = []
        marks = []
        cur = chunk
        for r in range(za):
            if r:
                cur = lax.ppermute(cur, "dp", z_next)
                marks.append(cur)
            beside = cur
            for t in range(yb):
                if t:
                    beside = lax.ppermute(beside, "dp", y_next)
                if cc == 2:
                    slots.append((index(z - r, y - t, c + 1), lax.ppermute(beside, "dp", c_next)))
                slots.append((index(z - r, y - t, c), beside))
        whole = tie(jnp.zeros((dp,) + chunk.shape, chunk.dtype), marks[0])
        for at, data in slots:
            whole = lax.dynamic_update_index_in_dim(whole, data, at, 0)
        return whole.reshape(dp * rows, chunk.shape[1]), marks

    def scatter_dp(parts):
        parts = parts.reshape(za, yb, cc, rows, -1)
        z, y, c = position()

        def add(a, b):
            return (a.astype(f32) + b.astype(f32)).astype(bf16)

        total = lax.dynamic_index_in_dim(parts, c, 2, False)
        if cc == 2:
            give = lax.dynamic_index_in_dim(parts, (c + 1) % cc, 2, False)
            give = lax.ppermute(give, "dp", c_next)
            total = add(total, give)
        total = total.reshape(za * yb, rows, -1)

        def core_sum(zi, yi):
            return lax.dynamic_index_in_dim(total, ((zi + za) % za) * yb + (yi + yb) % yb, 0, False)

        def mid_sum(zi):
            acc = core_sum(zi, y - 1)
            for r in range(2, yb + 1):
                acc = lax.ppermute(acc, "dp", y_next)
                acc = add(acc, core_sum(zi, y - r))
            return acc

        acc = mid_sum(z - 1)
        marks = [acc]
        for r in range(2, za + 1):
            acc = add(lax.ppermute(acc, "dp", z_next), mid_sum(z - r))
            marks.append(acc)
        return acc, marks

    def swap(a):
        return lax.ppermute(a, "seq", [(0, 1), (1, 0)])

    def own_seq(a, axis):
        n = a.shape[axis] // seq
        return lax.dynamic_slice_in_dim(a, lax.axis_index("seq") * n, n, axis)

    def on_device(x_in, cotangent, params, moment_one, moment_two):
        s = lax.axis_index("seq")
        first = s == 0
        k = lax.axis_index("dp") * seq + s
        halfs = params.astype(bf16)

        def ordered(a, other):
            return jnp.concatenate([jnp.where(first, a, other), jnp.where(first, other, a)], axis=0)

        def flip(a, cut):
            return jnp.where(first, a, jnp.concatenate([a[:, cut:], a[:, :cut]], axis=1))

        at = IN + OUT - k * flat
        padded = jnp.pad(halfs, (SMALL, SMALL))
        tail = lax.dynamic_slice(padded, (jnp.clip(at + SMALL, 0, flat + SMALL),), (SMALL,))
        tail = jnp.pad(tail, (0, rows * side - SMALL)).reshape(rows, side)
        tail = tail + swap(tail)

        chunk = plan.pack(halfs, k)
        input_rows = k <= plan.mix
        part_b = jnp.where(input_rows, flip(chunk[:, :DI], inner), chunk[:, :DI])
        mid = chunk[:, DI : 2 * DI]
        part_a = jnp.concatenate(
            [
                jnp.where(input_rows, flip(mid, inner), mid),
                jnp.where(input_rows, chunk[:, 4 * D :], tail),
            ],
            axis=1,
        )
        if plan.mix_out:
            keep = (k == plan.mix) & (jnp.arange(rows) >= plan.mix_in)[:, None]
            part_b = jnp.where(keep, chunk[:, :DI], part_b)
            part_a = jnp.where(keep, chunk[:, DI:], part_a)
        w_a, marks = gather_dp(part_a)
        part_b = tie(part_b, marks[-1])
        late = marks[1 % len(marks)]

        x_own = x_in[0]
        cot_own = cotangent[0]
        tokens = ordered(x_own, tie(swap(x_own), late))
        cot = ordered(cot_own, tie(swap(cot_own), late))
        count = tokens.shape[0]

        in_map = lax.dynamic_index_in_dim(jnp.asarray(plan.in_map.reshape(seq, -1)), tie(s, late), 0, False)
        turned = plan.out_map.copy()
        turned[1] = np.where(turned[1] >= 0, (turned[1] + inner) % DI, -1)
        out_map = lax.dynamic_index_in_dim(
            jnp.asarray(turned.transpose(0, 2, 1, 3).reshape(seq, 4, -1)), tie(s, late), 0, False
        )
        pick_in = (jnp.arange(D)[:, None] == in_map[None, :]).astype(bf16)
        pick_out = (jnp.arange(DI)[None, :, None] == out_map[:, None, :]).astype(bf16)

        small = w_a[(dp - 1) * rows :, 2 * D :].reshape(-1)
        pieces = []
        offset = 0
        for length in (K * CONV, CONV, D, DI, H, H, H):
            pieces.append(small[offset : offset + length].astype(f32))
            offset += length
        conv_w, conv_b, norm_g, gate_g, a_log, dt_bias, skip_gain = pieces
        conv_w = conv_w.reshape(K, CONV)

        wide = tokens.astype(f32)
        scale = lax.rsqrt(jnp.mean(wide * wide, axis=-1, keepdims=True) + norm_eps)
        normed = (wide * scale * norm_g[None, :]).astype(bf16)
        normed_k = dot(normed, pick_in).astype(bf16)

        x_own_part, x_other, bcdt = call(
            functools.partial(front_kernel, depth),
            [((count, inner), f32), ((count, inner), bf16), ((count, side), bf16)],
            (normed_k, w_a),
            4.0,
        )
        w_b, marks = gather_dp(part_b)
        bcdt = bcdt.astype(f32) + tie(swap(bcdt), marks[-1]).astype(f32)
        x_pre = (x_own_part + swap(x_other).astype(f32)).astype(bf16)
        bc_pre = bcdt[:, : 2 * N].astype(bf16)
        dt_raw = own_seq(bcdt[:, 2 * N : 2 * N + H], 1).astype(bf16).astype(f32)
        dt_in = dt_raw + own_seq(dt_bias, 0)[None, :]
        step_size = jax.nn.softplus(dt_in)
        alog = own_seq(a_log, 0)[None, :]
        ssd_args = (
            x_pre,
            bc_pre,
            own_seq(conv_w[:, :DI], 1),
            own_seq(conv_b[:DI], 0)[None, :],
            conv_w[:, DI:],
            conv_b[None, DI:],
            step_size,
            step_size.T,
            alog,
            alog.T,
            jnp.repeat(own_seq(skip_gain, 0), hsize)[None, :],
        )
        ssd_out = ssd_forward(hsize, ssd_args)

        z_own_part, z_other = call(
            functools.partial(front_kernel, depth),
            [((count, inner), f32), ((count, inner), bf16)],
            (normed_k, w_b),
            3.0,
        )
        gate_in = (z_own_part + swap(z_other).astype(f32)).astype(bf16).astype(f32)
        dg_own, dg_other = call(
            functools.partial(gate_grad_kernel, base),
            [((count, inner), f32), ((count, inner), bf16)],
            (cot, w_b, w_a, pick_out),
            6.0,
        )
        d_gated = dg_own + swap(dg_other).astype(f32)

        gain = own_seq(gate_g, 0)[None, :]
        sig = jax.nn.sigmoid(gate_in)
        swish = gate_in * sig
        gated = ssd_out * swish
        weighted = d_gated * gain
        sums = jnp.stack([jnp.sum(gated * gated, axis=1), jnp.sum(weighted * gated, axis=1)])
        sums = sums + swap(sums)
        g_scale = lax.rsqrt(sums[0] / DI + norm_eps)[:, None]
        cross = (sums[1] / DI)[:, None]
        gn_own = (gated * g_scale * gain).astype(bf16)
        d_gate_g = jnp.sum(d_gated * gated * g_scale, axis=0)
        d_pre = g_scale * weighted - gated * g_scale**3 * cross
        d_ssd = d_pre * swish
        dz_own = (d_pre * ssd_out * (sig + swish * (1.0 - sig))).astype(bf16)
        gn_own, dz_own, d_ssd = lax.optimization_barrier((gn_own, dz_own, d_ssd))
        gn_other = swap(gn_own)
        dz_other = swap(dz_own)

        d_x, d_bcpre, d_dtraw, d_wx, d_bx, d_wb, d_bb, d_head, d_skip = ssd_backward(
            hsize, ssd_args + (jax.nn.sigmoid(dt_in), d_ssd)
        )
        d_alog, d_dtbias = d_head[0], d_head[1]
        d_skip = jnp.sum(d_skip.reshape(-1, hsize), axis=1)

        gn_k = call(
            pick_kernel, [((4, count, n_out * rows), bf16)], (gn_own, gn_other, pick_out), 3.0
        )[0]
        d_b = jnp.concatenate([dz_own, dz_other], axis=1)
        parts_b = call(
            functools.partial(weight_grad_kernel, depth, base, 0),
            [((dp * rows, DI), bf16)],
            (normed_k, d_b, gn_k, cot),
            5.0,
        )[0]
        grad_b, _ = scatter_dp(parts_b)

        bcdt_own = jnp.concatenate([d_bcpre, d_dtraw], axis=1).astype(bf16)
        dx_other, bcdt_other = swap(d_x), swap(bcdt_own)
        dx_other, bcdt_other, _ = lax.optimization_barrier((dx_other, bcdt_other, parts_b))
        d_bc = (bcdt_own[:, : 2 * N].astype(f32) + bcdt_other[:, : 2 * N].astype(f32)).astype(bf16)
        dt_pair = jnp.where(
            first,
            jnp.concatenate([bcdt_own[:, 2 * N :], bcdt_other[:, 2 * N :]], axis=1),
            jnp.concatenate([bcdt_other[:, 2 * N :], bcdt_own[:, 2 * N :]], axis=1),
        )
        blank = jnp.zeros((count, WIDE - PROJ), bf16)
        d_a = jnp.concatenate([d_x, dx_other, d_bc, dt_pair, blank], axis=1)
        d_normed = call(
            functools.partial(input_grad_kernel, depth),
            [((count, D), f32)],
            (d_b, d_a, w_b, w_a, pick_in),
            5.0,
        )[0]

        d_norm_g = jnp.sum(d_normed * wide * scale, axis=0)

        def spread(a, width):
            full = jnp.zeros(a.shape[:-1] + (width,), f32)
            start = (0,) * (a.ndim - 1) + (s * a.shape[-1],)
            return lax.dynamic_update_slice(full, a, start)

        small_grad = jnp.concatenate(
            [
                jnp.concatenate([spread(d_wx, DI), d_wb], axis=1).reshape(-1),
                spread(d_bx[0], DI),
                d_bb[0],
                d_norm_g,
                spread(d_gate_g, DI),
                spread(d_alog, H),
                spread(d_dtbias, H),
                spread(d_skip, H),
            ]
        )
        small_grad = jnp.pad(small_grad, (0, rows * side - SMALL)).reshape(rows, side)
        small_grad = (small_grad + swap(small_grad)).astype(bf16)

        parts_a = call(
            functools.partial(weight_grad_kernel, depth, base, 2),
            [((dp * rows, 2 * D + side), bf16)],
            (normed_k, d_a, gn_k, cot, small_grad),
            5.0,
        )[0]
        grad_a, _ = scatter_dp(parts_a)

        y_part = call(
            functools.partial(out_kernel, base),
            [((count, D), f32)],
            (tie(gn_k, parts_a), w_b, w_a),
            4.0,
        )[0]

        def own_tokens(a):
            half = count // 2
            low, high = a[:half], a[half:]
            got = swap(jnp.where(first, high, low).astype(bf16))
            return jnp.where(first, low, high) + got.astype(f32)

        d_own = own_tokens(d_normed)
        y_own = own_tokens(y_part) + x_own.astype(f32)
        wide_own = x_own.astype(f32)
        scale_own = lax.rsqrt(jnp.mean(wide_own * wide_own, axis=-1, keepdims=True) + norm_eps)
        a_own = d_own * norm_g[None, :]
        d_wide = scale_own * a_own - wide_own * scale_own**3 * jnp.mean(
            a_own * wide_own, axis=-1, keepdims=True
        )
        input_grad = (cot_own.astype(f32) + d_wide).astype(bf16)

        def unflip(a, cut):
            keep = k > plan.mix
            if plan.mix_out:
                keep = keep | ((k == plan.mix) & (jnp.arange(rows) >= plan.mix_in)[:, None])
            return jnp.where(keep, a, flip(a, cut))

        grad_a, grad_b = grad_a.astype(f32), grad_b.astype(f32)
        grad_chunk = jnp.concatenate(
            [unflip(grad_b, inner), unflip(grad_a[:, : 2 * D], inner), grad_a[:, 2 * D :]], axis=1
        )
        shard = plan.unpack(grad_chunk, k)
        region = jnp.where(k >= (dp - 1) * seq, grad_a[:, 2 * D :], 0.0)
        wing = jnp.pad(region.reshape(-1)[:SMALL], (flat, flat))
        shard = shard + lax.dynamic_slice(wing, (jnp.clip(flat - at, 0, flat + SMALL),), (flat,))
        updated, first_new, second_new = adamw(params, shard, moment_one, moment_two)
        return (y_own.astype(bf16)[None], input_grad[None], shard, updated, first_new, second_new)

    return on_device


def make(dp, seq):
    def on_device(x_in, cotangent, params, moment_one, moment_two):
        flat = params.shape[0]
        if seq == 2 and small_fits(dp, Plan(dp, seq, flat)):
            return make_pair(dp, flat)(x_in, cotangent, params, moment_one, moment_two)
        return make_general(dp, seq)(x_in, cotangent, params, moment_one, moment_two)

    return on_device


def solution(mesh):
    return jax.shard_map(
        make(mesh.shape["dp"], mesh.shape["seq"]),
        mesh=mesh,
        in_specs=(
            P("dp", "seq", None),
            P("dp", "seq", None),
            P(("dp", "seq")),
            P(("dp", "seq")),
            P(("dp", "seq")),
        ),
        out_specs=(
            P("dp", "seq", None),
            P("dp", "seq", None),
            P(("dp", "seq")),
            P(("dp", "seq")),
            P(("dp", "seq")),
            P(("dp", "seq")),
        ),
        check_vma=False,
    )
```

```python
import functools
import jax
import jax.numpy as jnp
import numpy as np
from jax import lax
from jax.experimental import pallas as pl
from jax.experimental.pallas import tpu as pltpu
from jax.sharding import PartitionSpec as P

D = 1024
DI = 2048
N = 128
K = 4
SPAN = 128
H = 32
CONV = 2304
PROJ = 4384
WIDE = 4480
IN = D * PROJ
OUT = DI * D
SMALL = K * CONV + CONV + D + DI + 3 * H

norm_eps = 1e-05
learn_rate = 0.005
beta_one = 0.9
beta_two = 0.95
adam_eps = 1e-08
weight_decay = 0.1
adam_step = 10

bf16 = jnp.bfloat16
f32 = jnp.float32


def ceil_to(value, unit):
    return -(-value // unit) * unit


def factors(count):
    core = 2 if count % 2 == 0 else 1
    rest = count // core
    mid = 1
    while rest % (mid * 2) == 0 and (mid * 2) ** 2 <= rest * 1:
        mid *= 2
    return rest // mid, mid, core


def dot(a, b, dims=((1,), (0,))):
    return lax.dot_general(a, b, (dims, ((), ())), preferred_element_type=f32)


def col_roll(a, steps):
    rows = a.shape[0]
    at = lax.broadcasted_iota(jnp.int32, a.shape, 0)
    if steps >= 0:
        return jnp.where(at >= steps, pltpu.roll(a, steps, 0), 0.0)
    return jnp.where(at < rows + steps, pltpu.roll(a, rows + steps, 0), 0.0)


def conv_act(x, taps, bias):
    acc = bias + taps[K - 1 : K] * x
    for k in range(1, K):
        acc = acc + taps[K - 1 - k : K - k] * col_roll(x, k)
    sig = 1.0 / (1.0 + jnp.exp(-acc))
    return acc, sig


def conv_back(x, taps, d_acc):
    d_x = taps[K - 1 : K] * d_acc
    d_taps = [jnp.sum(d_acc * x, axis=0, keepdims=True)]
    for k in range(1, K):
        d_x = d_x + taps[K - 1 - k : K - k] * col_roll(d_acc, -k)
        d_taps.insert(0, jnp.sum(d_acc * col_roll(x, k), axis=0, keepdims=True))
    return d_x, d_taps, jnp.sum(d_acc, axis=0, keepdims=True)


def fine(a, b, dims):
    return lax.dot_general(
        a, b, (dims, ((), ())), precision=lax.Precision.HIGHEST, preferred_element_type=f32
    )


def tri_parts():
    row = lax.broadcasted_iota(jnp.int32, (SPAN, SPAN), 0)
    col = lax.broadcasted_iota(jnp.int32, (SPAN, SPAN), 1)
    return row >= col, row == col


def rates(c, step_ref, turn_ref, alog_ref, alog_turn_ref, lower):
    span = slice(c * SPAN, (c + 1) * SPAN)
    rate = step_ref[span, :] * -jnp.exp(alog_ref[...])
    rate_turn = turn_ref[:, span] * -jnp.exp(alog_turn_ref[...])
    within = fine(lower, rate, ((1,), (0,)))
    within_turn = fine(rate_turn, lower, ((1,), (1,)))
    return rate, within, within_turn


def lanes_of(pair, first, second):
    lane = lax.broadcasted_iota(jnp.int32, (1, 2 * pair), 1)
    return jnp.where(lane < pair, first, second)


def ssd_forward_kernel(
    hsize, x_ref, bc_ref, wx_ref, bx_ref, wb_ref, bb_ref, step_ref, turn_ref, alog_ref, alog_turn_ref, skip_ref, out_ref
):
    rows, inner = x_ref.shape
    blocks = rows // SPAN
    causal, _ = tri_parts()
    lower = causal.astype(f32)
    acc, sig = conv_act(bc_ref[...].astype(f32), wb_ref[...], bb_ref[...])
    bc = (acc * sig).astype(bf16)
    b_blk = [bc[c * SPAN : (c + 1) * SPAN, :N] for c in range(blocks)]
    c_blk = [bc[c * SPAN : (c + 1) * SPAN, N:] for c in range(blocks)]
    cross = [dot(c_blk[c], b_blk[c], ((1,), (1,))) for c in range(blocks)]
    rated = [rates(c, step_ref, turn_ref, alog_ref, alog_turn_ref, lower) for c in range(blocks)]
    width = 2 * hsize
    lane = lax.broadcasted_iota(jnp.int32, (1, width), 1)
    masks = [(lane < hsize).astype(f32), (lane >= hsize).astype(f32)]
    for g in range(inner // width):
        cols = slice(g * width, (g + 1) * width)
        acc, sig = conv_act(x_ref[:, cols].astype(f32), wx_ref[:, cols], bx_ref[:, cols])
        vals = acc * sig
        state = None
        for c in range(blocks):
            span = slice(c * SPAN, (c + 1) * SPAN)
            _, within, within_turn = rated[c]
            v = vals[span]
            mix, split = [], []
            for i in range(2):
                h = 2 * g + i
                gap = within[:, h : h + 1] - within_turn[h : h + 1, :]
                mix.append(
                    (jnp.exp(jnp.where(causal, gap, -10000.0)) * cross[c] * turn_ref[h : h + 1, span]).astype(bf16)
                )
                split.append((v * masks[i]).astype(bf16))
            out = dot(jnp.concatenate(mix, axis=1), jnp.concatenate(split, axis=0))
            w0, w1 = within[:, 2 * g : 2 * g + 1], within[:, 2 * g + 1 : 2 * g + 2]
            if state is not None:
                out = out + lanes_of(hsize, jnp.exp(w0), jnp.exp(w1)) * dot(c_blk[c], state.astype(bf16))
            out_ref[span, cols] = out + skip_ref[:, cols] * v
            if c < blocks - 1:
                e0, e1 = w0[SPAN - 1 :], w1[SPAN - 1 :]
                tail = lanes_of(
                    hsize,
                    jnp.exp(e0 - w0) * step_ref[span, 2 * g : 2 * g + 1],
                    jnp.exp(e1 - w1) * step_ref[span, 2 * g + 1 : 2 * g + 2],
                )
                fresh = dot(b_blk[c], (tail * v).astype(bf16), ((0,), (0,)))
                if state is not None:
                    fresh = fresh + lanes_of(hsize, jnp.exp(e0), jnp.exp(e1)) * state
                state = fresh


def ssd_backward_kernel(
    hsize, x_ref, bc_ref, wx_ref, bx_ref, wb_ref, bb_ref, step_ref, turn_ref, alog_ref, alog_turn_ref, skip_ref,
    slope_ref, dy_ref, dx_ref, dbc_ref, ddt_ref, dwx_ref, dbx_ref, dwb_ref, dbb_ref, dhead_ref, dskip_ref,
    dcross_ref, dbmat_ref, dcmat_ref, col_ref, scol_ref, row_ref, srow_ref,
):
    rows, inner = x_ref.shape
    heads = step_ref.shape[1]
    blocks = rows // SPAN
    causal, eye = tri_parts()
    lower = causal.astype(f32)
    eye = eye.astype(f32)
    bc_in = bc_ref[...].astype(f32)
    bc_acc, bc_sig = conv_act(bc_in, wb_ref[...], bb_ref[...])
    bc = (bc_acc * bc_sig).astype(bf16)
    b_blk = [bc[c * SPAN : (c + 1) * SPAN, :N] for c in range(blocks)]
    c_blk = [bc[c * SPAN : (c + 1) * SPAN, N:] for c in range(blocks)]
    cross = [dot(c_blk[c], b_blk[c], ((1,), (1,))) for c in range(blocks)]
    rated = [rates(c, step_ref, turn_ref, alog_ref, alog_turn_ref, lower) for c in range(blocks)]
    for ref in (dcross_ref, dbmat_ref, dcmat_ref, col_ref, scol_ref, row_ref, srow_ref):
        ref[...] = jnp.zeros_like(ref)
    width = 2 * hsize
    lane = lax.broadcasted_iota(jnp.int32, (1, width), 1)
    masks = [(lane < hsize).astype(f32), (lane >= hsize).astype(f32)]
    head_lane = lax.broadcasted_iota(jnp.int32, (1, heads), 1)
    head_row = lax.broadcasted_iota(jnp.int32, (heads, 1), 0)
    last_row = lax.broadcasted_iota(jnp.int32, (SPAN, 1), 0) == SPAN - 1
    for g in range(inner // width):
        cols = slice(g * width, (g + 1) * width)
        x = x_ref[:, cols].astype(f32)
        acc, sig = conv_act(x, wx_ref[:, cols], bx_ref[:, cols])
        vals = acc * sig
        states, tails, decays = [None], [], []
        for c in range(blocks):
            span = slice(c * SPAN, (c + 1) * SPAN)
            within = rated[c][1]
            w0, w1 = within[:, 2 * g : 2 * g + 1], within[:, 2 * g + 1 : 2 * g + 2]
            e0, e1 = w0[SPAN - 1 :], w1[SPAN - 1 :]
            if c < blocks - 1:
                tails.append(
                    lanes_of(
                        hsize,
                        jnp.exp(e0 - w0) * step_ref[span, 2 * g : 2 * g + 1],
                        jnp.exp(e1 - w1) * step_ref[span, 2 * g + 1 : 2 * g + 2],
                    )
                )
                decays.append(lanes_of(hsize, jnp.exp(e0), jnp.exp(e1)))
                fresh = dot(b_blk[c], (tails[c] * vals[span]).astype(bf16), ((0,), (0,)))
                if states[c] is not None:
                    fresh = fresh + decays[c] * states[c]
                states.append(fresh)
        d_state = None
        d_vals = [None] * blocks
        d_skip = jnp.zeros((1, width), f32)
        for c in reversed(range(blocks)):
            span = slice(c * SPAN, (c + 1) * SPAN)
            _, within, within_turn = rated[c]
            v = vals[span]
            v_low = v.astype(bf16)
            dy = dy_ref[span, cols].astype(f32)
            ws = [within[:, 2 * g + i : 2 * g + i + 1] for i in range(2)]
            mix, split, d_w = [], [], []
            d_cross = None
            for i in range(2):
                h = 2 * g + i
                turn = turn_ref[h : h + 1, span]
                decay = jnp.exp(jnp.where(causal, ws[i] - within_turn[h : h + 1, :], -10000.0))
                scored = decay * cross[c]
                mix.append((scored * turn).astype(bf16))
                d_half = (dy * masks[i]).astype(bf16)
                split.append(d_half)
                d_mix = dot(d_half, v_low, ((1,), (1,)))
                raw = d_mix * scored
                part = d_mix * decay * turn
                d_cross = part if d_cross is None else d_cross + part
                d_w.append(jnp.sum(raw * turn, axis=1, keepdims=True))
                raw_sum = jnp.sum(raw, axis=0, keepdims=True)
                row_ref[c] += jnp.where(head_row == h, -raw_sum * turn, 0.0)
                srow_ref[c] += jnp.where(head_row == h, raw_sum, 0.0)
            dcross_ref[c] += d_cross
            d_v = dot(jnp.concatenate(mix, axis=0), jnp.concatenate(split, axis=0), ((0,), (0,)))
            d_v = d_v + skip_ref[:, cols] * dy
            d_skip = d_skip + jnp.sum(dy * v, axis=0, keepdims=True)
            d_enter = None
            if states[c] is not None:
                st = states[c].astype(bf16)
                lifted = lanes_of(hsize, jnp.exp(ws[0]), jnp.exp(ws[1])) * dy
                lift_low = lifted.astype(bf16)
                dcmat_ref[span] += dot(lift_low, st, ((1,), (1,)))
                d_enter = dot(c_blk[c], lift_low, ((0,), (0,)))
                prod = lifted * dot(c_blk[c], st)
                for i in range(2):
                    d_w[i] = d_w[i] + jnp.sum(prod * masks[i], axis=1, keepdims=True)
            if d_state is not None:
                ds_low = d_state.astype(bf16)
                back = dot(b_blk[c], ds_low)
                d_v = d_v + tails[c] * back
                dbmat_ref[span] += dot((tails[c] * v).astype(bf16), ds_low, ((1,), (1,)))
                along = v * back
                if states[c] is not None:
                    held = decays[c] * d_state * states[c]
                for i in range(2):
                    h = 2 * g + i
                    d_tail = jnp.sum(along * masks[i], axis=1, keepdims=True)
                    reach = jnp.exp(ws[i][SPAN - 1 :] - ws[i])
                    scol_ref[c] += jnp.where(head_lane == h, d_tail * reach, 0.0)
                    fall = d_tail * reach * step_ref[span, h : h + 1]
                    d_end = jnp.sum(fall, axis=0, keepdims=True)
                    if states[c] is not None:
                        d_end = d_end + jnp.sum(
                            jnp.sum(held * masks[i], axis=1, keepdims=True), axis=0, keepdims=True
                        )
                    d_w[i] = d_w[i] - fall + jnp.where(last_row, d_end, 0.0)
                if d_enter is not None:
                    d_enter = d_enter + decays[c] * d_state
            for i in range(2):
                col_ref[c] += jnp.where(head_lane == 2 * g + i, d_w[i], 0.0)
            d_state = d_enter
            d_vals[c] = d_v
        d_acc = jnp.concatenate(d_vals, axis=0) * (sig + vals * (1.0 - sig))
        d_x, d_taps, d_bias = conv_back(x, wx_ref[:, cols], d_acc)
        dx_ref[:, cols] = d_x.astype(bf16)
        for k in range(K):
            dwx_ref[k : k + 1, cols] = d_taps[k]
        dbx_ref[:, cols] = d_bias
        dskip_ref[:, cols] = d_skip
    d_alog = jnp.zeros((1, heads), f32)
    d_dtb = jnp.zeros((1, heads), f32)
    for c in range(blocks):
        span = slice(c * SPAN, (c + 1) * SPAN)
        d_w = col_ref[c] + fine(eye, row_ref[c], ((1,), (1,)))
        d_step = scol_ref[c] + fine(eye, srow_ref[c], ((1,), (1,)))
        d_rate = fine(lower, d_w, ((0,), (0,)))
        d_alog = d_alog + jnp.sum(rated[c][0] * d_rate, axis=0, keepdims=True)
        d_dt = (d_step - jnp.exp(alog_ref[...]) * d_rate) * slope_ref[span, :]
        ddt_ref[span, :] = d_dt
        d_dtb = d_dtb + jnp.sum(d_dt, axis=0, keepdims=True)
        low = dcross_ref[c].astype(bf16)
        dcmat_ref[span] += dot(low, b_blk[c])
        dbmat_ref[span] += dot(low, c_blk[c], ((0,), (0,)))
    dhead_ref[0:1, :] = d_alog
    dhead_ref[1:2, :] = d_dtb
    d_bc = jnp.concatenate([dbmat_ref[...], dcmat_ref[...]], axis=1)
    d_acc = d_bc * (bc_sig + bc_acc * bc_sig * (1.0 - bc_sig))
    d_x, d_taps, d_bias = conv_back(bc_in, wb_ref[...], d_acc)
    dbc_ref[...] = d_x
    for k in range(K):
        dwb_ref[k : k + 1, :] = d_taps[k]
    dbb_ref[...] = d_bias


def vmem_specs(count):
    return [pl.BlockSpec(memory_space=pltpu.VMEM)] * count


def ssd_forward(hsize, args):
    return pl.pallas_call(
        functools.partial(ssd_forward_kernel, hsize),
        out_shape=jax.ShapeDtypeStruct(args[0].shape, f32),
        in_specs=vmem_specs(len(args)),
        out_specs=vmem_specs(1)[0],
        cost_estimate=pl.CostEstimate(flops=int(2.5e9), transcendentals=0, bytes_accessed=int(1e7)),
        name="ssd_forward",
    )(*args)


def ssd_backward(hsize, args):
    rows, inner = args[0].shape
    heads = args[6].shape[1]
    blocks = rows // SPAN
    shapes = [
        ((rows, inner), bf16),
        ((rows, 2 * N), f32),
        ((rows, heads), f32),
        ((K, inner), f32),
        ((1, inner), f32),
        ((K, 2 * N), f32),
        ((1, 2 * N), f32),
        ((2, heads), f32),
        ((1, inner), f32),
    ]
    return pl.pallas_call(
        functools.partial(ssd_backward_kernel, hsize),
        out_shape=[jax.ShapeDtypeStruct(a, b) for a, b in shapes],
        in_specs=vmem_specs(len(args)),
        out_specs=vmem_specs(len(shapes)),
        scratch_shapes=[
            pltpu.VMEM((blocks, SPAN, SPAN), f32),
            pltpu.VMEM((rows, N), f32),
            pltpu.VMEM((rows, N), f32),
            pltpu.VMEM((blocks, SPAN, heads), f32),
            pltpu.VMEM((blocks, SPAN, heads), f32),
            pltpu.VMEM((blocks, heads, SPAN), f32),
            pltpu.VMEM((blocks, heads, SPAN), f32),
        ],
        cost_estimate=pl.CostEstimate(flops=int(6e9), transcendentals=0, bytes_accessed=int(2.4e7)),
        name="ssd_backward",
    )(*args)


def adamw(param_vec, grad_vec, first, second):
    first_new = beta_one * first + (1.0 - beta_one) * grad_vec
    second_new = beta_two * second + (1.0 - beta_two) * grad_vec * grad_vec
    first_hat = first_new / (1.0 - beta_one**adam_step)
    second_hat = second_new / (1.0 - beta_two**adam_step)
    updated = param_vec - learn_rate * (
        first_hat / (jnp.sqrt(second_hat) + adam_eps) + weight_decay * param_vec
    )
    return (updated, first_new, second_new)


class Plan:
    def __init__(self, dp, seq, flat):
        self.dp, self.seq, self.flat = dp, seq, flat
        self.total = dp * seq
        count = self.total
        self.mix = IN // flat
        last_in = -(-IN // flat)
        rows_in = max(
            -(-(((k * flat) % PROJ) + min(flat, IN - k * flat)) // PROJ) for k in range(last_in)
        )
        rows_out = max(
            -(-(((k * flat - IN) % D) + flat) // D) for k in range(self.mix, count)
        )
        self.rows = ceil_to(max(rows_in, -(-rows_out // 4)), 8)
        self.in_len = IN - self.mix * flat
        self.mix_in = -(-(((self.mix * flat) % PROJ) + self.in_len) // PROJ)
        self.mix_out = -(-(flat - self.in_len) // D)
        self.mix_free = self.rows - self.mix_in
        assert 4 * self.mix_free >= self.mix_out
        rows = self.rows
        self.j_in = self.mix // seq + 1
        self.j_out = self.mix // seq
        n_in, n_out = self.j_in, dp - self.j_out
        self.in_map = np.full((seq, n_in, rows), -1, np.int32)
        self.out_map = np.full((seq, n_out, 4, rows), -1, np.int32)
        m = np.arange(rows)
        for s in range(seq):
            for j in range(n_in):
                k = j * seq + s
                if k > self.mix:
                    continue
                first = (k * flat) // PROJ
                used = min(rows, D - first)
                if k == self.mix:
                    used = self.mix_in
                self.in_map[s, j, :used] = first + m[:used]
            for j in range(n_out):
                k = (j + self.j_out) * seq + s
                if k < self.mix:
                    continue
                for b in range(4):
                    if k == self.mix:
                        q = b * self.mix_free + (m - self.mix_in)
                        ok = (m >= self.mix_in) & (q < self.mix_out)
                    else:
                        q = (k * flat - IN) // D + b * rows + m
                        ok = q < min(DI, -(-((k + 1) * flat - IN) // D))
                    self.out_map[s, j, b] = np.where(ok, q, -1)

    def windows(self):
        rows, seq = self.rows, self.seq
        table = np.zeros((seq, self.dp - self.j_out, 4, 3), np.int32)
        for s in range(seq):
            for j in range(self.dp - self.j_out):
                k = (j + self.j_out) * seq + s
                for b in range(4):
                    if k < self.mix:
                        continue
                    if k == self.mix:
                        start = b * self.mix_free - self.mix_in
                        low = self.mix_in
                        high = min(rows, low + max(0, self.mix_out - b * self.mix_free))
                    else:
                        start = (k * self.flat - IN) // D + b * rows
                        low = 0
                        stop = min(DI, -(-((k + 1) * self.flat - IN) // D))
                        high = min(rows, max(0, stop - start))
                    table[s, j, b] = ((start + s * (DI // seq)) % DI, low, high)
        return table.reshape(seq, -1)

    def pack(self, flat, k):
        rows, size = self.rows, self.flat
        shift = (k * size) % PROJ
        span = rows * PROJ
        buf = jnp.pad(flat, (PROJ, span - size))
        win = lax.dynamic_slice(buf, (PROJ - shift,), (span,)).reshape(rows, PROJ)
        win = jnp.pad(win, ((0, 0), (0, WIDE - PROJ)))
        off = (k * size - IN) % D
        span = 4 * rows * D
        buf = jnp.pad(flat, (D, span - size))
        out = lax.dynamic_slice(buf, (D - off,), (span,)).reshape(4, rows, D)
        out = jnp.concatenate([out[b] for b in range(4)] + [jnp.zeros((rows, WIDE - 4 * D), flat.dtype)], axis=1)
        head = flat[self.in_len :]
        free = self.mix_free
        head = jnp.pad(head, (0, 4 * free * D - head.shape[0])).reshape(4, free, D)
        low = jnp.concatenate([head[b] for b in range(4)] + [jnp.zeros((free, WIDE - 4 * D), flat.dtype)], axis=1)
        mixed = jnp.concatenate([win[: self.mix_in], low], axis=0)
        return jnp.where(k < self.mix, win, jnp.where(k > self.mix, out, mixed))

    def unpack(self, chunk, k):
        rows, size = self.rows, self.flat
        shift = (k * size) % PROJ
        line = chunk[:, :PROJ].reshape(-1)
        line = jnp.pad(line, (0, max(0, PROJ + size - rows * PROJ)))
        win = lax.dynamic_slice(line, (shift,), (size,))
        off = (k * size - IN) % D
        line = jnp.concatenate([chunk[:, b * D : (b + 1) * D] for b in range(4)], axis=0).reshape(-1)
        line = jnp.pad(line, (0, max(0, D + size - 4 * rows * D)))
        out = lax.dynamic_slice(line, (off,), (size,))
        low = chunk[self.mix_in :]
        low = jnp.concatenate([low[:, b * D : (b + 1) * D] for b in range(4)], axis=0)
        mixed = jnp.concatenate([win[: self.in_len], low.reshape(-1)[: size - self.in_len]])
        return jnp.where(k < self.mix, win, jnp.where(k > self.mix, out, mixed))


def make_general(dp, seq):
    za, yb, cc = factors(dp)

    def place(z, y, c):
        return ((z % za) * yb + (y % yb)) * cc + (c % cc)

    def perm(dz, dy, dc):
        return [
            (place(z, y, c), place(z + dz, y + dy, c + dc))
            for z in range(za)
            for y in range(yb)
            for c in range(cc)
        ]

    z_next, y_next, c_next = perm(1, 0, 0), perm(0, 1, 0), perm(0, 0, 1)

    def gather_dp(chunk):
        j = lax.axis_index("dp")
        z, y, c = j // (yb * cc), (j // cc) % yb, j % cc
        whole = jnp.zeros((dp,) + chunk.shape, chunk.dtype)
        slots = []
        cur = chunk
        for r in range(za):
            if r:
                cur = lax.ppermute(cur, "dp", z_next)
            side = cur
            for t in range(yb):
                if t:
                    side = lax.ppermute(side, "dp", y_next)
                slots.append((z - r, y - t, c, side))
                if cc == 2:
                    slots.append((z - r, y - t, c + 1, lax.ppermute(side, "dp", c_next)))
        for zi, yi, ci, data in slots:
            at = (((zi + za) % za) * yb + (yi + yb) % yb) * cc + ci % cc
            whole = lax.dynamic_update_index_in_dim(whole, data, at, 0)
        return whole

    def scatter_dp(parts):
        j = lax.axis_index("dp")
        z, y, c = j // (yb * cc), (j // cc) % yb, j % cc

        def pick(zi, yi, ci):
            at = (((zi + za) % za) * yb + (yi + yb) % yb) * cc + ci % cc
            return lax.dynamic_index_in_dim(parts, at, 0, False)

        def core_sum(zi, yi):
            own = pick(zi, yi, c)
            if cc == 2:
                got = lax.ppermute(pick(zi, yi, c + 1), "dp", c_next)
                own = (own.astype(f32) + got.astype(f32)).astype(bf16)
            return own

        def mid_sum(zi):
            acc = None
            for r in range(1, yb + 1):
                mine = core_sum(zi, y - r)
                if acc is not None:
                    acc = (acc.astype(f32) + mine.astype(f32)).astype(bf16)
                else:
                    acc = mine
                if r < yb:
                    acc = lax.ppermute(acc, "dp", y_next)
            return acc

        acc = None
        for r in range(1, za + 1):
            mine = mid_sum(z - r)
            if acc is not None:
                acc = acc.astype(f32) + mine.astype(f32)
            else:
                acc = mine
            if r < za:
                acc = lax.ppermute(acc.astype(bf16), "dp", z_next)
        return acc.astype(f32)

    def swap_seq(a):
        return lax.ppermute(a, "seq", [(0, 1), (1, 0)])

    def halves(a, axis):
        n = a.shape[axis] // 2
        return lax.slice_in_dim(a, 0, n, axis=axis), lax.slice_in_dim(a, n, 2 * n, axis=axis)

    def gather_seq(a, axis):
        if seq != 2:
            return lax.all_gather(a, "seq", axis=axis, tiled=True)
        first = lax.axis_index("seq") == 0
        other = swap_seq(a)
        return jnp.concatenate([jnp.where(first, a, other), jnp.where(first, other, a)], axis=axis)

    def scatter_seq(a, axis):
        if seq != 2:
            return lax.psum_scatter(a, "seq", scatter_dimension=axis, tiled=True)
        first = lax.axis_index("seq") == 0
        low, high = halves(a, axis)
        got = swap_seq(jnp.where(first, high, low).astype(bf16))
        return jnp.where(first, low, high) + got.astype(f32)

    def sum_seq(a):
        if seq != 2:
            return lax.psum(a, "seq")
        a = a.astype(bf16)
        return a.astype(f32) + swap_seq(a).astype(f32)

    def sum_seq_wide(a):
        if seq != 2:
            return lax.psum(a, "seq")
        return a + swap_seq(a)

    def own_seq(a, axis):
        n = a.shape[axis] // seq
        return lax.dynamic_slice_in_dim(a, lax.axis_index("seq") * n, n, axis)

    def sum_all(a):
        for axis, count in (("seq", seq), ("dp", dp)):
            step = 1
            while step < count:
                a = a + lax.ppermute(a, axis, [(i, i ^ step) for i in range(count)])
                step *= 2
        return a

    def on_device(x_in, cotangent, params, moment_one, moment_two):
        size = params.shape[0]
        plan = Plan(dp, seq, size)
        rows = plan.rows
        s = lax.axis_index("seq")
        k = lax.axis_index("dp") * seq + s
        halfs = params.astype(bf16)

        x_own = x_in[0]
        cot_own = cotangent[0]
        tokens = gather_seq(x_own, 0)
        cot = gather_seq(cot_own, 0)

        base = IN + OUT
        at = base - k * size
        padded = jnp.pad(halfs, (SMALL, SMALL))
        tail = lax.dynamic_slice(padded, (jnp.clip(at + SMALL, 0, size + SMALL),), (SMALL,))
        tail = jnp.pad(tail, (0, -SMALL % D)).reshape(-1, D)
        small = sum_all(tail).reshape(-1)
        pieces = []
        offset = 0
        for length in (K * CONV, CONV, D, DI, H, H, H):
            pieces.append(small[offset : offset + length].astype(f32))
            offset += length
        conv_w, conv_b, norm_g, gate_g, a_log, dt_bias, skip_gain = pieces
        conv_w = conv_w.reshape(K, CONV)

        chunk = plan.pack(halfs, k)
        whole = gather_dp(chunk)
        n_in, n_out = plan.j_in, dp - plan.j_out
        w_in = whole[:n_in].reshape(n_in * rows, WIDE)
        w_out = [
            whole[plan.j_out :, :, b * D : (b + 1) * D].reshape(n_out * rows, D) for b in range(4)
        ]
        in_map = lax.dynamic_index_in_dim(jnp.asarray(plan.in_map.reshape(seq, -1)), s, 0, False)
        out_map = lax.dynamic_index_in_dim(
            jnp.asarray(plan.out_map.transpose(0, 2, 1, 3).reshape(seq, 4, -1)), s, 0, False
        )
        pick_in = (jnp.arange(D)[:, None] == in_map[None, :]).astype(bf16)
        pick_out = [(jnp.arange(DI)[:, None] == out_map[b][None, :]).astype(bf16) for b in range(4)]

        wide = tokens.astype(f32)
        scale = lax.rsqrt(jnp.mean(wide * wide, axis=-1, keepdims=True) + norm_eps)
        normed = (wide * scale * norm_g[None, :]).astype(bf16)
        normed_k = dot(normed, pick_in).astype(bf16)
        partial = dot(normed_k, w_in)

        x_part = scatter_seq(partial[:, DI : 2 * DI], 1)
        bcdt = sum_seq(partial[:, 2 * DI : PROJ])
        z_part = scatter_seq(partial[:, :DI], 1)
        gate_in = z_part.astype(bf16).astype(f32)
        x_pre = x_part.astype(bf16)
        bc_pre = bcdt[:, : 2 * N].astype(bf16)
        dt_raw = own_seq(bcdt[:, 2 * N :], 1).astype(bf16).astype(f32)
        hsize = DI // H
        dt_in = dt_raw + own_seq(dt_bias, 0)[None, :]
        step_size = jax.nn.softplus(dt_in)
        alog = own_seq(a_log, 0)[None, :]
        ssd_args = (
            x_pre,
            bc_pre,
            own_seq(conv_w[:, :DI], 1),
            own_seq(conv_b[:DI], 0)[None, :],
            conv_w[:, DI:],
            conv_b[None, DI:],
            step_size,
            step_size.T,
            alog,
            alog.T,
            jnp.repeat(own_seq(skip_gain, 0), hsize)[None, :],
        )
        ssd_out = ssd_forward(hsize, ssd_args)

        d_gated = None
        for b in range(4):
            piece = dot(cot, w_out[b], ((1,), (1,))).astype(bf16)
            piece = dot(piece, pick_out[b], ((1,), (1,)))
            d_gated = piece if d_gated is None else d_gated + piece
        d_gated = scatter_seq(d_gated, 1)

        gain = own_seq(gate_g, 0)[None, :]
        sig = jax.nn.sigmoid(gate_in)
        swish = gate_in * sig
        gated = ssd_out * swish
        weighted = d_gated * gain
        sums = jnp.stack([jnp.sum(gated * gated, axis=1), jnp.sum(weighted * gated, axis=1)])
        sums = sum_seq_wide(sums)
        g_scale = lax.rsqrt(sums[0] / DI + norm_eps)[:, None]
        cross = (sums[1] / DI)[:, None]
        gated_norm = (gated * g_scale * gain).astype(bf16)
        d_gate_g = jnp.sum(d_gated * gated * g_scale, axis=0)
        d_pre = g_scale * weighted - gated * g_scale**3 * cross
        d_ssd = d_pre * swish
        d_gate_in = d_pre * ssd_out * (sig + swish * (1.0 - sig))

        gn_full = gather_seq(gated_norm, 1)
        gn_k = [dot(gn_full, pick_out[b]).astype(bf16) for b in range(4)]
        y_part = None
        for b in range(4):
            piece = dot(gn_k[b], w_out[b])
            y_part = piece if y_part is None else y_part + piece
        y_own = scatter_seq(y_part, 0) + x_own.astype(f32)

        d_x, d_bcpre, d_dtraw, d_wx, d_bx, d_wb, d_bb, d_head, d_skip = ssd_backward(
            hsize, ssd_args + (jax.nn.sigmoid(dt_in), d_ssd)
        )
        d_alog, d_dtbias = d_head[0], d_head[1]
        d_skip = jnp.sum(d_skip.reshape(-1, hsize), axis=1)
        d_z_full = gather_seq(d_gate_in.astype(bf16), 1)
        d_x_full = gather_seq(d_x, 1)
        d_bc = sum_seq(d_bcpre).astype(bf16)
        d_dt_full = gather_seq(d_dtraw.astype(bf16), 1)
        pad = jnp.zeros((d_bc.shape[0], WIDE - PROJ), bf16)
        d_mixed = jnp.concatenate([d_z_full, d_x_full, d_bc, d_dt_full, pad], axis=1)

        g_in = dot(normed_k, d_mixed, ((0,), (0,))).astype(bf16).reshape(n_in, rows, WIDE)
        g_out = jnp.concatenate(
            [dot(gn_k[b], cot, ((0,), (0,))).astype(bf16).reshape(n_out, rows, D) for b in range(4)]
            + [jnp.zeros((n_out, rows, WIDE - 4 * D), bf16)],
            axis=2,
        )
        both = n_in + n_out - dp
        parts = jnp.concatenate(
            [g_in[: n_in - both], g_in[n_in - both :] + g_out[:both], g_out[both:]], axis=0
        )

        dn_k = dot(d_mixed, w_in, ((1,), (1,))).astype(bf16)
        d_normed = scatter_seq(dot(dn_k, pick_in, ((1,), (1,))), 0)
        wide_own = x_own.astype(f32)
        scale_own = lax.rsqrt(jnp.mean(wide_own * wide_own, axis=-1, keepdims=True) + norm_eps)
        a_own = d_normed * norm_g[None, :]
        d_norm_g = jnp.sum(d_normed * wide_own * scale_own, axis=0)
        d_wide = scale_own * a_own - wide_own * scale_own**3 * jnp.mean(
            a_own * wide_own, axis=-1, keepdims=True
        )
        input_grad = (cot_own.astype(f32) + d_wide).astype(bf16)

        def spread(a, width):
            full = jnp.zeros(a.shape[:-1] + (width,), f32)
            start = (0,) * (a.ndim - 1) + (s * a.shape[-1],)
            return lax.dynamic_update_slice(full, a, start)

        small_grad = jnp.concatenate(
            [
                jnp.concatenate([spread(d_wx, DI), d_wb], axis=1).reshape(-1),
                spread(d_bx[0], DI),
                d_bb[0],
                d_norm_g,
                spread(d_gate_g, DI),
                spread(d_alog, H),
                spread(d_dtbias, H),
                spread(d_skip, H),
            ]
        )
        small_grad = jnp.pad(small_grad, (0, -SMALL % D)).reshape(-1, D)
        small_grad = sum_all(small_grad).reshape(-1)[:SMALL]

        grad_chunk = scatter_dp(parts)
        shard = plan.unpack(grad_chunk, k)
        wing = jnp.pad(small_grad, (size, size))
        shard = shard + lax.dynamic_slice(
            wing, (jnp.clip(size - at, 0, size + SMALL),), (size,)
        )
        updated, first_new, second_new = adamw(params, shard, moment_one, moment_two)
        return (y_own.astype(bf16)[None], input_grad[None], shard, updated, first_new, second_new)

    return on_device


def matmul_cost(flops, size):
    return pl.CostEstimate(flops=flops, transcendentals=0, bytes_accessed=size)


def call(kernel, shapes, args, micros, scratch=(), tables=0, raw=0):
    specs = [pl.BlockSpec(memory_space=pltpu.SMEM)] * tables
    specs += [pl.BlockSpec(memory_space=pl.ANY)] * raw
    specs += vmem_specs(len(args) - tables - raw)
    return pl.pallas_call(
        kernel,
        out_shape=[jax.ShapeDtypeStruct(a, b) for a, b in shapes],
        in_specs=specs,
        out_specs=vmem_specs(len(shapes)),
        scratch_shapes=list(scratch),
        cost_estimate=matmul_cost(int(micros * 5e8), int(micros * 2e6)),
    )(*args)


def front_kernel(depth, slots, rows, at_ref, *refs):
    parts, nk_ref, w_ref, own_ref, other_ref = refs[:slots], *refs[slots : slots + 4]
    sems = refs[-1]
    copies = []
    for i, part in enumerate(parts):
        start = pl.multiple_of(at_ref[i] * rows, 8)
        copies.append(pltpu.make_async_copy(part, w_ref.at[pl.ds(start, rows), :], sems.at[i]))
    for copy in copies:
        copy.start()
    for copy in copies:
        copy.wait()
    half = own_ref.shape[1]
    nk = nk_ref[...]
    own_ref[...] = dot(nk, w_ref[:depth, :half])
    other_ref[...] = dot(nk, w_ref[:depth, half : 2 * half]).astype(bf16)
    if len(refs) > slots + 5:
        refs[slots + 4][...] = dot(nk, w_ref[:depth, 2 * half :]).astype(bf16)


def window_mask(rows, low, high):
    at = lax.broadcasted_iota(jnp.int32, (rows, 1), 0)
    return (at >= low) & (at < high)


def gate_grad_kernel(base, rows, tab_ref, wb_ref, wa_ref, cot_ref, own_ref, other_ref, buf_ref, acc_ref, sems):
    half = own_ref.shape[1]
    count = buf_ref.shape[1]
    copies = []
    for b in range(4):
        ref = wb_ref if b < 2 else wa_ref
        c = b % 2
        copies.append(
            pltpu.make_async_copy(
                ref.at[pl.ds(base, count), pl.ds(c * D, D)], buf_ref.at[b], sems.at[b]
            )
        )
    for copy in copies:
        copy.start()
    acc_ref[...] = jnp.zeros_like(acc_ref)
    for b in range(4):
        copies[b].wait()
        piece = dot(buf_ref[b], cot_ref[...], ((1,), (1,)))
        for j in range(count // rows):
            n = (j * 4 + b) * 3
            keep = window_mask(rows, tab_ref[n + 1], tab_ref[n + 2])
            part = jnp.where(keep, piece[j * rows : (j + 1) * rows], 0.0)
            part = jnp.concatenate([part, jnp.zeros((8, part.shape[1]), f32)], axis=0)
            start = tab_ref[n]
            near = pl.multiple_of((start // 8) * 8, 8)
            acc_ref[pl.ds(near, rows + 8), :] += pltpu.roll(part, start - near, 0)
    acc_ref[: rows + 8] += acc_ref[DI : DI + rows + 8]
    own_ref[...] = acc_ref[:half].T
    other_ref[...] = acc_ref[half : 2 * half].T.astype(bf16)


def pick_kernel(rows, tab_ref, own_ref, other_ref, gk_ref, turn_ref):
    half = own_ref.shape[1]
    turn_ref[:half] = own_ref[...].astype(f32).T
    turn_ref[half : 2 * half] = other_ref[...].astype(f32).T
    turn_ref[DI : DI + rows + 8] = turn_ref[: rows + 8]
    for b in range(4):
        for j in range(gk_ref.shape[1] // rows):
            n = (j * 4 + b) * 3
            keep = window_mask(rows, tab_ref[n + 1], tab_ref[n + 2])
            start = tab_ref[n]
            near = pl.multiple_of((start // 8) * 8, 8)
            part = pltpu.roll(turn_ref[pl.ds(near, rows + 8), :], (rows + 8 - (start - near)) % (rows + 8), 0)
            part = jnp.where(keep, part[:rows], 0.0)
            gk_ref[b, j * rows : (j + 1) * rows, :] = part.astype(bf16)


def out_kernel(base, wb_ref, wa_ref, gk_ref, y_ref, buf_ref, sems):
    count = buf_ref.shape[1]
    copies = []
    for b in range(4):
        ref = wb_ref if b < 2 else wa_ref
        c = b % 2
        copies.append(
            pltpu.make_async_copy(
                ref.at[pl.ds(base, count), pl.ds(c * D, D)], buf_ref.at[b], sems.at[b]
            )
        )
    for copy in copies:
        copy.start()
    total = None
    for b in range(4):
        copies[b].wait()
        piece = dot(gk_ref[b], buf_ref[b], ((0,), (0,)))
        total = piece if total is None else total + piece
    y_ref[...] = total


def weight_grad_kernel(depth, base, first, nk_ref, d_ref, gk_ref, cot_ref, out_ref):
    cols = out_ref.shape[1]
    nk = nk_ref[...]
    for n in range(0, cols, D):
        stop = min(n + D, cols)
        top = dot(nk, d_ref[:, n:stop], ((0,), (0,)))
        out_ref[:base, n:stop] = top[:base].astype(bf16)
        if n + D <= 2 * D:
            low = dot(gk_ref[first + n // D], cot_ref[...])
            out_ref[base:depth, n:stop] = (top[base:] + low[: depth - base]).astype(bf16)
            out_ref[depth:, n:stop] = low[depth - base :].astype(bf16)
        else:
            out_ref[base:depth, n:stop] = top[base:].astype(bf16)
            out_ref[depth:, n:stop] = jnp.zeros((out_ref.shape[0] - depth, stop - n), bf16)


def input_grad_kernel(depth, db_ref, da_ref, wb_ref, wa_ref, pick_ref, out_ref):
    dn = dot(db_ref[...], wb_ref[:depth], ((1,), (1,))) + dot(da_ref[...], wa_ref[:depth], ((1,), (1,)))
    out_ref[...] = dot(dn.astype(bf16), pick_ref[...], ((1,), (1,)))


def tie(value, token):
    return lax.optimization_barrier((value, token))[0]


def small_fits(dp, plan):
    start = (dp - 1) * plan.seq
    return plan.rows * (WIDE - 4 * D) >= SMALL and start > plan.mix and start * plan.flat <= IN + OUT


def make_pair(dp, flat):
    seq = 2
    plan = Plan(dp, seq, flat)
    rows = plan.rows
    za, yb, cc = factors(dp)
    inner = DI // seq
    hsize = DI // H
    side = WIDE - 4 * D
    n_in, n_out = plan.j_in, dp - plan.j_out
    depth, base = n_in * rows, plan.j_out * rows

    def place(z, y, c):
        return ((z % za) * yb + (y % yb)) * cc + (c % cc)

    def perm(dz, dy, dc):
        return [
            (place(z, y, c), place(z + dz, y + dy, c + dc))
            for z in range(za)
            for y in range(yb)
            for c in range(cc)
        ]

    z_next, y_next, c_next = perm(1, 0, 0), perm(0, 1, 0), perm(0, 0, 1)

    def position():
        j = lax.axis_index("dp")
        return j // (yb * cc), (j // cc) % yb, j % cc

    def index(z, y, c):
        return (((z + za) % za) * yb + (y + yb) % yb) * cc + c % cc

    def gather_dp(chunk):
        z, y, c = position()
        slots = []
        marks = []
        cur = chunk
        for r in range(za):
            if r:
                cur = lax.ppermute(cur, "dp", z_next)
                marks.append(cur)
            beside = cur
            for t in range(yb):
                if t:
                    beside = lax.ppermute(beside, "dp", y_next)
                if cc == 2:
                    slots.append((index(z - r, y - t, c + 1), lax.ppermute(beside, "dp", c_next)))
                slots.append((index(z - r, y - t, c), beside))
        return jnp.stack([at for at, _ in slots]).astype(jnp.int32), [data for _, data in slots], marks

    def scatter_dp(parts):
        parts = parts.reshape(za, yb, cc, rows, -1)
        z, y, c = position()

        def add(a, b):
            return (a.astype(f32) + b.astype(f32)).astype(bf16)

        total = lax.dynamic_index_in_dim(parts, c, 2, False)
        if cc == 2:
            give = lax.dynamic_index_in_dim(parts, (c + 1) % cc, 2, False)
            give = lax.ppermute(give, "dp", c_next)
            total = add(total, give)
        total = total.reshape(za * yb, rows, -1)

        def core_sum(zi, yi):
            return lax.dynamic_index_in_dim(total, ((zi + za) % za) * yb + (yi + yb) % yb, 0, False)

        def mid_sum(zi):
            acc = core_sum(zi, y - 1)
            for r in range(2, yb + 1):
                acc = lax.ppermute(acc, "dp", y_next)
                acc = add(acc, core_sum(zi, y - r))
            return acc

        acc = mid_sum(z - 1)
        marks = [acc]
        for r in range(2, za + 1):
            acc = add(lax.ppermute(acc, "dp", z_next), mid_sum(z - r))
            marks.append(acc)
        return acc, marks

    def swap(a):
        return lax.ppermute(a, "seq", [(0, 1), (1, 0)])

    def sum_all(a, marks):
        a = a + swap(a)
        steps = []
        step = 1
        while step < dp:
            steps.append(step)
            step *= 2
        steps = steps[:1] + steps[2:] + steps[1:2]
        for n, step in enumerate(steps):
            got = lax.ppermute(a, "dp", [(i, i ^ step) for i in range(dp)])
            if n:
                got = tie(got, marks[min(n - 1, len(marks) - 1)])
            a = a + got
        return a

    def own_seq(a, axis):
        n = a.shape[axis] // seq
        return lax.dynamic_slice_in_dim(a, lax.axis_index("seq") * n, n, axis)

    def on_device(x_in, cotangent, params, moment_one, moment_two):
        s = lax.axis_index("seq")
        first = s == 0
        k = lax.axis_index("dp") * seq + s
        halfs = params.astype(bf16)

        def ordered(a, other):
            return jnp.concatenate([jnp.where(first, a, other), jnp.where(first, other, a)], axis=0)

        def flip(a, cut):
            return jnp.where(first, a, jnp.concatenate([a[:, cut:], a[:, :cut]], axis=1))

        at = IN + OUT - k * flat
        padded = jnp.pad(halfs, (SMALL, SMALL))
        tail = lax.dynamic_slice(padded, (jnp.clip(at + SMALL, 0, flat + SMALL),), (SMALL,))
        tail = jnp.pad(tail, (0, rows * side - SMALL)).reshape(rows, side)
        tail = tail + swap(tail)

        chunk = plan.pack(halfs, k)
        input_rows = k <= plan.mix
        part_b = jnp.where(input_rows, flip(chunk[:, :DI], inner), chunk[:, :DI])
        mid = chunk[:, DI : 2 * DI]
        part_a = jnp.concatenate(
            [
                jnp.where(input_rows, flip(mid, inner), mid),
                jnp.where(input_rows, chunk[:, 4 * D :], tail),
            ],
            axis=1,
        )
        if plan.mix_out:
            keep = (k == plan.mix) & (jnp.arange(rows) >= plan.mix_in)[:, None]
            part_b = jnp.where(keep, chunk[:, :DI], part_b)
            part_a = jnp.where(keep, chunk[:, DI:], part_a)
        at_a, slots_a, marks = gather_dp(part_a)
        part_b = tie(part_b, marks[-1])
        late = marks[1 % len(marks)]

        x_own = x_in[0]
        cot_own = cotangent[0]
        tokens = ordered(x_own, tie(swap(x_own), late))
        cot = ordered(cot_own, tie(swap(cot_own), late))
        count = tokens.shape[0]

        in_map = lax.dynamic_index_in_dim(jnp.asarray(plan.in_map.reshape(seq, -1)), tie(s, late), 0, False)
        table = lax.dynamic_index_in_dim(jnp.asarray(plan.windows()), s, 0, False)
        pick_in = (jnp.arange(D)[:, None] == in_map[None, :]).astype(bf16)
        mine = at_a == dp - 1
        small = functools.reduce(
            jnp.add, [jnp.where(mine[i], a[:, 2 * D :], 0) for i, a in enumerate(slots_a)]
        ).reshape(-1)
        pieces = []
        offset = 0
        for length in (K * CONV, CONV, D, DI, H, H, H):
            pieces.append(small[offset : offset + length].astype(f32))
            offset += length
        conv_w, conv_b, norm_g, gate_g, a_log, dt_bias, skip_gain = pieces
        conv_w = conv_w.reshape(K, CONV)

        wide = tokens.astype(f32)
        scale = lax.rsqrt(jnp.mean(wide * wide, axis=-1, keepdims=True) + norm_eps)
        normed = (wide * scale * norm_g[None, :]).astype(bf16)
        normed_k = dot(normed, pick_in).astype(bf16)

        w_a, x_own_part, x_other, bcdt = call(
            functools.partial(front_kernel, depth, dp, rows),
            [
                ((dp * rows, 2 * D + side), bf16),
                ((count, inner), f32),
                ((count, inner), bf16),
                ((count, side), bf16),
            ],
            (at_a, *slots_a, normed_k),
            5.0,
            scratch=[pltpu.SemaphoreType.DMA((dp,))],
            tables=1,
            raw=dp,
        )
        at_b, slots_b, marks = gather_dp(part_b)
        bcdt = bcdt.astype(f32) + tie(swap(bcdt), marks[-1]).astype(f32)
        x_pre = (x_own_part + swap(x_other).astype(f32)).astype(bf16)
        bc_pre = bcdt[:, : 2 * N].astype(bf16)
        dt_raw = own_seq(bcdt[:, 2 * N : 2 * N + H], 1).astype(bf16).astype(f32)
        dt_in = dt_raw + own_seq(dt_bias, 0)[None, :]
        step_size = jax.nn.softplus(dt_in)
        alog = own_seq(a_log, 0)[None, :]
        ssd_args = (
            x_pre,
            bc_pre,
            own_seq(conv_w[:, :DI], 1),
            own_seq(conv_b[:DI], 0)[None, :],
            conv_w[:, DI:],
            conv_b[None, DI:],
            step_size,
            step_size.T,
            alog,
            alog.T,
            jnp.repeat(own_seq(skip_gain, 0), hsize)[None, :],
        )
        ssd_out = ssd_forward(hsize, ssd_args)

        w_b, z_own_part, z_other = call(
            functools.partial(front_kernel, depth, dp, rows),
            [((dp * rows, DI), bf16), ((count, inner), f32), ((count, inner), bf16)],
            (at_b, *slots_b, normed_k),
            5.0,
            scratch=[pltpu.SemaphoreType.DMA((dp,))],
            tables=1,
            raw=dp,
        )
        span = n_out * rows
        held = [pltpu.VMEM((4, span, D), bf16)]
        dg_own, dg_other = call(
            functools.partial(gate_grad_kernel, base, rows),
            [((count, inner), f32), ((count, inner), bf16)],
            (table, w_b, w_a, cot),
            5.0,
            scratch=held + [pltpu.VMEM((DI + rows + 8, count), f32), pltpu.SemaphoreType.DMA((4,))],
            tables=1,
            raw=2,
        )
        gate_in = (z_own_part + swap(z_other).astype(f32)).astype(bf16).astype(f32)
        d_gated = dg_own + swap(dg_other).astype(f32)

        gain = own_seq(gate_g, 0)[None, :]
        sig = jax.nn.sigmoid(gate_in)
        swish = gate_in * sig
        gated = ssd_out * swish
        weighted = d_gated * gain
        sums = jnp.stack([jnp.sum(gated * gated, axis=1), jnp.sum(weighted * gated, axis=1)])
        sums = sums + swap(sums)
        g_scale = lax.rsqrt(sums[0] / DI + norm_eps)[:, None]
        cross = (sums[1] / DI)[:, None]
        gn_own = (gated * g_scale * gain).astype(bf16)
        d_gate_g = jnp.sum(d_gated * gated * g_scale, axis=0)
        d_pre = g_scale * weighted - gated * g_scale**3 * cross
        d_ssd = d_pre * swish
        dz_own = (d_pre * ssd_out * (sig + swish * (1.0 - sig))).astype(bf16)
        gn_own, dz_own, d_ssd = lax.optimization_barrier((gn_own, dz_own, d_ssd))
        gn_other = swap(gn_own)
        dz_other = swap(dz_own)

        d_x, d_bcpre, d_dtraw, d_wx, d_bx, d_wb, d_bb, d_head, d_skip = ssd_backward(
            hsize, ssd_args + (jax.nn.sigmoid(dt_in), d_ssd)
        )
        d_alog, d_dtbias = d_head[0], d_head[1]
        d_skip = jnp.sum(d_skip.reshape(-1, hsize), axis=1)

        gn_k = call(
            functools.partial(pick_kernel, rows),
            [((4, span, count), bf16)],
            (table, gn_own, gn_other),
            3.0,
            scratch=[pltpu.VMEM((DI + rows + 8, count), f32)],
            tables=1,
        )[0]
        d_b = jnp.concatenate([dz_own, dz_other], axis=1)
        parts_b = call(
            functools.partial(weight_grad_kernel, depth, base, 0),
            [((dp * rows, DI), bf16)],
            (normed_k, d_b, gn_k, cot),
            5.0,
        )[0]
        grad_b, _ = scatter_dp(parts_b)

        bcdt_own = jnp.concatenate([d_bcpre, d_dtraw], axis=1).astype(bf16)
        dx_other, bcdt_other = swap(d_x), swap(bcdt_own)
        dx_other, bcdt_other, _ = lax.optimization_barrier((dx_other, bcdt_other, parts_b))
        d_bc = (bcdt_own[:, : 2 * N].astype(f32) + bcdt_other[:, : 2 * N].astype(f32)).astype(bf16)
        dt_pair = jnp.where(
            first,
            jnp.concatenate([bcdt_own[:, 2 * N :], bcdt_other[:, 2 * N :]], axis=1),
            jnp.concatenate([bcdt_other[:, 2 * N :], bcdt_own[:, 2 * N :]], axis=1),
        )
        blank = jnp.zeros((count, WIDE - PROJ), bf16)
        d_a = jnp.concatenate([d_x, dx_other, d_bc, dt_pair, blank], axis=1)
        parts_a = call(
            functools.partial(weight_grad_kernel, depth, base, 2),
            [((dp * rows, 2 * D + side), bf16)],
            (normed_k, d_a, gn_k, cot),
            5.0,
        )[0]
        grad_a, marks_a = scatter_dp(parts_a)

        d_normed = call(
            functools.partial(input_grad_kernel, depth),
            [((count, D), f32)],
            (d_b, tie(d_a, parts_a), w_b, w_a, pick_in),
            5.0,
        )[0]

        d_norm_g = jnp.sum(d_normed * wide * scale, axis=0)

        def spread(a, width):
            full = jnp.zeros(a.shape[:-1] + (width,), f32)
            start = (0,) * (a.ndim - 1) + (s * a.shape[-1],)
            return lax.dynamic_update_slice(full, a, start)

        small_grad = jnp.concatenate(
            [
                jnp.concatenate([spread(d_wx, DI), d_wb], axis=1).reshape(-1),
                spread(d_bx[0], DI),
                d_bb[0],
                d_norm_g,
                spread(d_gate_g, DI),
                spread(d_alog, H),
                spread(d_dtbias, H),
                spread(d_skip, H),
            ]
        )
        small_grad = jnp.pad(small_grad, (0, -SMALL % D)).reshape(-1, D)
        small_grad = sum_all(small_grad, marks_a).reshape(-1)[:SMALL]

        y_part = call(
            functools.partial(out_kernel, base),
            [((count, D), f32)],
            (w_b, w_a, tie(gn_k, d_normed)),
            4.0,
            scratch=held + [pltpu.SemaphoreType.DMA((4,))],
            raw=2,
        )[0]

        def own_tokens(a):
            half = count // 2
            low, high = a[:half], a[half:]
            got = swap(jnp.where(first, high, low).astype(bf16))
            return jnp.where(first, low, high) + got.astype(f32)

        d_own = own_tokens(d_normed)
        y_own = own_tokens(y_part) + x_own.astype(f32)
        wide_own = x_own.astype(f32)
        scale_own = lax.rsqrt(jnp.mean(wide_own * wide_own, axis=-1, keepdims=True) + norm_eps)
        a_own = d_own * norm_g[None, :]
        d_wide = scale_own * a_own - wide_own * scale_own**3 * jnp.mean(
            a_own * wide_own, axis=-1, keepdims=True
        )
        input_grad = (cot_own.astype(f32) + d_wide).astype(bf16)

        def unflip(a, cut):
            keep = k > plan.mix
            if plan.mix_out:
                keep = keep | ((k == plan.mix) & (jnp.arange(rows) >= plan.mix_in)[:, None])
            return jnp.where(keep, a, flip(a, cut))

        grad_a, grad_b = grad_a.astype(f32), grad_b.astype(f32)
        grad_chunk = jnp.concatenate(
            [unflip(grad_b, inner), unflip(grad_a[:, : 2 * D], inner), grad_a[:, 2 * D :]], axis=1
        )
        shard = plan.unpack(grad_chunk, k)
        wing = jnp.pad(small_grad, (flat, flat))
        shard = shard + lax.dynamic_slice(wing, (jnp.clip(flat - at, 0, flat + SMALL),), (flat,))
        updated, first_new, second_new = adamw(params, shard, moment_one, moment_two)
        return (y_own.astype(bf16)[None], input_grad[None], shard, updated, first_new, second_new)

    return on_device


def make(dp, seq):
    def on_device(x_in, cotangent, params, moment_one, moment_two):
        flat = params.shape[0]
        if seq == 2 and small_fits(dp, Plan(dp, seq, flat)):
            return make_pair(dp, flat)(x_in, cotangent, params, moment_one, moment_two)
        return make_general(dp, seq)(x_in, cotangent, params, moment_one, moment_two)

    return on_device


def solution(mesh):
    return jax.shard_map(
        make(mesh.shape["dp"], mesh.shape["seq"]),
        mesh=mesh,
        in_specs=(
            P("dp", "seq", None),
            P("dp", "seq", None),
            P(("dp", "seq")),
            P(("dp", "seq")),
            P(("dp", "seq")),
        ),
        out_specs=(
            P("dp", "seq", None),
            P("dp", "seq", None),
            P(("dp", "seq")),
            P(("dp", "seq")),
            P(("dp", "seq")),
            P(("dp", "seq")),
        ),
        check_vma=False,
    )
```

```python
import functools
import jax
import jax.numpy as jnp
import numpy as np
from jax import lax
from jax.experimental import pallas as pl
from jax.experimental.pallas import tpu as pltpu
from jax.sharding import PartitionSpec as P

D = 1024
DI = 2048
N = 128
K = 4
SPAN = 128
H = 32
CONV = 2304
PROJ = 4384
WIDE = 4480
IN = D * PROJ
OUT = DI * D
SMALL = K * CONV + CONV + D + DI + 3 * H

norm_eps = 1e-05
learn_rate = 0.005
beta_one = 0.9
beta_two = 0.95
adam_eps = 1e-08
weight_decay = 0.1
adam_step = 10

bf16 = jnp.bfloat16
f32 = jnp.float32


def ceil_to(value, unit):
    return -(-value // unit) * unit


def factors(count):
    core = 2 if count % 2 == 0 else 1
    rest = count // core
    mid = 1
    while rest % (mid * 2) == 0 and (mid * 2) ** 2 <= rest * 1:
        mid *= 2
    return rest // mid, mid, core


def dot(a, b, dims=((1,), (0,))):
    return lax.dot_general(a, b, (dims, ((), ())), preferred_element_type=f32)


def col_roll(a, steps):
    rows = a.shape[0]
    at = lax.broadcasted_iota(jnp.int32, a.shape, 0)
    if steps >= 0:
        return jnp.where(at >= steps, pltpu.roll(a, steps, 0), 0.0)
    return jnp.where(at < rows + steps, pltpu.roll(a, rows + steps, 0), 0.0)


def conv_act(x, taps, bias):
    acc = bias + taps[K - 1 : K] * x
    for k in range(1, K):
        acc = acc + taps[K - 1 - k : K - k] * col_roll(x, k)
    sig = 1.0 / (1.0 + jnp.exp(-acc))
    return acc, sig


def conv_back(x, taps, d_acc):
    d_x = taps[K - 1 : K] * d_acc
    d_taps = [jnp.sum(d_acc * x, axis=0, keepdims=True)]
    for k in range(1, K):
        d_x = d_x + taps[K - 1 - k : K - k] * col_roll(d_acc, -k)
        d_taps.insert(0, jnp.sum(d_acc * col_roll(x, k), axis=0, keepdims=True))
    return d_x, d_taps, jnp.sum(d_acc, axis=0, keepdims=True)


def fine(a, b, dims):
    return lax.dot_general(
        a, b, (dims, ((), ())), precision=lax.Precision.HIGHEST, preferred_element_type=f32
    )


def tri_parts():
    row = lax.broadcasted_iota(jnp.int32, (SPAN, SPAN), 0)
    col = lax.broadcasted_iota(jnp.int32, (SPAN, SPAN), 1)
    return row >= col, row == col


def rates(c, step_ref, turn_ref, alog_ref, alog_turn_ref, lower):
    span = slice(c * SPAN, (c + 1) * SPAN)
    rate = step_ref[span, :] * -jnp.exp(alog_ref[...])
    rate_turn = turn_ref[:, span] * -jnp.exp(alog_turn_ref[...])
    within = fine(lower, rate, ((1,), (0,)))
    within_turn = fine(rate_turn, lower, ((1,), (1,)))
    return rate, within, within_turn


def lanes_of(pair, first, second):
    lane = lax.broadcasted_iota(jnp.int32, (1, 2 * pair), 1)
    return jnp.where(lane < pair, first, second)


def ssd_forward_kernel(
    hsize, x_ref, bc_ref, wx_ref, bx_ref, wb_ref, bb_ref, step_ref, turn_ref, alog_ref, alog_turn_ref, skip_ref, out_ref
):
    rows, inner = x_ref.shape
    blocks = rows // SPAN
    causal, _ = tri_parts()
    lower = causal.astype(f32)
    acc, sig = conv_act(bc_ref[...].astype(f32), wb_ref[...], bb_ref[...])
    bc = (acc * sig).astype(bf16)
    b_blk = [bc[c * SPAN : (c + 1) * SPAN, :N] for c in range(blocks)]
    c_blk = [bc[c * SPAN : (c + 1) * SPAN, N:] for c in range(blocks)]
    cross = [dot(c_blk[c], b_blk[c], ((1,), (1,))) for c in range(blocks)]
    rated = [rates(c, step_ref, turn_ref, alog_ref, alog_turn_ref, lower) for c in range(blocks)]
    width = 2 * hsize
    lane = lax.broadcasted_iota(jnp.int32, (1, width), 1)
    masks = [(lane < hsize).astype(f32), (lane >= hsize).astype(f32)]
    for g in range(inner // width):
        cols = slice(g * width, (g + 1) * width)
        acc, sig = conv_act(x_ref[:, cols].astype(f32), wx_ref[:, cols], bx_ref[:, cols])
        vals = acc * sig
        state = None
        for c in range(blocks):
            span = slice(c * SPAN, (c + 1) * SPAN)
            _, within, within_turn = rated[c]
            v = vals[span]
            mix, split = [], []
            for i in range(2):
                h = 2 * g + i
                gap = within[:, h : h + 1] - within_turn[h : h + 1, :]
                mix.append(
                    (jnp.exp(jnp.where(causal, gap, -10000.0)) * cross[c] * turn_ref[h : h + 1, span]).astype(bf16)
                )
                split.append((v * masks[i]).astype(bf16))
            out = dot(jnp.concatenate(mix, axis=1), jnp.concatenate(split, axis=0))
            w0, w1 = within[:, 2 * g : 2 * g + 1], within[:, 2 * g + 1 : 2 * g + 2]
            if state is not None:
                out = out + lanes_of(hsize, jnp.exp(w0), jnp.exp(w1)) * dot(c_blk[c], state.astype(bf16))
            out_ref[span, cols] = out + skip_ref[:, cols] * v
            if c < blocks - 1:
                e0, e1 = w0[SPAN - 1 :], w1[SPAN - 1 :]
                tail = lanes_of(
                    hsize,
                    jnp.exp(e0 - w0) * step_ref[span, 2 * g : 2 * g + 1],
                    jnp.exp(e1 - w1) * step_ref[span, 2 * g + 1 : 2 * g + 2],
                )
                fresh = dot(b_blk[c], (tail * v).astype(bf16), ((0,), (0,)))
                if state is not None:
                    fresh = fresh + lanes_of(hsize, jnp.exp(e0), jnp.exp(e1)) * state
                state = fresh


def ssd_backward_kernel(
    hsize, x_ref, bc_ref, wx_ref, bx_ref, wb_ref, bb_ref, step_ref, turn_ref, alog_ref, alog_turn_ref, skip_ref,
    slope_ref, dy_ref, dx_ref, dbc_ref, ddt_ref, dwx_ref, dbx_ref, dwb_ref, dbb_ref, dhead_ref, dskip_ref,
    dcross_ref, dbmat_ref, dcmat_ref, col_ref, scol_ref, row_ref, srow_ref,
):
    rows, inner = x_ref.shape
    heads = step_ref.shape[1]
    blocks = rows // SPAN
    causal, eye = tri_parts()
    lower = causal.astype(f32)
    eye = eye.astype(f32)
    bc_in = bc_ref[...].astype(f32)
    bc_acc, bc_sig = conv_act(bc_in, wb_ref[...], bb_ref[...])
    bc = (bc_acc * bc_sig).astype(bf16)
    b_blk = [bc[c * SPAN : (c + 1) * SPAN, :N] for c in range(blocks)]
    c_blk = [bc[c * SPAN : (c + 1) * SPAN, N:] for c in range(blocks)]
    cross = [dot(c_blk[c], b_blk[c], ((1,), (1,))) for c in range(blocks)]
    rated = [rates(c, step_ref, turn_ref, alog_ref, alog_turn_ref, lower) for c in range(blocks)]
    for ref in (dcross_ref, dbmat_ref, dcmat_ref, col_ref, scol_ref, row_ref, srow_ref):
        ref[...] = jnp.zeros_like(ref)
    width = 2 * hsize
    lane = lax.broadcasted_iota(jnp.int32, (1, width), 1)
    masks = [(lane < hsize).astype(f32), (lane >= hsize).astype(f32)]
    head_lane = lax.broadcasted_iota(jnp.int32, (1, heads), 1)
    head_row = lax.broadcasted_iota(jnp.int32, (heads, 1), 0)
    last_row = lax.broadcasted_iota(jnp.int32, (SPAN, 1), 0) == SPAN - 1
    for g in range(inner // width):
        cols = slice(g * width, (g + 1) * width)
        x = x_ref[:, cols].astype(f32)
        acc, sig = conv_act(x, wx_ref[:, cols], bx_ref[:, cols])
        vals = acc * sig
        states, tails, decays = [None], [], []
        for c in range(blocks):
            span = slice(c * SPAN, (c + 1) * SPAN)
            within = rated[c][1]
            w0, w1 = within[:, 2 * g : 2 * g + 1], within[:, 2 * g + 1 : 2 * g + 2]
            e0, e1 = w0[SPAN - 1 :], w1[SPAN - 1 :]
            if c < blocks - 1:
                tails.append(
                    lanes_of(
                        hsize,
                        jnp.exp(e0 - w0) * step_ref[span, 2 * g : 2 * g + 1],
                        jnp.exp(e1 - w1) * step_ref[span, 2 * g + 1 : 2 * g + 2],
                    )
                )
                decays.append(lanes_of(hsize, jnp.exp(e0), jnp.exp(e1)))
                fresh = dot(b_blk[c], (tails[c] * vals[span]).astype(bf16), ((0,), (0,)))
                if states[c] is not None:
                    fresh = fresh + decays[c] * states[c]
                states.append(fresh)
        d_state = None
        d_vals = [None] * blocks
        d_skip = jnp.zeros((1, width), f32)
        for c in reversed(range(blocks)):
            span = slice(c * SPAN, (c + 1) * SPAN)
            _, within, within_turn = rated[c]
            v = vals[span]
            v_low = v.astype(bf16)
            dy = dy_ref[span, cols].astype(f32)
            ws = [within[:, 2 * g + i : 2 * g + i + 1] for i in range(2)]
            mix, split, d_w = [], [], []
            d_cross = None
            for i in range(2):
                h = 2 * g + i
                turn = turn_ref[h : h + 1, span]
                decay = jnp.exp(jnp.where(causal, ws[i] - within_turn[h : h + 1, :], -10000.0))
                scored = decay * cross[c]
                mix.append((scored * turn).astype(bf16))
                d_half = (dy * masks[i]).astype(bf16)
                split.append(d_half)
                d_mix = dot(d_half, v_low, ((1,), (1,)))
                raw = d_mix * scored
                part = d_mix * decay * turn
                d_cross = part if d_cross is None else d_cross + part
                d_w.append(jnp.sum(raw * turn, axis=1, keepdims=True))
                raw_sum = jnp.sum(raw, axis=0, keepdims=True)
                row_ref[c] += jnp.where(head_row == h, -raw_sum * turn, 0.0)
                srow_ref[c] += jnp.where(head_row == h, raw_sum, 0.0)
            dcross_ref[c] += d_cross
            d_v = dot(jnp.concatenate(mix, axis=0), jnp.concatenate(split, axis=0), ((0,), (0,)))
            d_v = d_v + skip_ref[:, cols] * dy
            d_skip = d_skip + jnp.sum(dy * v, axis=0, keepdims=True)
            d_enter = None
            if states[c] is not None:
                st = states[c].astype(bf16)
                lifted = lanes_of(hsize, jnp.exp(ws[0]), jnp.exp(ws[1])) * dy
                lift_low = lifted.astype(bf16)
                dcmat_ref[span] += dot(lift_low, st, ((1,), (1,)))
                d_enter = dot(c_blk[c], lift_low, ((0,), (0,)))
                prod = lifted * dot(c_blk[c], st)
                for i in range(2):
                    d_w[i] = d_w[i] + jnp.sum(prod * masks[i], axis=1, keepdims=True)
            if d_state is not None:
                ds_low = d_state.astype(bf16)
                back = dot(b_blk[c], ds_low)
                d_v = d_v + tails[c] * back
                dbmat_ref[span] += dot((tails[c] * v).astype(bf16), ds_low, ((1,), (1,)))
                along = v * back
                if states[c] is not None:
                    held = decays[c] * d_state * states[c]
                for i in range(2):
                    h = 2 * g + i
                    d_tail = jnp.sum(along * masks[i], axis=1, keepdims=True)
                    reach = jnp.exp(ws[i][SPAN - 1 :] - ws[i])
                    scol_ref[c] += jnp.where(head_lane == h, d_tail * reach, 0.0)
                    fall = d_tail * reach * step_ref[span, h : h + 1]
                    d_end = jnp.sum(fall, axis=0, keepdims=True)
                    if states[c] is not None:
                        d_end = d_end + jnp.sum(
                            jnp.sum(held * masks[i], axis=1, keepdims=True), axis=0, keepdims=True
                        )
                    d_w[i] = d_w[i] - fall + jnp.where(last_row, d_end, 0.0)
                if d_enter is not None:
                    d_enter = d_enter + decays[c] * d_state
            for i in range(2):
                col_ref[c] += jnp.where(head_lane == 2 * g + i, d_w[i], 0.0)
            d_state = d_enter
            d_vals[c] = d_v
        d_acc = jnp.concatenate(d_vals, axis=0) * (sig + vals * (1.0 - sig))
        d_x, d_taps, d_bias = conv_back(x, wx_ref[:, cols], d_acc)
        dx_ref[:, cols] = d_x.astype(bf16)
        for k in range(K):
            dwx_ref[k : k + 1, cols] = d_taps[k]
        dbx_ref[:, cols] = d_bias
        dskip_ref[:, cols] = d_skip
    d_alog = jnp.zeros((1, heads), f32)
    d_dtb = jnp.zeros((1, heads), f32)
    for c in range(blocks):
        span = slice(c * SPAN, (c + 1) * SPAN)
        d_w = col_ref[c] + fine(eye, row_ref[c], ((1,), (1,)))
        d_step = scol_ref[c] + fine(eye, srow_ref[c], ((1,), (1,)))
        d_rate = fine(lower, d_w, ((0,), (0,)))
        d_alog = d_alog + jnp.sum(rated[c][0] * d_rate, axis=0, keepdims=True)
        d_dt = (d_step - jnp.exp(alog_ref[...]) * d_rate) * slope_ref[span, :]
        ddt_ref[span, :] = d_dt
        d_dtb = d_dtb + jnp.sum(d_dt, axis=0, keepdims=True)
        low = dcross_ref[c].astype(bf16)
        dcmat_ref[span] += dot(low, b_blk[c])
        dbmat_ref[span] += dot(low, c_blk[c], ((0,), (0,)))
    dhead_ref[0:1, :] = d_alog
    dhead_ref[1:2, :] = d_dtb
    d_bc = jnp.concatenate([dbmat_ref[...], dcmat_ref[...]], axis=1)
    d_acc = d_bc * (bc_sig + bc_acc * bc_sig * (1.0 - bc_sig))
    d_x, d_taps, d_bias = conv_back(bc_in, wb_ref[...], d_acc)
    dbc_ref[...] = d_x
    for k in range(K):
        dwb_ref[k : k + 1, :] = d_taps[k]
    dbb_ref[...] = d_bias


def vmem_specs(count):
    return [pl.BlockSpec(memory_space=pltpu.VMEM)] * count


def ssd_forward(hsize, args):
    return pl.pallas_call(
        functools.partial(ssd_forward_kernel, hsize),
        out_shape=jax.ShapeDtypeStruct(args[0].shape, f32),
        in_specs=vmem_specs(len(args)),
        out_specs=vmem_specs(1)[0],
        cost_estimate=pl.CostEstimate(flops=int(2.5e9), transcendentals=0, bytes_accessed=int(1e7)),
        name="ssd_forward",
    )(*args)


def ssd_backward(hsize, args):
    rows, inner = args[0].shape
    heads = args[6].shape[1]
    blocks = rows // SPAN
    shapes = [
        ((rows, inner), bf16),
        ((rows, 2 * N), f32),
        ((rows, heads), f32),
        ((K, inner), f32),
        ((1, inner), f32),
        ((K, 2 * N), f32),
        ((1, 2 * N), f32),
        ((2, heads), f32),
        ((1, inner), f32),
    ]
    return pl.pallas_call(
        functools.partial(ssd_backward_kernel, hsize),
        out_shape=[jax.ShapeDtypeStruct(a, b) for a, b in shapes],
        in_specs=vmem_specs(len(args)),
        out_specs=vmem_specs(len(shapes)),
        scratch_shapes=[
            pltpu.VMEM((blocks, SPAN, SPAN), f32),
            pltpu.VMEM((rows, N), f32),
            pltpu.VMEM((rows, N), f32),
            pltpu.VMEM((blocks, SPAN, heads), f32),
            pltpu.VMEM((blocks, SPAN, heads), f32),
            pltpu.VMEM((blocks, heads, SPAN), f32),
            pltpu.VMEM((blocks, heads, SPAN), f32),
        ],
        cost_estimate=pl.CostEstimate(flops=int(6e9), transcendentals=0, bytes_accessed=int(2.4e7)),
        name="ssd_backward",
    )(*args)


def adamw(param_vec, grad_vec, first, second):
    first_new = beta_one * first + (1.0 - beta_one) * grad_vec
    second_new = beta_two * second + (1.0 - beta_two) * grad_vec * grad_vec
    first_hat = first_new / (1.0 - beta_one**adam_step)
    second_hat = second_new / (1.0 - beta_two**adam_step)
    updated = param_vec - learn_rate * (
        first_hat / (jnp.sqrt(second_hat) + adam_eps) + weight_decay * param_vec
    )
    return (updated, first_new, second_new)


class Plan:
    def __init__(self, dp, seq, flat):
        self.dp, self.seq, self.flat = dp, seq, flat
        self.total = dp * seq
        count = self.total
        self.mix = IN // flat
        last_in = -(-IN // flat)
        rows_in = max(
            -(-(((k * flat) % PROJ) + min(flat, IN - k * flat)) // PROJ) for k in range(last_in)
        )
        rows_out = max(
            -(-(((k * flat - IN) % D) + flat) // D) for k in range(self.mix, count)
        )
        self.rows = ceil_to(max(rows_in, -(-rows_out // 4)), 8)
        self.in_len = IN - self.mix * flat
        self.mix_in = -(-(((self.mix * flat) % PROJ) + self.in_len) // PROJ)
        self.mix_out = -(-(flat - self.in_len) // D)
        self.mix_free = self.rows - self.mix_in
        assert 4 * self.mix_free >= self.mix_out
        rows = self.rows
        self.j_in = self.mix // seq + 1
        self.j_out = self.mix // seq
        n_in, n_out = self.j_in, dp - self.j_out
        self.in_map = np.full((seq, n_in, rows), -1, np.int32)
        self.out_map = np.full((seq, n_out, 4, rows), -1, np.int32)
        m = np.arange(rows)
        for s in range(seq):
            for j in range(n_in):
                k = j * seq + s
                if k > self.mix:
                    continue
                first = (k * flat) // PROJ
                used = min(rows, D - first)
                if k == self.mix:
                    used = self.mix_in
                self.in_map[s, j, :used] = first + m[:used]
            for j in range(n_out):
                k = (j + self.j_out) * seq + s
                if k < self.mix:
                    continue
                for b in range(4):
                    if k == self.mix:
                        q = b * self.mix_free + (m - self.mix_in)
                        ok = (m >= self.mix_in) & (q < self.mix_out)
                    else:
                        q = (k * flat - IN) // D + b * rows + m
                        ok = q < min(DI, -(-((k + 1) * flat - IN) // D))
                    self.out_map[s, j, b] = np.where(ok, q, -1)

    def windows(self):
        rows, seq = self.rows, self.seq
        table = np.zeros((seq, self.dp - self.j_out, 4, 3), np.int32)
        for s in range(seq):
            for j in range(self.dp - self.j_out):
                k = (j + self.j_out) * seq + s
                for b in range(4):
                    if k < self.mix:
                        continue
                    if k == self.mix:
                        start = b * self.mix_free - self.mix_in
                        low = self.mix_in
                        high = min(rows, low + max(0, self.mix_out - b * self.mix_free))
                    else:
                        start = (k * self.flat - IN) // D + b * rows
                        low = 0
                        stop = min(DI, -(-((k + 1) * self.flat - IN) // D))
                        high = min(rows, max(0, stop - start))
                    table[s, j, b] = ((start + s * (DI // seq)) % DI, low, high)
        return table.reshape(seq, -1)

    def pack(self, flat, k):
        rows, size = self.rows, self.flat
        shift = (k * size) % PROJ
        span = rows * PROJ
        buf = jnp.pad(flat, (PROJ, span - size))
        win = lax.dynamic_slice(buf, (PROJ - shift,), (span,)).reshape(rows, PROJ)
        win = jnp.pad(win, ((0, 0), (0, WIDE - PROJ)))
        off = (k * size - IN) % D
        span = 4 * rows * D
        buf = jnp.pad(flat, (D, span - size))
        out = lax.dynamic_slice(buf, (D - off,), (span,)).reshape(4, rows, D)
        out = jnp.concatenate([out[b] for b in range(4)] + [jnp.zeros((rows, WIDE - 4 * D), flat.dtype)], axis=1)
        head = flat[self.in_len :]
        free = self.mix_free
        head = jnp.pad(head, (0, 4 * free * D - head.shape[0])).reshape(4, free, D)
        low = jnp.concatenate([head[b] for b in range(4)] + [jnp.zeros((free, WIDE - 4 * D), flat.dtype)], axis=1)
        mixed = jnp.concatenate([win[: self.mix_in], low], axis=0)
        return jnp.where(k < self.mix, win, jnp.where(k > self.mix, out, mixed))

    def unpack(self, chunk, k):
        rows, size = self.rows, self.flat
        shift = (k * size) % PROJ
        line = chunk[:, :PROJ].reshape(-1)
        line = jnp.pad(line, (0, max(0, PROJ + size - rows * PROJ)))
        win = lax.dynamic_slice(line, (shift,), (size,))
        off = (k * size - IN) % D
        line = jnp.concatenate([chunk[:, b * D : (b + 1) * D] for b in range(4)], axis=0).reshape(-1)
        line = jnp.pad(line, (0, max(0, D + size - 4 * rows * D)))
        out = lax.dynamic_slice(line, (off,), (size,))
        low = chunk[self.mix_in :]
        low = jnp.concatenate([low[:, b * D : (b + 1) * D] for b in range(4)], axis=0)
        mixed = jnp.concatenate([win[: self.in_len], low.reshape(-1)[: size - self.in_len]])
        return jnp.where(k < self.mix, win, jnp.where(k > self.mix, out, mixed))


def make_general(dp, seq):
    za, yb, cc = factors(dp)

    def place(z, y, c):
        return ((z % za) * yb + (y % yb)) * cc + (c % cc)

    def perm(dz, dy, dc):
        return [
            (place(z, y, c), place(z + dz, y + dy, c + dc))
            for z in range(za)
            for y in range(yb)
            for c in range(cc)
        ]

    z_next, y_next, c_next = perm(1, 0, 0), perm(0, 1, 0), perm(0, 0, 1)

    def gather_dp(chunk):
        j = lax.axis_index("dp")
        z, y, c = j // (yb * cc), (j // cc) % yb, j % cc
        whole = jnp.zeros((dp,) + chunk.shape, chunk.dtype)
        slots = []
        cur = chunk
        for r in range(za):
            if r:
                cur = lax.ppermute(cur, "dp", z_next)
            side = cur
            for t in range(yb):
                if t:
                    side = lax.ppermute(side, "dp", y_next)
                slots.append((z - r, y - t, c, side))
                if cc == 2:
                    slots.append((z - r, y - t, c + 1, lax.ppermute(side, "dp", c_next)))
        for zi, yi, ci, data in slots:
            at = (((zi + za) % za) * yb + (yi + yb) % yb) * cc + ci % cc
            whole = lax.dynamic_update_index_in_dim(whole, data, at, 0)
        return whole

    def scatter_dp(parts):
        j = lax.axis_index("dp")
        z, y, c = j // (yb * cc), (j // cc) % yb, j % cc

        def pick(zi, yi, ci):
            at = (((zi + za) % za) * yb + (yi + yb) % yb) * cc + ci % cc
            return lax.dynamic_index_in_dim(parts, at, 0, False)

        def core_sum(zi, yi):
            own = pick(zi, yi, c)
            if cc == 2:
                got = lax.ppermute(pick(zi, yi, c + 1), "dp", c_next)
                own = (own.astype(f32) + got.astype(f32)).astype(bf16)
            return own

        def mid_sum(zi):
            acc = None
            for r in range(1, yb + 1):
                mine = core_sum(zi, y - r)
                if acc is not None:
                    acc = (acc.astype(f32) + mine.astype(f32)).astype(bf16)
                else:
                    acc = mine
                if r < yb:
                    acc = lax.ppermute(acc, "dp", y_next)
            return acc

        acc = None
        for r in range(1, za + 1):
            mine = mid_sum(z - r)
            if acc is not None:
                acc = acc.astype(f32) + mine.astype(f32)
            else:
                acc = mine
            if r < za:
                acc = lax.ppermute(acc.astype(bf16), "dp", z_next)
        return acc.astype(f32)

    def swap_seq(a):
        return lax.ppermute(a, "seq", [(0, 1), (1, 0)])

    def halves(a, axis):
        n = a.shape[axis] // 2
        return lax.slice_in_dim(a, 0, n, axis=axis), lax.slice_in_dim(a, n, 2 * n, axis=axis)

    def gather_seq(a, axis):
        if seq != 2:
            return lax.all_gather(a, "seq", axis=axis, tiled=True)
        first = lax.axis_index("seq") == 0
        other = swap_seq(a)
        return jnp.concatenate([jnp.where(first, a, other), jnp.where(first, other, a)], axis=axis)

    def scatter_seq(a, axis):
        if seq != 2:
            return lax.psum_scatter(a, "seq", scatter_dimension=axis, tiled=True)
        first = lax.axis_index("seq") == 0
        low, high = halves(a, axis)
        got = swap_seq(jnp.where(first, high, low).astype(bf16))
        return jnp.where(first, low, high) + got.astype(f32)

    def sum_seq(a):
        if seq != 2:
            return lax.psum(a, "seq")
        a = a.astype(bf16)
        return a.astype(f32) + swap_seq(a).astype(f32)

    def sum_seq_wide(a):
        if seq != 2:
            return lax.psum(a, "seq")
        return a + swap_seq(a)

    def own_seq(a, axis):
        n = a.shape[axis] // seq
        return lax.dynamic_slice_in_dim(a, lax.axis_index("seq") * n, n, axis)

    def sum_all(a):
        for axis, count in (("seq", seq), ("dp", dp)):
            step = 1
            while step < count:
                a = a + lax.ppermute(a, axis, [(i, i ^ step) for i in range(count)])
                step *= 2
        return a

    def on_device(x_in, cotangent, params, moment_one, moment_two):
        size = params.shape[0]
        plan = Plan(dp, seq, size)
        rows = plan.rows
        s = lax.axis_index("seq")
        k = lax.axis_index("dp") * seq + s
        halfs = params.astype(bf16)

        x_own = x_in[0]
        cot_own = cotangent[0]
        tokens = gather_seq(x_own, 0)
        cot = gather_seq(cot_own, 0)

        base = IN + OUT
        at = base - k * size
        padded = jnp.pad(halfs, (SMALL, SMALL))
        tail = lax.dynamic_slice(padded, (jnp.clip(at + SMALL, 0, size + SMALL),), (SMALL,))
        tail = jnp.pad(tail, (0, -SMALL % D)).reshape(-1, D)
        small = sum_all(tail).reshape(-1)
        pieces = []
        offset = 0
        for length in (K * CONV, CONV, D, DI, H, H, H):
            pieces.append(small[offset : offset + length].astype(f32))
            offset += length
        conv_w, conv_b, norm_g, gate_g, a_log, dt_bias, skip_gain = pieces
        conv_w = conv_w.reshape(K, CONV)

        chunk = plan.pack(halfs, k)
        whole = gather_dp(chunk)
        n_in, n_out = plan.j_in, dp - plan.j_out
        w_in = whole[:n_in].reshape(n_in * rows, WIDE)
        w_out = [
            whole[plan.j_out :, :, b * D : (b + 1) * D].reshape(n_out * rows, D) for b in range(4)
        ]
        in_map = lax.dynamic_index_in_dim(jnp.asarray(plan.in_map.reshape(seq, -1)), s, 0, False)
        out_map = lax.dynamic_index_in_dim(
            jnp.asarray(plan.out_map.transpose(0, 2, 1, 3).reshape(seq, 4, -1)), s, 0, False
        )
        pick_in = (jnp.arange(D)[:, None] == in_map[None, :]).astype(bf16)
        pick_out = [(jnp.arange(DI)[:, None] == out_map[b][None, :]).astype(bf16) for b in range(4)]

        wide = tokens.astype(f32)
        scale = lax.rsqrt(jnp.mean(wide * wide, axis=-1, keepdims=True) + norm_eps)
        normed = (wide * scale * norm_g[None, :]).astype(bf16)
        normed_k = dot(normed, pick_in).astype(bf16)
        partial = dot(normed_k, w_in)

        x_part = scatter_seq(partial[:, DI : 2 * DI], 1)
        bcdt = sum_seq(partial[:, 2 * DI : PROJ])
        z_part = scatter_seq(partial[:, :DI], 1)
        gate_in = z_part.astype(bf16).astype(f32)
        x_pre = x_part.astype(bf16)
        bc_pre = bcdt[:, : 2 * N].astype(bf16)
        dt_raw = own_seq(bcdt[:, 2 * N :], 1).astype(bf16).astype(f32)
        hsize = DI // H
        dt_in = dt_raw + own_seq(dt_bias, 0)[None, :]
        step_size = jax.nn.softplus(dt_in)
        alog = own_seq(a_log, 0)[None, :]
        ssd_args = (
            x_pre,
            bc_pre,
            own_seq(conv_w[:, :DI], 1),
            own_seq(conv_b[:DI], 0)[None, :],
            conv_w[:, DI:],
            conv_b[None, DI:],
            step_size,
            step_size.T,
            alog,
            alog.T,
            jnp.repeat(own_seq(skip_gain, 0), hsize)[None, :],
        )
        ssd_out = ssd_forward(hsize, ssd_args)

        d_gated = None
        for b in range(4):
            piece = dot(cot, w_out[b], ((1,), (1,))).astype(bf16)
            piece = dot(piece, pick_out[b], ((1,), (1,)))
            d_gated = piece if d_gated is None else d_gated + piece
        d_gated = scatter_seq(d_gated, 1)

        gain = own_seq(gate_g, 0)[None, :]
        sig = jax.nn.sigmoid(gate_in)
        swish = gate_in * sig
        gated = ssd_out * swish
        weighted = d_gated * gain
        sums = jnp.stack([jnp.sum(gated * gated, axis=1), jnp.sum(weighted * gated, axis=1)])
        sums = sum_seq_wide(sums)
        g_scale = lax.rsqrt(sums[0] / DI + norm_eps)[:, None]
        cross = (sums[1] / DI)[:, None]
        gated_norm = (gated * g_scale * gain).astype(bf16)
        d_gate_g = jnp.sum(d_gated * gated * g_scale, axis=0)
        d_pre = g_scale * weighted - gated * g_scale**3 * cross
        d_ssd = d_pre * swish
        d_gate_in = d_pre * ssd_out * (sig + swish * (1.0 - sig))

        gn_full = gather_seq(gated_norm, 1)
        gn_k = [dot(gn_full, pick_out[b]).astype(bf16) for b in range(4)]
        y_part = None
        for b in range(4):
            piece = dot(gn_k[b], w_out[b])
            y_part = piece if y_part is None else y_part + piece
        y_own = scatter_seq(y_part, 0) + x_own.astype(f32)

        d_x, d_bcpre, d_dtraw, d_wx, d_bx, d_wb, d_bb, d_head, d_skip = ssd_backward(
            hsize, ssd_args + (jax.nn.sigmoid(dt_in), d_ssd)
        )
        d_alog, d_dtbias = d_head[0], d_head[1]
        d_skip = jnp.sum(d_skip.reshape(-1, hsize), axis=1)
        d_z_full = gather_seq(d_gate_in.astype(bf16), 1)
        d_x_full = gather_seq(d_x, 1)
        d_bc = sum_seq(d_bcpre).astype(bf16)
        d_dt_full = gather_seq(d_dtraw.astype(bf16), 1)
        pad = jnp.zeros((d_bc.shape[0], WIDE - PROJ), bf16)
        d_mixed = jnp.concatenate([d_z_full, d_x_full, d_bc, d_dt_full, pad], axis=1)

        g_in = dot(normed_k, d_mixed, ((0,), (0,))).astype(bf16).reshape(n_in, rows, WIDE)
        g_out = jnp.concatenate(
            [dot(gn_k[b], cot, ((0,), (0,))).astype(bf16).reshape(n_out, rows, D) for b in range(4)]
            + [jnp.zeros((n_out, rows, WIDE - 4 * D), bf16)],
            axis=2,
        )
        both = n_in + n_out - dp
        parts = jnp.concatenate(
            [g_in[: n_in - both], g_in[n_in - both :] + g_out[:both], g_out[both:]], axis=0
        )

        dn_k = dot(d_mixed, w_in, ((1,), (1,))).astype(bf16)
        d_normed = scatter_seq(dot(dn_k, pick_in, ((1,), (1,))), 0)
        wide_own = x_own.astype(f32)
        scale_own = lax.rsqrt(jnp.mean(wide_own * wide_own, axis=-1, keepdims=True) + norm_eps)
        a_own = d_normed * norm_g[None, :]
        d_norm_g = jnp.sum(d_normed * wide_own * scale_own, axis=0)
        d_wide = scale_own * a_own - wide_own * scale_own**3 * jnp.mean(
            a_own * wide_own, axis=-1, keepdims=True
        )
        input_grad = (cot_own.astype(f32) + d_wide).astype(bf16)

        def spread(a, width):
            full = jnp.zeros(a.shape[:-1] + (width,), f32)
            start = (0,) * (a.ndim - 1) + (s * a.shape[-1],)
            return lax.dynamic_update_slice(full, a, start)

        small_grad = jnp.concatenate(
            [
                jnp.concatenate([spread(d_wx, DI), d_wb], axis=1).reshape(-1),
                spread(d_bx[0], DI),
                d_bb[0],
                d_norm_g,
                spread(d_gate_g, DI),
                spread(d_alog, H),
                spread(d_dtbias, H),
                spread(d_skip, H),
            ]
        )
        small_grad = jnp.pad(small_grad, (0, -SMALL % D)).reshape(-1, D)
        small_grad = sum_all(small_grad).reshape(-1)[:SMALL]

        grad_chunk = scatter_dp(parts)
        shard = plan.unpack(grad_chunk, k)
        wing = jnp.pad(small_grad, (size, size))
        shard = shard + lax.dynamic_slice(
            wing, (jnp.clip(size - at, 0, size + SMALL),), (size,)
        )
        updated, first_new, second_new = adamw(params, shard, moment_one, moment_two)
        return (y_own.astype(bf16)[None], input_grad[None], shard, updated, first_new, second_new)

    return on_device


def matmul_cost(flops, size):
    return pl.CostEstimate(flops=flops, transcendentals=0, bytes_accessed=size)


def call(kernel, shapes, args, micros, scratch=(), tables=0, raw=0):
    specs = [pl.BlockSpec(memory_space=pltpu.SMEM)] * tables
    specs += [pl.BlockSpec(memory_space=pl.ANY)] * raw
    specs += vmem_specs(len(args) - tables - raw)
    return pl.pallas_call(
        kernel,
        out_shape=[jax.ShapeDtypeStruct(a, b) for a, b in shapes],
        in_specs=specs,
        out_specs=vmem_specs(len(shapes)),
        scratch_shapes=list(scratch),
        cost_estimate=matmul_cost(int(micros * 5e8), int(micros * 2e6)),
    )(*args)


def front_kernel(depth, slots, rows, at_ref, *refs):
    parts, nk_ref, w_ref, own_ref, other_ref = refs[:slots], *refs[slots : slots + 4]
    sems = refs[-1]
    copies = []
    for i, part in enumerate(parts):
        start = pl.multiple_of(at_ref[i] * rows, 8)
        copies.append(pltpu.make_async_copy(part, w_ref.at[pl.ds(start, rows), :], sems.at[i]))
    for copy in copies:
        copy.start()
    for copy in copies:
        copy.wait()
    half = own_ref.shape[1]
    nk = nk_ref[...]
    own_ref[...] = dot(nk, w_ref[:depth, :half])
    other_ref[...] = dot(nk, w_ref[:depth, half : 2 * half]).astype(bf16)
    if len(refs) > slots + 5:
        refs[slots + 4][...] = dot(nk, w_ref[:depth, 2 * half :]).astype(bf16)


def small_kernel(slots, want, cols, at_ref, *refs):
    parts, out_ref, sem = refs[:slots], refs[slots], refs[slots + 1]
    for i, part in enumerate(parts):

        @pl.when(at_ref[i] == want)
        def _(part=part):
            copy = pltpu.make_async_copy(part.at[:, pl.ds(cols, out_ref.shape[1])], out_ref, sem)
            copy.start()
            copy.wait()


def window_mask(rows, low, high):
    at = lax.broadcasted_iota(jnp.int32, (rows, 1), 0)
    return (at >= low) & (at < high)


def gate_grad_kernel(base, rows, tab_ref, wb_ref, wa_ref, cot_ref, own_ref, other_ref, buf_ref, acc_ref, sems):
    half = own_ref.shape[1]
    count = buf_ref.shape[1]
    copies = []
    for b in range(4):
        ref = wb_ref if b < 2 else wa_ref
        c = b % 2
        copies.append(
            pltpu.make_async_copy(
                ref.at[pl.ds(base, count), pl.ds(c * D, D)], buf_ref.at[b], sems.at[b]
            )
        )
    for copy in copies:
        copy.start()
    acc_ref[...] = jnp.zeros_like(acc_ref)
    for b in range(4):
        copies[b].wait()
        piece = dot(buf_ref[b], cot_ref[...], ((1,), (1,)))
        for j in range(count // rows):
            n = (j * 4 + b) * 3
            keep = window_mask(rows, tab_ref[n + 1], tab_ref[n + 2])
            part = jnp.where(keep, piece[j * rows : (j + 1) * rows], 0.0)
            part = jnp.concatenate([part, jnp.zeros((8, part.shape[1]), f32)], axis=0)
            start = tab_ref[n]
            near = pl.multiple_of((start // 8) * 8, 8)
            acc_ref[pl.ds(near, rows + 8), :] += pltpu.roll(part, start - near, 0)
    acc_ref[: rows + 8] += acc_ref[DI : DI + rows + 8]
    own_ref[...] = acc_ref[:half].T
    other_ref[...] = acc_ref[half : 2 * half].T.astype(bf16)


def pick_kernel(rows, tab_ref, own_ref, other_ref, gk_ref, turn_ref):
    half = own_ref.shape[1]
    turn_ref[:half] = own_ref[...].astype(f32).T
    turn_ref[half : 2 * half] = other_ref[...].astype(f32).T
    turn_ref[DI : DI + rows + 8] = turn_ref[: rows + 8]
    for b in range(4):
        for j in range(gk_ref.shape[1] // rows):
            n = (j * 4 + b) * 3
            keep = window_mask(rows, tab_ref[n + 1], tab_ref[n + 2])
            start = tab_ref[n]
            near = pl.multiple_of((start // 8) * 8, 8)
            part = pltpu.roll(turn_ref[pl.ds(near, rows + 8), :], (rows + 8 - (start - near)) % (rows + 8), 0)
            part = jnp.where(keep, part[:rows], 0.0)
            gk_ref[b, j * rows : (j + 1) * rows, :] = part.astype(bf16)


def out_kernel(base, wb_ref, wa_ref, gk_ref, y_ref, buf_ref, sems):
    count = buf_ref.shape[1]
    copies = []
    for b in range(4):
        ref = wb_ref if b < 2 else wa_ref
        c = b % 2
        copies.append(
            pltpu.make_async_copy(
                ref.at[pl.ds(base, count), pl.ds(c * D, D)], buf_ref.at[b], sems.at[b]
            )
        )
    for copy in copies:
        copy.start()
    total = None
    for b in range(4):
        copies[b].wait()
        piece = dot(gk_ref[b], buf_ref[b], ((0,), (0,)))
        total = piece if total is None else total + piece
    y_ref[...] = total


def weight_grad_kernel(depth, base, first, nk_ref, d_ref, gk_ref, cot_ref, out_ref):
    cols = out_ref.shape[1]
    nk = nk_ref[...]
    for n in range(0, cols, D):
        stop = min(n + D, cols)
        top = dot(nk, d_ref[:, n:stop], ((0,), (0,)))
        out_ref[:base, n:stop] = top[:base].astype(bf16)
        if n + D <= 2 * D:
            low = dot(gk_ref[first + n // D], cot_ref[...])
            out_ref[base:depth, n:stop] = (top[base:] + low[: depth - base]).astype(bf16)
            out_ref[depth:, n:stop] = low[depth - base :].astype(bf16)
        else:
            out_ref[base:depth, n:stop] = top[base:].astype(bf16)
            out_ref[depth:, n:stop] = jnp.zeros((out_ref.shape[0] - depth, stop - n), bf16)


def input_grad_kernel(depth, db_ref, da_ref, wb_ref, wa_ref, pick_ref, out_ref):
    dn = dot(db_ref[...], wb_ref[:depth], ((1,), (1,))) + dot(da_ref[...], wa_ref[:depth], ((1,), (1,)))
    out_ref[...] = dot(dn.astype(bf16), pick_ref[...], ((1,), (1,)))


def tie(value, token):
    return lax.optimization_barrier((value, token))[0]


def small_fits(dp, plan):
    start = (dp - 1) * plan.seq
    return plan.rows * (WIDE - 4 * D) >= SMALL and start > plan.mix and start * plan.flat <= IN + OUT


def make_pair(dp, flat):
    seq = 2
    plan = Plan(dp, seq, flat)
    rows = plan.rows
    za, yb, cc = factors(dp)
    inner = DI // seq
    hsize = DI // H
    side = WIDE - 4 * D
    n_in, n_out = plan.j_in, dp - plan.j_out
    depth, base = n_in * rows, plan.j_out * rows

    ring = list(range(0, za, 2)) + list(range(za - 1 - za % 2, 0, -2))
    seat = [ring.index(z) for z in range(za)]

    def place(z, y, c):
        return (ring[z % za] * yb + (y % yb)) * cc + (c % cc)

    def perm(dz, dy, dc):
        return [
            (place(z, y, c), place(z + dz, y + dy, c + dc))
            for z in range(za)
            for y in range(yb)
            for c in range(cc)
        ]

    z_next, y_next, c_next = perm(1, 0, 0), perm(0, 1, 0), perm(0, 0, 1)

    def position():
        j = lax.axis_index("dp")
        return jnp.asarray(seat, jnp.int32)[j // (yb * cc)], (j // cc) % yb, j % cc

    def level(z):
        return jnp.asarray(ring, jnp.int32)[(z + za) % za]

    def index(z, y, c):
        return (level(z) * yb + (y + yb) % yb) * cc + c % cc

    def gather_dp(chunk):
        z, y, c = position()
        slots = []
        marks = []
        cur = chunk
        for r in range(za):
            if r:
                cur = lax.ppermute(cur, "dp", z_next)
                marks.append(cur)
            beside = cur
            for t in range(yb):
                if t:
                    beside = lax.ppermute(beside, "dp", y_next)
                if cc == 2:
                    mate = lax.ppermute(beside, "dp", c_next)
                    slots.append((index(z - r, y - t, c + 1), mate))
                slots.append((index(z - r, y - t, c), beside))
        return jnp.stack([at for at, _ in slots]).astype(jnp.int32), [data for _, data in slots], marks

    def scatter_dp(parts):
        parts = parts.reshape(za, yb, cc, rows, -1)
        z, y, c = position()

        def add(a, b):
            return (a.astype(f32) + b.astype(f32)).astype(bf16)

        total = lax.dynamic_index_in_dim(parts, c, 2, False)
        if cc == 2:
            give = lax.dynamic_index_in_dim(parts, (c + 1) % cc, 2, False)
            give = lax.ppermute(give, "dp", c_next)
            total = add(total, give)
        total = total.reshape(za * yb, rows, -1)

        def core_sum(zi, yi):
            return lax.dynamic_index_in_dim(total, level(zi) * yb + (yi + yb) % yb, 0, False)

        def mid_sum(zi):
            acc = core_sum(zi, y - 1)
            for r in range(2, yb + 1):
                acc = lax.ppermute(acc, "dp", y_next)
                acc = add(acc, core_sum(zi, y - r))
            return acc

        acc = mid_sum(z - 1)
        marks = [acc]
        for r in range(2, za + 1):
            acc = lax.ppermute(acc, "dp", z_next)
            acc = add(acc, mid_sum(z - r))
            marks.append(acc)
        return acc, marks

    def swap(a):
        return lax.ppermute(a, "seq", [(0, 1), (1, 0)])

    def sum_all(a, marks):
        a = a + swap(a)
        steps = []
        step = 1
        while step < dp:
            steps.append(step)
            step *= 2
        steps = steps[:1] + steps[2:] + steps[1:2]
        for n, step in enumerate(steps):
            got = lax.ppermute(a, "dp", [(i, i ^ step) for i in range(dp)])
            if n:
                got = tie(got, marks[min(n - 1, len(marks) - 1)])
            a = a + got
        return a

    def own_seq(a, axis):
        n = a.shape[axis] // seq
        return lax.dynamic_slice_in_dim(a, lax.axis_index("seq") * n, n, axis)

    def on_device(x_in, cotangent, params, moment_one, moment_two):
        s = lax.axis_index("seq")
        first = s == 0
        k = lax.axis_index("dp") * seq + s
        halfs = params.astype(bf16)

        def ordered(a, other):
            return jnp.concatenate([jnp.where(first, a, other), jnp.where(first, other, a)], axis=0)

        def flip(a, cut):
            return jnp.where(first, a, jnp.concatenate([a[:, cut:], a[:, :cut]], axis=1))

        at = IN + OUT - k * flat
        padded = jnp.pad(halfs, (SMALL, SMALL))
        tail = lax.dynamic_slice(padded, (jnp.clip(at + SMALL, 0, flat + SMALL),), (SMALL,))
        tail = jnp.pad(tail, (0, rows * side - SMALL)).reshape(rows, side)
        tail = tail + swap(tail)

        chunk = plan.pack(halfs, k)
        input_rows = k <= plan.mix
        part_b = jnp.where(input_rows, flip(chunk[:, :DI], inner), chunk[:, :DI])
        mid = chunk[:, DI : 2 * DI]
        part_a = jnp.concatenate(
            [
                jnp.where(input_rows, flip(mid, inner), mid),
                jnp.where(input_rows, chunk[:, 4 * D :], tail),
            ],
            axis=1,
        )
        if plan.mix_out:
            keep = (k == plan.mix) & (jnp.arange(rows) >= plan.mix_in)[:, None]
            part_b = jnp.where(keep, chunk[:, :DI], part_b)
            part_a = jnp.where(keep, chunk[:, DI:], part_a)
        at_a, slots_a, marks = gather_dp(part_a)
        part_b = tie(part_b, marks[-1])
        late = marks[1 % len(marks)]

        x_own = x_in[0]
        cot_own = cotangent[0]
        tokens = ordered(x_own, tie(swap(x_own), late))
        cot = ordered(cot_own, tie(swap(cot_own), late))
        count = tokens.shape[0]

        in_map = lax.dynamic_index_in_dim(jnp.asarray(plan.in_map.reshape(seq, -1)), tie(s, late), 0, False)
        table = lax.dynamic_index_in_dim(jnp.asarray(plan.windows()), s, 0, False)
        pick_in = (jnp.arange(D)[:, None] == in_map[None, :]).astype(bf16)
        small = call(
            functools.partial(small_kernel, dp, dp - 1, 2 * D),
            [((rows, side), bf16)],
            (at_a, *slots_a),
            1.0,
            scratch=[pltpu.SemaphoreType.DMA],
            tables=1,
            raw=dp,
        )[0].reshape(-1)
        pieces = []
        offset = 0
        for length in (K * CONV, CONV, D, DI, H, H, H):
            pieces.append(small[offset : offset + length].astype(f32))
            offset += length
        conv_w, conv_b, norm_g, gate_g, a_log, dt_bias, skip_gain = pieces
        conv_w = conv_w.reshape(K, CONV)

        wide = tokens.astype(f32)
        scale = lax.rsqrt(jnp.mean(wide * wide, axis=-1, keepdims=True) + norm_eps)
        normed = (wide * scale * norm_g[None, :]).astype(bf16)
        normed_k = dot(normed, pick_in).astype(bf16)

        w_a, x_own_part, x_other, bcdt = call(
            functools.partial(front_kernel, depth, dp, rows),
            [
                ((dp * rows, 2 * D + side), bf16),
                ((count, inner), f32),
                ((count, inner), bf16),
                ((count, side), bf16),
            ],
            (at_a, *slots_a, normed_k),
            5.0,
            scratch=[pltpu.SemaphoreType.DMA((dp,))],
            tables=1,
            raw=dp,
        )
        at_b, slots_b, marks = gather_dp(part_b)
        bcdt = bcdt.astype(f32) + tie(swap(bcdt), marks[-1]).astype(f32)
        x_pre = (x_own_part + swap(x_other).astype(f32)).astype(bf16)
        bc_pre = bcdt[:, : 2 * N].astype(bf16)
        dt_raw = own_seq(bcdt[:, 2 * N : 2 * N + H], 1).astype(bf16).astype(f32)
        dt_in = dt_raw + own_seq(dt_bias, 0)[None, :]
        step_size = jax.nn.softplus(dt_in)
        alog = own_seq(a_log, 0)[None, :]
        ssd_args = (
            x_pre,
            bc_pre,
            own_seq(conv_w[:, :DI], 1),
            own_seq(conv_b[:DI], 0)[None, :],
            conv_w[:, DI:],
            conv_b[None, DI:],
            step_size,
            step_size.T,
            alog,
            alog.T,
            jnp.repeat(own_seq(skip_gain, 0), hsize)[None, :],
        )
        ssd_out = ssd_forward(hsize, ssd_args)

        w_b, z_own_part, z_other = call(
            functools.partial(front_kernel, depth, dp, rows),
            [((dp * rows, DI), bf16), ((count, inner), f32), ((count, inner), bf16)],
            (at_b, *slots_b, normed_k),
            5.0,
            scratch=[pltpu.SemaphoreType.DMA((dp,))],
            tables=1,
            raw=dp,
        )
        span = n_out * rows
        held = [pltpu.VMEM((4, span, D), bf16)]
        dg_own, dg_other = call(
            functools.partial(gate_grad_kernel, base, rows),
            [((count, inner), f32), ((count, inner), bf16)],
            (table, w_b, w_a, cot),
            5.0,
            scratch=held + [pltpu.VMEM((DI + rows + 8, count), f32), pltpu.SemaphoreType.DMA((4,))],
            tables=1,
            raw=2,
        )
        gate_in = (z_own_part + swap(z_other).astype(f32)).astype(bf16).astype(f32)
        d_gated = dg_own + swap(dg_other).astype(f32)

        gain = own_seq(gate_g, 0)[None, :]
        sig = jax.nn.sigmoid(gate_in)
        swish = gate_in * sig
        gated = ssd_out * swish
        weighted = d_gated * gain
        sums = jnp.stack([jnp.sum(gated * gated, axis=1), jnp.sum(weighted * gated, axis=1)])
        sums = sums + swap(sums)
        g_scale = lax.rsqrt(sums[0] / DI + norm_eps)[:, None]
        cross = (sums[1] / DI)[:, None]
        gn_own = (gated * g_scale * gain).astype(bf16)
        d_gate_g = jnp.sum(d_gated * gated * g_scale, axis=0)
        d_pre = g_scale * weighted - gated * g_scale**3 * cross
        d_ssd = d_pre * swish
        dz_own = (d_pre * ssd_out * (sig + swish * (1.0 - sig))).astype(bf16)
        gn_own, dz_own, d_ssd = lax.optimization_barrier((gn_own, dz_own, d_ssd))
        gn_other = swap(gn_own)
        dz_other = swap(dz_own)

        d_x, d_bcpre, d_dtraw, d_wx, d_bx, d_wb, d_bb, d_head, d_skip = ssd_backward(
            hsize, ssd_args + (jax.nn.sigmoid(dt_in), d_ssd)
        )
        d_alog, d_dtbias = d_head[0], d_head[1]
        d_skip = jnp.sum(d_skip.reshape(-1, hsize), axis=1)

        gn_k = call(
            functools.partial(pick_kernel, rows),
            [((4, span, count), bf16)],
            (table, gn_own, gn_other),
            3.0,
            scratch=[pltpu.VMEM((DI + rows + 8, count), f32)],
            tables=1,
        )[0]
        d_b = jnp.concatenate([dz_own, dz_other], axis=1)
        parts_b = call(
            functools.partial(weight_grad_kernel, depth, base, 0),
            [((dp * rows, DI), bf16)],
            (normed_k, d_b, gn_k, cot),
            5.0,
        )[0]
        grad_b, _ = scatter_dp(parts_b)

        bcdt_own = jnp.concatenate([d_bcpre, d_dtraw], axis=1).astype(bf16)
        dx_other, bcdt_other = swap(d_x), swap(bcdt_own)
        dx_other, bcdt_other, _ = lax.optimization_barrier((dx_other, bcdt_other, parts_b))
        d_bc = (bcdt_own[:, : 2 * N].astype(f32) + bcdt_other[:, : 2 * N].astype(f32)).astype(bf16)
        dt_pair = jnp.where(
            first,
            jnp.concatenate([bcdt_own[:, 2 * N :], bcdt_other[:, 2 * N :]], axis=1),
            jnp.concatenate([bcdt_other[:, 2 * N :], bcdt_own[:, 2 * N :]], axis=1),
        )
        blank = jnp.zeros((count, WIDE - PROJ), bf16)
        d_a = jnp.concatenate([d_x, dx_other, d_bc, dt_pair, blank], axis=1)
        parts_a = call(
            functools.partial(weight_grad_kernel, depth, base, 2),
            [((dp * rows, 2 * D + side), bf16)],
            (normed_k, d_a, gn_k, cot),
            5.0,
        )[0]
        grad_a, marks_a = scatter_dp(parts_a)

        d_normed = call(
            functools.partial(input_grad_kernel, depth),
            [((count, D), f32)],
            (d_b, tie(d_a, parts_a), w_b, w_a, pick_in),
            5.0,
        )[0]

        d_norm_g = jnp.sum(d_normed * wide * scale, axis=0)

        def spread(a, width):
            full = jnp.zeros(a.shape[:-1] + (width,), f32)
            start = (0,) * (a.ndim - 1) + (s * a.shape[-1],)
            return lax.dynamic_update_slice(full, a, start)

        small_grad = jnp.concatenate(
            [
                jnp.concatenate([spread(d_wx, DI), d_wb], axis=1).reshape(-1),
                spread(d_bx[0], DI),
                d_bb[0],
                d_norm_g,
                spread(d_gate_g, DI),
                spread(d_alog, H),
                spread(d_dtbias, H),
                spread(d_skip, H),
            ]
        )
        small_grad = jnp.pad(small_grad, (0, -SMALL % D)).reshape(-1, D)
        small_grad = sum_all(small_grad, marks_a).reshape(-1)[:SMALL]

        y_part = call(
            functools.partial(out_kernel, base),
            [((count, D), f32)],
            (w_b, w_a, tie(gn_k, d_normed)),
            4.0,
            scratch=held + [pltpu.SemaphoreType.DMA((4,))],
            raw=2,
        )[0]

        def own_tokens(a):
            half = count // 2
            low, high = a[:half], a[half:]
            got = swap(jnp.where(first, high, low).astype(bf16))
            return jnp.where(first, low, high) + got.astype(f32)

        d_own = own_tokens(d_normed)
        y_own = own_tokens(y_part) + x_own.astype(f32)
        wide_own = x_own.astype(f32)
        scale_own = lax.rsqrt(jnp.mean(wide_own * wide_own, axis=-1, keepdims=True) + norm_eps)
        a_own = d_own * norm_g[None, :]
        d_wide = scale_own * a_own - wide_own * scale_own**3 * jnp.mean(
            a_own * wide_own, axis=-1, keepdims=True
        )
        input_grad = (cot_own.astype(f32) + d_wide).astype(bf16)

        def unflip(a, cut):
            keep = k > plan.mix
            if plan.mix_out:
                keep = keep | ((k == plan.mix) & (jnp.arange(rows) >= plan.mix_in)[:, None])
            return jnp.where(keep, a, flip(a, cut))

        grad_a, grad_b = grad_a.astype(f32), grad_b.astype(f32)
        grad_chunk = jnp.concatenate(
            [unflip(grad_b, inner), unflip(grad_a[:, : 2 * D], inner), grad_a[:, 2 * D :]], axis=1
        )
        shard = plan.unpack(grad_chunk, k)
        wing = jnp.pad(small_grad, (flat, flat))
        shard = shard + lax.dynamic_slice(wing, (jnp.clip(flat - at, 0, flat + SMALL),), (flat,))
        updated, first_new, second_new = adamw(params, shard, moment_one, moment_two)
        return (y_own.astype(bf16)[None], input_grad[None], shard, updated, first_new, second_new)

    return on_device


def make(dp, seq):
    def on_device(x_in, cotangent, params, moment_one, moment_two):
        flat = params.shape[0]
        if seq == 2 and small_fits(dp, Plan(dp, seq, flat)):
            return make_pair(dp, flat)(x_in, cotangent, params, moment_one, moment_two)
        return make_general(dp, seq)(x_in, cotangent, params, moment_one, moment_two)

    return on_device


def solution(mesh):
    return jax.shard_map(
        make(mesh.shape["dp"], mesh.shape["seq"]),
        mesh=mesh,
        in_specs=(
            P("dp", "seq", None),
            P("dp", "seq", None),
            P(("dp", "seq")),
            P(("dp", "seq")),
            P(("dp", "seq")),
        ),
        out_specs=(
            P("dp", "seq", None),
            P("dp", "seq", None),
            P(("dp", "seq")),
            P(("dp", "seq")),
            P(("dp", "seq")),
            P(("dp", "seq")),
        ),
        check_vma=False,
    )
```
